32 devices in a mesh: space: 4 (over y, core), shard: 8 (over z, x).
Axes of the slice: x: 2, y: 2, z: 4, core: 2. Of those that a mesh axis runs over, the one named last changes fastest.
Arguments:
- volume_field: float32 [2, 16, 16, 128, 128], P(None, None, 'space', 'shard'), may hold values from -6 to 6
- source: float32 [2, 16, 16, 128, 128], P(None, None, 'space', 'shard'), may hold values from -6 to 6
- material: int32 [16, 128, 128], P('space', 'shard'), may hold values from 0 to 7
- mat_real: float32 [8], replicated, may hold values from 0.5 to 4
- mat_loss: float32 [8], replicated, may hold values from 0.1 to 1.5
- surface_map: int32 [512, 128], P(('space', 'shard')), may hold values from 0 to 8191
- near_boxes: int32 [512, 4], P(('space', 'shard')), may hold values from 0 to 511, as said below
- near_blocks: bfloat16 [4, 256, 256], replicated, may hold values from -0.1875 to 0.1875
- radiate: bfloat16 [2, 128, 512], replicated, may hold values from -0.375 to 0.375
- interp: bfloat16 [512, 2048], replicated, may hold values from -0.25 to 0.25
- phase_angle: float32 [8, 2048], replicated, may hold values from -3.140625 to 3.140625
- far_parents: int32 [64, 8], replicated, may hold values from 0 to 63
- far_kind: int32 [64, 8], replicated, may hold values from 0 to 315
- translate: float32 [316, 2, 2048], P(None, None, 'shard'), may hold values from -0.18 to 0.18
Outputs:
- volume_out: float32 [2, 16, 16, 128, 128], P(None, None, 'space', 'shard')
- forcing: float32 [512, 16, 256], P(('space', 'shard'))
The draws below stay inside these ranges and needn't reach their ends.
Inputs may be any that keep to these rules, and one draw needn't show every extreme that they name: near_boxes[b, 0] = b; every other entry is a box of the same group of 128 boxes (boxes g * 128 to (g + 1) * 128 - 1) whose index lies from 16 below to 31 above the first box of b's run of 16 boxes.
All inputs are finite; a program needn't handle non-finite values.
Results may differ from the reference program's by a relative error of at most 0.015.
Values may be sent and summed in bfloat16 or wider, within the bound.
No kernel may reach another device: no remote copies, remote signals or barrier semaphores. Data moves between devices by JAX's collectives and lax.ppermute only.
A program may use at most 128 MiB of HBM per device.

```python
import math
import jax
import jax.numpy as jnp
from jax import lax

EXC = 16
U = 128
L = 512
PD = 2048
NEAR = 4
FAR = 8
KINDS = 316
MATS = 8
NZ = 128
CX = 4
CY = 16
BOX_DEV = 16
NX = 16
NY = 128
GROUP_BOXES = 128
BOXES = 512
PARENTS = 64
N_SHARD = 8


def draw_near_boxes(key, part):
    box_index = jnp.arange(BOXES, dtype=jnp.int32)
    device_rank = box_index // BOX_DEV
    group_start = box_index // GROUP_BOXES * GROUP_BOXES
    lowest = jnp.maximum(device_rank * BOX_DEV - BOX_DEV, group_start)
    highest = jnp.minimum(device_rank * BOX_DEV + 2 * BOX_DEV, group_start + GROUP_BOXES)
    offsets = jax.random.randint(jax.random.fold_in(key, 7), (BOXES, NEAR - 1), 0, 1 << 20, dtype=jnp.int32)
    picked = lowest[:, None] + offsets % (highest - lowest)[:, None]
    return jnp.concatenate([box_index[:, None], picked], axis=1).astype(jnp.int32)


def set_ends(drawn, own_key, low, top_value):
    shape = drawn.shape
    spot = [jax.random.randint(jax.random.fold_in(own_key, axis), (), 0, shape[axis]) for axis in range(len(shape))]
    drawn = drawn.at[tuple(spot)].set(low)
    longest = shape.index(max(shape))
    spot[longest] = (spot[longest] + 1) % shape[longest]
    return drawn.at[tuple(spot)].set(top_value)


def shard_levels(rng, dims, cuts, low, high):
    def one(axis_at, parts):
        steps = jax.random.uniform(jax.random.fold_in(jax.random.fold_in(rng, 6), axis_at), (parts,), jnp.float32, low / len(cuts), high / len(cuts))
        return jnp.repeat(jnp.exp(steps), dims[axis_at] // parts).reshape((-1,) + (1,) * (len(dims) - axis_at - 1))

    level = one(*cuts[0])
    for cut in cuts[1:]:
        level = level * one(*cut)
    return level


def scatter_about(own_key, extent, deviation, most, split=(), kind=jnp.bfloat16):
    values = jax.random.normal(own_key, extent, jnp.float32) * deviation
    if len(split) > 0:
        values = shard_levels(own_key, extent, split, -0.22, 0.18) * values
    return jnp.clip(values, min=-most, max=most).astype(kind)


def setup_inputs(seed: int = 0) -> dict:
    seeds = jax.random.split(jax.random.key(seed), 15)
    return {
        "volume_field": scatter_about(seeds[0], (2, EXC, NX, NY, NZ), 1.0, 6.0, ((2, 4), (3, 8)), jnp.float32),
        "source": scatter_about(seeds[1], (2, EXC, NX, NY, NZ), 1.0, 6.0, ((2, 4), (3, 8)), jnp.float32),
        "material": set_ends(jax.random.randint(seeds[2], (NX, NY, NZ), 0, MATS), jax.random.fold_in(seeds[2], 1), 0, MATS - 1).astype(jnp.int32),
        "mat_real": jnp.clip(jnp.exp(jax.random.uniform(seeds[3], (MATS,), jnp.float32, math.log(0.5), math.log(4.0))), 0.5, 4.0),
        "mat_loss": jnp.clip(jax.random.uniform(seeds[4], (MATS,), jnp.float32, 0.1, 1.5), 0.1, 1.5),
        "surface_map": set_ends(jax.random.randint(seeds[5], (BOXES, U), 0, CX * CY * NZ), jax.random.fold_in(seeds[5], 1), 0, (CX * CY * NZ) - 1).astype(jnp.int32),
        "near_boxes": draw_near_boxes(jax.random.fold_in(seeds[14], 71), 0),
        "near_blocks": scatter_about(seeds[7], (NEAR, 2 * U, 2 * U), (2 * U * NEAR) ** -0.5, 0.1875),
        "radiate": scatter_about(seeds[8], (2, U, L), (2 * U) ** -0.5, 0.375),
        "interp": scatter_about(seeds[9], (L, PD), L ** -0.5, 0.25),
        "phase_angle": jnp.clip(jax.random.uniform(seeds[10], (8, PD), jnp.float32, -3.140625, 3.140625), -3.140625, 3.140625),
        "far_parents": set_ends(jax.random.randint(seeds[11], (PARENTS, FAR), 0, PARENTS), jax.random.fold_in(seeds[11], 1), 0, PARENTS - 1).astype(jnp.int32),
        "far_kind": set_ends(jax.random.randint(seeds[12], (PARENTS, FAR), 0, KINDS), jax.random.fold_in(seeds[12], 1), 0, KINDS - 1).astype(jnp.int32),
        "translate": scatter_about(seeds[13], (KINDS, 2, PD), 0.03, 0.18, ((2, 8),), jnp.float32),
    }


relaxation = 0.8


def neighbour_sum(padded):
    core = padded[:, :, 1:-1, 1:-1]
    result = padded[:, :, 2:, 1:-1] + padded[:, :, :-2, 1:-1]
    result = result + padded[:, :, 1:-1, 2:] + padded[:, :, 1:-1, :-2]
    zero_layer = jnp.zeros(core.shape[:-1] + (1,), core.dtype)
    upper = jnp.concatenate([core[..., 1:], zero_layer], axis=-1)
    lower = jnp.concatenate([zero_layer, core[..., :-1]], axis=-1)
    return result + upper + lower


def relax_sweep(current, neighbours, source, diagonal_coef, loss_coef):
    real_part = diagonal_coef * current[0] - neighbours[0] - loss_coef * current[1]
    imag_part = diagonal_coef * current[1] - neighbours[1] + loss_coef * current[0]
    applied = jnp.stack([real_part, imag_part])
    return current + relaxation * (source - applied) / diagonal_coef


def block_matrix(radiate):
    upper = jnp.concatenate([radiate[0], radiate[1]], axis=1)
    lower = jnp.concatenate([-radiate[1], radiate[0]], axis=1)
    return jnp.concatenate([upper, lower], axis=0)


def aggregate(leaf_rows, interp, cosine, sine_part):
    parent_count = leaf_rows.shape[0] // 8
    excite = leaf_rows.shape[1]
    spread = jnp.dot(leaf_rows.reshape(-1, interp.shape[0]), interp, preferred_element_type=jnp.float32)
    spread = spread.reshape(parent_count, 8, excite, 2, interp.shape[1])
    cosine_wide = cosine[None, :, None, :]
    sine_wide = sine_part[None, :, None, :]
    real_part = jnp.sum(cosine_wide * spread[:, :, :, 0] - sine_wide * spread[:, :, :, 1], axis=1)
    imag_part = jnp.sum(sine_wide * spread[:, :, :, 0] + cosine_wide * spread[:, :, :, 1], axis=1)
    return jnp.stack([real_part, imag_part], axis=2).astype(jnp.bfloat16)


def combine_far(sources, table):
    real_table = table[:, :, None, 0]
    imag_table = table[:, :, None, 1]
    real_part = jnp.sum(real_table * sources[:, :, :, 0] - imag_table * sources[:, :, :, 1], axis=1)
    imag_part = jnp.sum(imag_table * sources[:, :, :, 0] + real_table * sources[:, :, :, 1], axis=1)
    return jnp.stack([real_part, imag_part], axis=2)


def disaggregate(incoming_rows, interp, cosine, sine_part, weights):
    parent_count = incoming_rows.shape[0]
    excite = incoming_rows.shape[1]
    widened = incoming_rows.astype(jnp.float32)[:, None]
    cosine_wide = cosine[None, :, None, :]
    sine_wide = sine_part[None, :, None, :]
    real_part = cosine_wide * widened[:, :, :, 0] + sine_wide * widened[:, :, :, 1]
    imag_part = cosine_wide * widened[:, :, :, 1] - sine_wide * widened[:, :, :, 0]
    shifted = jnp.stack([real_part, imag_part], axis=3).astype(jnp.bfloat16)
    leaf_in = jnp.dot(shifted.reshape(-1, interp.shape[1]), interp.T, preferred_element_type=jnp.float32).astype(jnp.bfloat16)
    leaf_in = leaf_in.reshape(parent_count * 8 * excite, 2 * interp.shape[0])
    far_part = jnp.dot(leaf_in, weights.T, preferred_element_type=jnp.float32)
    return far_part.reshape(parent_count * 8, excite, weights.shape[0])


def reference(volume_field, source, material, mat_real, mat_loss, surface_map, near_boxes, near_blocks, radiate, interp, phase_angle, far_parents, far_kind, translate):
    diagonal_coef = 6.0 + mat_real[material]
    loss_coef = mat_loss[material]
    current = volume_field
    for sweep_index in range(2):
        padded = jnp.pad(current, ((0, 0), (0, 0), (1, 1), (1, 1), (0, 0)))
        current = relax_sweep(current, neighbour_sum(padded), source, diagonal_coef, loss_coef)
    box_index = jnp.arange(BOXES, dtype=jnp.int32)[:, None]
    device_rank = box_index // BOX_DEV
    grid_x = (device_rank // N_SHARD) * CX + surface_map // (CY * NZ)
    grid_y = (device_rank % N_SHARD) * CY + (surface_map // NZ) % CY
    grid_z = surface_map % NZ
    sampled = current[:, :, grid_x, grid_y, grid_z]
    currents = jnp.transpose(sampled, (2, 1, 0, 3)).reshape(BOXES, EXC, 2 * U).astype(jnp.bfloat16)
    near_force = jnp.zeros((BOXES, EXC, 2 * U), jnp.float32)
    for slot_index in range(NEAR):
        picked = currents[near_boxes[:, slot_index]].reshape(BOXES * EXC, 2 * U)
        near_force = near_force + jnp.dot(picked, near_blocks[slot_index], preferred_element_type=jnp.float32).reshape(BOXES, EXC, 2 * U)
    weights = block_matrix(radiate)
    leaf = jnp.dot(currents.reshape(BOXES * EXC, 2 * U), weights, preferred_element_type=jnp.float32).astype(jnp.bfloat16)
    leaf = leaf.reshape(BOXES, EXC, 2, L)
    cosine = jnp.cos(phase_angle)
    sine_part = jnp.sin(phase_angle)
    block_size = math.gcd(PARENTS, 32)
    block_count = PARENTS // block_size

    def parent_block(leaf_rows):
        return aggregate(leaf_rows, interp, cosine, sine_part)

    parents = lax.map(parent_block, leaf.reshape(block_count, block_size * 8, EXC, 2, L)).reshape(PARENTS, EXC, 2, PD)

    def far_block(lists):
        source_ids, kinds = lists
        sources = parents[source_ids].astype(jnp.float32)
        table = translate[kinds]
        return combine_far(sources, table).astype(jnp.bfloat16)

    incoming = lax.map(far_block, (far_parents.reshape(block_count, block_size, FAR), far_kind.reshape(block_count, block_size, FAR)))

    def back_block(incoming_rows):
        return disaggregate(incoming_rows, interp, cosine, sine_part, weights)

    far_force = lax.map(back_block, incoming).reshape(BOXES, EXC, 2 * U)
    forcing = near_force + far_force
    return current, forcing
```

```python
import jax
import jax.numpy as jnp
from jax import lax
from jax.experimental import pallas as pl
from jax.experimental.pallas import tpu as pltpu
from jax.sharding import PartitionSpec as P

relaxation = 0.8
f32 = jnp.float32
bf16 = jnp.bfloat16
CHILDREN = 8


def dot(a, b):
    return jnp.dot(a, b, preferred_element_type=f32)


def dot_t(a, b):
    return lax.dot_general(a, b, (((1,), (1,)), ((), ())), preferred_element_type=f32)


def half_turn(v):
    half = v.shape[-2] // 2
    rows = lax.broadcasted_iota(jnp.int32, v.shape, v.ndim - 2)
    swapped = pltpu.roll(v, half, v.ndim - 2)
    return jnp.where(rows < half, -swapped, swapped)


def log2(n):
    assert n & (n - 1) == 0
    return n.bit_length() - 1


def swap_pairs(n, first):
    pairs = []
    for i in range(first, n - 1, 2):
        pairs += [(i, i + 1), (i + 1, i)]
    return pairs


def swap(for_even, for_odd, axis):
    n = lax.axis_size(axis)
    return [lax.ppermute(v, axis, swap_pairs(n, k)) for k, v in enumerate((for_even, for_odd))]


def up_body(field, smap, radiate, interp, cosine, sine, cur, out, cells, rows, *, groups, slices):
    channels, cx, cy, nz = field.shape
    excite = channels // 2
    group = excite // groups
    boxes, unknowns = smap.shape
    for c in range(channels):
        t, e = divmod(c, excite)
        place = (e // group) * 2 * group + t * group + e % group
        for x in range(cx):
            for y in range(0, cy, 8):
                cells[x, pl.ds(y * channels + place, 8, stride=channels), :] = field[c, x, y : y + 8, :]
    lhs = jnp.concatenate([cells[x].astype(bf16) for x in range(cx)], axis=1)
    pair = 2
    for b in range(0, boxes, pair):
        keys = jnp.concatenate([smap[b + j : b + j + 1, :] for j in range(pair)], axis=1)
        key_z = keys & (nz - 1)
        key_y = (keys >> log2(nz)) & (cy - 1)
        key_x = keys >> (log2(nz) + log2(cy))
        level = lax.broadcasted_iota(jnp.int32, (nz, pair * unknowns), 0)
        hot = [
            jnp.where(level == jnp.where(key_x == x, key_z, -1), 1.0, 0.0).astype(bf16) for x in range(cx)
        ]
        picked = dot(lhs, jnp.concatenate(hot, axis=0))
        found = jnp.zeros((channels, pair * unknowns), f32)
        for y in range(cy):
            found = jnp.where(key_y == y, picked[y * channels : (y + 1) * channels], found)
        for j in range(pair):
            own = found[:, j * unknowns : (j + 1) * unknowns].reshape(groups, 2 * group, unknowns)
            turned = half_turn(own)
            both = jnp.concatenate([own, turned], axis=2).reshape(channels, 2 * unknowns)
            rows[(b + j) * channels : (b + j + 1) * channels, :] = both.astype(bf16)
            parts = [
                jnp.concatenate([own[s, t * group : (t + 1) * group] for s in range(groups)], axis=0)
                for t in range(2)
            ]
            cur[b + j] = jnp.concatenate(parts, axis=1).astype(bf16)
    leaf = dot(rows[...], radiate[...]).astype(bf16)
    directions = interp.shape[1]
    width = directions // slices
    tile = max(width, 256)
    parents = boxes // CHILDREN
    for n in range(0, directions, tile):
        spread = dot(leaf, interp[:, n : n + tile]).reshape(parents, CHILDREN, groups, 2 * group, tile)
        along = jnp.zeros((parents, groups, 2 * group, tile), f32)
        across = jnp.zeros((parents, groups, 2 * group, tile), f32)
        for child in range(CHILDREN):
            along = along + cosine[child : child + 1, n : n + tile] * spread[:, child]
            across = across + sine[child : child + 1, n : n + tile] * spread[:, child]
        whole = (along + half_turn(across)).astype(bf16)
        for s in range(groups):
            piece = jnp.concatenate([whole[p, s] for p in range(parents)], axis=0)
            for k in range(tile // width):
                out[s * slices + n // width + k] = piece[:, k * width : (k + 1) * width]


def up(field, smap, radiate, interp, cosine, sine, groups, slices):
    channels, cx, cy, nz = field.shape
    boxes, unknowns = smap.shape
    width = interp.shape[1] // slices
    piece_rows = boxes // CHILDREN * (channels // groups)
    return pl.pallas_call(
        lambda *refs: up_body(*refs, groups=groups, slices=slices),
        out_shape=(
            jax.ShapeDtypeStruct((boxes, channels // 2, 2 * unknowns), bf16),
            jax.ShapeDtypeStruct((groups * slices, piece_rows, width), bf16),
        ),
        scratch_shapes=[
            pltpu.VMEM((cx, cy * channels, nz), f32),
            pltpu.VMEM((boxes * channels, 2 * unknowns), bf16),
        ],
        name="up",
    )(field, smap, radiate, interp, cosine, sine)


def far_body(lists, kinds, sources, translate, out, plain, turned):
    targets, far = lists.shape
    devices, piece_rows, width = sources.shape
    per = targets // devices
    tile = piece_rows // per
    wide = sources[...].astype(f32).reshape(targets, tile, width)
    plain[...] = wide
    turned[...] = half_turn(wide)

    def one(d, _):
        results = []
        for j in range(per):
            t = d * per + j
            total = jnp.zeros((tile, width), f32)
            for f in range(far):
                p = lists[t, f]
                k = kinds[t, f]
                factor = translate[k]
                total = total + factor[0:1] * plain[p] + factor[1:2] * turned[p]
            results.append(total)
        out[d] = jnp.concatenate(results, axis=0).astype(bf16)
        return 0

    lax.fori_loop(0, devices, one, 0)


def far_combine(lists, kinds, sources, translate):
    targets = lists.shape[0]
    devices, piece_rows, width = sources.shape
    tile = piece_rows // (targets // devices)
    smem = pl.BlockSpec(memory_space=pltpu.SMEM)
    vmem = pl.BlockSpec(memory_space=pltpu.VMEM)
    return pl.pallas_call(
        far_body,
        out_shape=jax.ShapeDtypeStruct(sources.shape, bf16),
        in_specs=[smem, smem, vmem, vmem],
        out_specs=vmem,
        scratch_shapes=[pltpu.VMEM((targets, tile, width), f32)] * 2,
        name="far",
    )(lists, kinds, sources, translate)


def near_body(spots, own, first, second, blocks, out, boxes_all, rows):
    boxes, excite, k = own.shape
    slots = spots.shape[1]
    boxes_all[0:boxes] = own[...]
    boxes_all[boxes : 2 * boxes] = first[...]
    boxes_all[2 * boxes : 3 * boxes] = second[...]
    for b in range(boxes):
        for s in range(slots):
            rows[b * excite : (b + 1) * excite, s * k : (s + 1) * k] = boxes_all[spots[b, s]]
    out[...] = dot(rows[...], blocks[...]).reshape(out.shape)


def near_force(spots, own, first, second, blocks):
    boxes, excite, k = own.shape
    slots = spots.shape[1]
    smem = pl.BlockSpec(memory_space=pltpu.SMEM)
    vmem = pl.BlockSpec(memory_space=pltpu.VMEM)
    return pl.pallas_call(
        near_body,
        out_shape=jax.ShapeDtypeStruct((boxes, excite, k), f32),
        in_specs=[smem, vmem, vmem, vmem, vmem],
        out_specs=vmem,
        scratch_shapes=[
            pltpu.VMEM((3 * boxes, excite, k), bf16),
            pltpu.VMEM((boxes * excite, slots * k), bf16),
        ],
        name="near",
    )(spots, own, first, second, blocks.reshape(slots * k, k))


def down_body(pieces, near, radiate, interp, cosine, sine, out, shifted, *, groups, slices):
    _, piece_rows, width = pieces.shape
    boxes, excite, both = out.shape
    unknowns = both // 2
    group = excite // groups
    tile = 2 * group
    parents = boxes // CHILDREN
    for h in range(slices):
        lanes = slice(h * width, (h + 1) * width)
        for s in range(groups):
            incoming = pieces[s * slices + h].astype(f32).reshape(parents, tile, width)
            turned = half_turn(incoming)
            for p in range(parents):
                for child in range(0, CHILDREN):
                    row = ((p * CHILDREN + child) * groups + s) * tile
                    value = cosine[child : child + 1, lanes] * incoming[p] - sine[child : child + 1, lanes] * turned[p]
                    shifted[row : row + tile, lanes] = value
    leaf_in = dot_t(shifted[...].astype(bf16), interp[...]).astype(bf16)
    back = dot_t(leaf_in, radiate[...]).reshape(boxes, groups, tile, both)
    own = back[..., :unknowns] - half_turn(back[..., unknowns:])
    for b in range(boxes):
        parts = [
            jnp.concatenate([own[b, s, t * group : (t + 1) * group] for s in range(groups)], axis=0)
            for t in range(2)
        ]
        out[b] = jnp.concatenate(parts, axis=1) + near[b]


def down(pieces, near, radiate, interp, cosine, sine, groups, slices):
    boxes, excite, both = near.shape
    return pl.pallas_call(
        lambda *refs: down_body(*refs, groups=groups, slices=slices),
        out_shape=jax.ShapeDtypeStruct(near.shape, f32),
        scratch_shapes=[pltpu.VMEM((boxes * excite * 2, interp.shape[1]), f32)],
        name="down",
    )(pieces, near, radiate, interp, cosine, sine)


def padded_2(array, sides, width):
    for axis, dim in sides:
        peers, length = (lax.axis_size(axis), array.shape[dim])
        up_pairs = [(i, (i + 1) % peers) for i in range(peers - 1)]
        down_pairs = [(j, i) for i, j in up_pairs]
        last = lax.slice_in_dim(array, length - width, length, axis=dim)
        leading = lax.slice_in_dim(array, 0, width, axis=dim)
        before = lax.ppermute(last, axis, up_pairs)
        after = lax.ppermute(leading, axis, down_pairs)
        array = jnp.concatenate([before, array, after], axis=dim)
    return array


def neighbour_sum(padded):
    core = padded[:, :, 1:-1, 1:-1]
    result = padded[:, :, 2:, 1:-1] + padded[:, :, :-2, 1:-1]
    result = result + padded[:, :, 1:-1, 2:] + padded[:, :, 1:-1, :-2]
    zero_layer = jnp.zeros(core.shape[:-1] + (1,), core.dtype)
    upper = jnp.concatenate([core[..., 1:], zero_layer], axis=-1)
    lower = jnp.concatenate([zero_layer, core[..., :-1]], axis=-1)
    return result + upper + lower


def relax_sweep(current, neighbours, source, diagonal_coef, loss_coef):
    real_part = diagonal_coef * current[0] - neighbours[0] - loss_coef * current[1]
    imag_part = diagonal_coef * current[1] - neighbours[1] + loss_coef * current[0]
    applied = jnp.stack([real_part, imag_part])
    return current + relaxation * (source - applied) / diagonal_coef


def relax(volume_field, source, material, mat_real, mat_loss):
    excite, cells_x, cells_y, cells_z = volume_field.shape[1:]
    diagonal_coef = jnp.full(material.shape, 6.0, f32)
    loss_coef = jnp.zeros(material.shape, f32)
    for kind in range(mat_real.shape[0]):
        present = material == kind
        diagonal_coef = diagonal_coef + jnp.where(present, mat_real[kind], 0.0)
        loss_coef = loss_coef + jnp.where(present, mat_loss[kind], 0.0)
    channels = 2 * excite
    stacked = jnp.concatenate(
        [
            volume_field.reshape(channels, cells_x, cells_y, cells_z),
            source.reshape(channels, cells_x, cells_y, cells_z),
            diagonal_coef[None],
            loss_coef[None],
        ],
        axis=0,
    )
    widened = padded_2(stacked.astype(bf16), (("space", 1), ("shard", 2)), 2).astype(f32)
    outer_field = widened[:channels].reshape(2, excite, cells_x + 4, cells_y + 4, cells_z)
    outer_source = widened[channels : 2 * channels, 1:-1, 1:-1].reshape(
        2, excite, cells_x + 2, cells_y + 2, cells_z
    )
    row_global = lax.axis_index("space") * cells_x - 1 + jnp.arange(cells_x + 2, dtype=jnp.int32)
    column_global = lax.axis_index("shard") * cells_y - 1 + jnp.arange(cells_y + 2, dtype=jnp.int32)
    row_inside = (row_global >= 0) & (row_global < cells_x * lax.axis_size("space"))
    column_inside = (column_global >= 0) & (column_global < cells_y * lax.axis_size("shard"))
    inside = row_inside[:, None, None] & column_inside[None, :, None]
    outer_diagonal = jnp.where(inside, widened[2 * channels, 1:-1, 1:-1], 1.0)
    outer_loss = widened[2 * channels + 1, 1:-1, 1:-1]
    first_sweep = relax_sweep(
        outer_field[:, :, 1:-1, 1:-1], neighbour_sum(outer_field), outer_source, outer_diagonal, outer_loss
    )
    first_sweep = jnp.where(inside, first_sweep, 0.0)
    return relax_sweep(
        first_sweep[:, :, 1:-1, 1:-1], neighbour_sum(first_sweep), source, diagonal_coef, loss_coef
    )


def shards(
    volume_field,
    source,
    material,
    mat_real,
    mat_loss,
    surface_map,
    near_boxes,
    near_blocks,
    radiate,
    interp,
    phase_angle,
    far_parents,
    far_kind,
    translate,
):
    every = ("space", "shard")
    groups = lax.axis_size("space")
    slices = lax.axis_size("shard")
    excite, cells_x, cells_y, cells_z = volume_field.shape[1:]
    cosine = jnp.cos(phase_angle)
    sine = jnp.sin(phase_angle)
    weights = radiate.reshape(2 * radiate.shape[1], radiate.shape[2])
    current = relax(volume_field, source, material, mat_real, mat_loss)
    currents, pieces = up(
        current.reshape(2 * excite, cells_x, cells_y, cells_z),
        surface_map,
        weights,
        interp,
        cosine,
        sine,
        groups,
        slices,
    )
    directed = lax.all_to_all(pieces, every, split_axis=0, concat_axis=0, tiled=True)
    combined = far_combine(far_parents, far_kind, directed, translate)
    incoming = lax.all_to_all(combined, every, split_axis=0, concat_axis=0, tiled=True)

    shard = lax.axis_index("shard")
    rank = lax.axis_index("space") * slices + shard
    boxes = near_boxes.shape[0]
    first, second = swap(currents, currents, "shard")
    offset = near_boxes - rank * boxes
    even = shard % 2 == 0
    above = jnp.where(even, 0, boxes)
    below = jnp.where(even, 2 * boxes, boxes) + boxes
    spots = offset + jnp.where(offset < 0, below, jnp.where(offset < boxes, 0, above))
    near = near_force(spots, currents, first, second, near_blocks)
    forcing = down(incoming, near, weights, interp, cosine, sine, groups, slices)
    return (current, forcing)


def solution(mesh):
    return jax.shard_map(
        shards,
        mesh=mesh,
        in_specs=(
            P(None, None, "space", "shard", None),
            P(None, None, "space", "shard", None),
            P("space", "shard", None),
            P(),
            P(),
            P(("space", "shard"), None),
            P(("space", "shard"), None),
            P(),
            P(),
            P(),
            P(),
            P(),
            P(),
            P(None, None, "shard"),
        ),
        out_specs=(P(None, None, "space", "shard", None), P(("space", "shard"), None, None)),
        check_vma=False,
    )
```

```python
import jax
import jax.numpy as jnp
from jax import lax
from jax.experimental import pallas as pl
from jax.experimental.pallas import tpu as pltpu
from jax.sharding import PartitionSpec as P

relaxation = 0.8
f32 = jnp.float32
bf16 = jnp.bfloat16
CHILDREN = 8


def dot(a, b):
    return jnp.dot(a, b, preferred_element_type=f32)


def dot_t(a, b):
    return lax.dot_general(a, b, (((1,), (1,)), ((), ())), preferred_element_type=f32)


def half_turn(v):
    half = v.shape[-2] // 2
    rows = lax.broadcasted_iota(jnp.int32, v.shape, v.ndim - 2)
    swapped = pltpu.roll(v, half, v.ndim - 2)
    return jnp.where(rows < half, -swapped, swapped)


def log2(n):
    assert n & (n - 1) == 0
    return n.bit_length() - 1


def swap_pairs(n, first):
    pairs = []
    for i in range(first, n - 1, 2):
        pairs += [(i, i + 1), (i + 1, i)]
    return pairs


def swap(for_even, for_odd, axis):
    n = lax.axis_size(axis)
    return [lax.ppermute(v, axis, swap_pairs(n, k)) for k, v in enumerate((for_even, for_odd))]


def second_sweep(mat_real, mat_loss, field, sweep, columns, column_a, source, kinds, got_first, got_second, out, beside, store, cx, cy):
    total = field.shape[0] // cy
    channels = total // cx
    excite = channels // 2
    plane = channels * cy
    even = is_even("space")
    a, b = coefficients(kinds[...], mat_real, mat_loss, 0)

    def halo(side, start, size):
        one = got_first[start : start + size, :].astype(f32)
        two = got_second[start : start + size, :].astype(f32)
        return jnp.where(even, two, one) if side == 0 else jnp.where(even, one, two)

    faces = (0, cx - 1)
    for y_side in range(2):
        beside[y_side] = columns[y_side]
        for x_side, x in enumerate(faces):
            corner = halo(x_side, 2 * plane + y_side * channels, channels)
            factor = column_a[y_side, x : x + 1, :]
            for c in range(0, channels, 8):
                rows = pl.ds(c * cx + x, 8, stride=cx)
                beside.at[y_side][rows, :] = beside.at[y_side][rows, :] + factor * corner[c : c + 8]
    face_a = []
    for x_side in range(2):
        kind = halo(x_side, 2 * plane + 2 * channels, cy).astype(jnp.int32)
        face_a.append(coefficients(kind, mat_real, mat_loss, 1)[0])
    for e in range(excite):
        v = []
        for p in range(2):
            c = p * excite + e
            own = [sweep[(c * cx + x) * cy : (c * cx + x + 1) * cy, :] for x in range(cx)]
            outer = []
            for x_side, x in enumerate(faces):
                own[x] = own[x] + a[x * cy : (x + 1) * cy] * halo(x_side, c * cy, cy)
                before = field[(c * cx + x) * cy : (c * cx + x + 1) * cy, :]
                outer.append(halo(x_side, plane + c * cy, cy) + face_a[x_side] * before)
            v.append([outer[0]] + own + [outer[1]])
        for x in range(cx):
            sums = []
            for p in range(2):
                at = (p * excite + e) * cx + x
                w = v[p][x + 1]
                n = source[at * cy : (at + 1) * cy, :] + along_z(w)
                n = n + along_y(w, beside[0, at : at + 1, :], beside[1, at : at + 1, :])
                sums.append(n + v[p][x] + v[p][x + 2])
            new = relaxed((v[0][x + 1], v[1][x + 1]), sums, a[x * cy : (x + 1) * cy], b[x * cy : (x + 1) * cy])
            for p in range(2):
                at = (p * excite + e) * cx + x
                out[at * cy : (at + 1) * cy, :] = new[p]
                store(p, e, x, new[p])


def up_body(
    mat_real, mat_loss, field, sweep, columns, column_a, source, kinds, got_first, got_second,
    smap, radiate, interp, cosine, sine, volume, cur, out, beside, cells, rows, *, cx, cy, groups, slices
):
    nz = field.shape[1]
    channels = field.shape[0] // (cx * cy)
    excite = channels // 2
    group = excite // groups
    boxes, unknowns = smap.shape

    def store(t, e, x, value):
        place = (e // group) * 2 * group + t * group + e % group
        for y in range(0, cy, 8):
            cells.at[x][pl.ds(y * channels + place, 8, stride=channels), :] = value[y : y + 8]

    second_sweep(
        mat_real, mat_loss, field, sweep, columns, column_a, source, kinds, got_first, got_second,
        volume, beside, store, cx, cy
    )
    lhs = jnp.concatenate([cells[x].astype(bf16) for x in range(cx)], axis=1)
    pair = 2
    for b in range(0, boxes, pair):
        keys = jnp.concatenate([smap[b + j : b + j + 1, :] for j in range(pair)], axis=1)
        key_z = keys & (nz - 1)
        key_y = (keys >> log2(nz)) & (cy - 1)
        key_x = keys >> (log2(nz) + log2(cy))
        level = lax.broadcasted_iota(jnp.int32, (nz, pair * unknowns), 0)
        hot = [
            jnp.where(level == jnp.where(key_x == x, key_z, -1), 1.0, 0.0).astype(bf16) for x in range(cx)
        ]
        picked = dot(lhs, jnp.concatenate(hot, axis=0))
        found = jnp.zeros((channels, pair * unknowns), f32)
        for y in range(cy):
            found = jnp.where(key_y == y, picked[y * channels : (y + 1) * channels], found)
        for j in range(pair):
            own = found[:, j * unknowns : (j + 1) * unknowns].reshape(groups, 2 * group, unknowns)
            turned = half_turn(own)
            both = jnp.concatenate([own, turned], axis=2).reshape(channels, 2 * unknowns)
            rows[(b + j) * channels : (b + j + 1) * channels, :] = both.astype(bf16)
            parts = [
                jnp.concatenate([own[s, t * group : (t + 1) * group] for s in range(groups)], axis=0)
                for t in range(2)
            ]
            cur[b + j] = jnp.concatenate(parts, axis=1).astype(bf16)
    leaf = dot(rows[...], radiate[...]).astype(bf16)
    directions = interp.shape[1]
    width = directions // slices
    tile = max(width, 256)
    parents = boxes // CHILDREN
    for n in range(0, directions, tile):
        spread = dot(leaf, interp[:, n : n + tile]).reshape(parents, CHILDREN, groups, 2 * group, tile)
        along = jnp.zeros((parents, groups, 2 * group, tile), f32)
        across = jnp.zeros((parents, groups, 2 * group, tile), f32)
        for child in range(CHILDREN):
            along = along + cosine[child : child + 1, n : n + tile] * spread[:, child]
            across = across + sine[child : child + 1, n : n + tile] * spread[:, child]
        whole = (along + half_turn(across)).astype(bf16)
        for s in range(groups):
            piece = jnp.concatenate([whole[p, s] for p in range(parents)], axis=0)
            for k in range(tile // width):
                out[s * slices + n // width + k] = piece[:, k * width : (k + 1) * width]


def up(volume_args, smap, radiate, interp, cosine, sine, cx, cy, groups, slices):
    field = volume_args[2]
    nz = field.shape[1]
    total = field.shape[0] // cy
    channels = total // cx
    boxes, unknowns = smap.shape
    width = interp.shape[1] // slices
    piece_rows = boxes // CHILDREN * (channels // groups)
    smem = pl.BlockSpec(memory_space=pltpu.SMEM)
    vmem = pl.BlockSpec(memory_space=pltpu.VMEM)
    return pl.pallas_call(
        lambda *refs: up_body(*refs, cx=cx, cy=cy, groups=groups, slices=slices),
        out_shape=(
            jax.ShapeDtypeStruct(field.shape, f32),
            jax.ShapeDtypeStruct((boxes, channels // 2, 2 * unknowns), bf16),
            jax.ShapeDtypeStruct((groups * slices, piece_rows, width), bf16),
        ),
        in_specs=[smem, smem] + [vmem] * 13,
        out_specs=(vmem,) * 3,
        scratch_shapes=[
            pltpu.VMEM((2, total, nz), f32),
            pltpu.VMEM((cx, cy * channels, nz), f32),
            pltpu.VMEM((boxes * channels, 2 * unknowns), bf16),
        ],
        name="up",
    )(*volume_args, smap, radiate, interp, cosine, sine)


def far_body(lists, kinds, sources, translate, out, plain, turned):
    targets, far = lists.shape
    devices, piece_rows, width = sources.shape
    per = targets // devices
    tile = piece_rows // per
    wide = sources[...].astype(f32).reshape(targets, tile, width)
    plain[...] = wide
    turned[...] = half_turn(wide)

    def one(d, _):
        results = []
        for j in range(per):
            t = d * per + j
            total = jnp.zeros((tile, width), f32)
            for f in range(far):
                p = lists[t, f]
                k = kinds[t, f]
                factor = translate[k]
                total = total + factor[0:1] * plain[p] + factor[1:2] * turned[p]
            results.append(total)
        out[d] = jnp.concatenate(results, axis=0).astype(bf16)
        return 0

    lax.fori_loop(0, devices, one, 0)


def far_combine(lists, kinds, sources, translate):
    targets = lists.shape[0]
    devices, piece_rows, width = sources.shape
    tile = piece_rows // (targets // devices)
    smem = pl.BlockSpec(memory_space=pltpu.SMEM)
    vmem = pl.BlockSpec(memory_space=pltpu.VMEM)
    return pl.pallas_call(
        far_body,
        out_shape=jax.ShapeDtypeStruct(sources.shape, bf16),
        in_specs=[smem, smem, vmem, vmem],
        out_specs=vmem,
        scratch_shapes=[pltpu.VMEM((targets, tile, width), f32)] * 2,
        name="far",
    )(lists, kinds, sources, translate)


def near_body(spots, own, first, second, blocks, out, boxes_all, rows):
    boxes, excite, k = own.shape
    slots = spots.shape[1]
    boxes_all[0:boxes] = own[...]
    boxes_all[boxes : 2 * boxes] = first[...]
    boxes_all[2 * boxes : 3 * boxes] = second[...]
    for b in range(boxes):
        for s in range(slots):
            rows[b * excite : (b + 1) * excite, s * k : (s + 1) * k] = boxes_all[spots[b, s]]
    out[...] = dot(rows[...], blocks[...]).reshape(out.shape)


def near_force(spots, own, first, second, blocks):
    boxes, excite, k = own.shape
    slots = spots.shape[1]
    smem = pl.BlockSpec(memory_space=pltpu.SMEM)
    vmem = pl.BlockSpec(memory_space=pltpu.VMEM)
    return pl.pallas_call(
        near_body,
        out_shape=jax.ShapeDtypeStruct((boxes, excite, k), f32),
        in_specs=[smem, vmem, vmem, vmem, vmem],
        out_specs=vmem,
        scratch_shapes=[
            pltpu.VMEM((3 * boxes, excite, k), bf16),
            pltpu.VMEM((boxes * excite, slots * k), bf16),
        ],
        name="near",
    )(spots, own, first, second, blocks.reshape(slots * k, k))


def down_body(pieces, near, radiate, interp, cosine, sine, out, shifted, *, groups, slices):
    _, piece_rows, width = pieces.shape
    boxes, excite, both = out.shape
    unknowns = both // 2
    group = excite // groups
    tile = 2 * group
    parents = boxes // CHILDREN
    for h in range(slices):
        lanes = slice(h * width, (h + 1) * width)
        for s in range(groups):
            incoming = pieces[s * slices + h].astype(f32).reshape(parents, tile, width)
            turned = half_turn(incoming)
            for p in range(parents):
                for child in range(0, CHILDREN):
                    row = ((p * CHILDREN + child) * groups + s) * tile
                    value = cosine[child : child + 1, lanes] * incoming[p] - sine[child : child + 1, lanes] * turned[p]
                    shifted[row : row + tile, lanes] = value
    leaf_in = dot_t(shifted[...].astype(bf16), interp[...]).astype(bf16)
    back = dot_t(leaf_in, radiate[...]).reshape(boxes, groups, tile, both)
    own = back[..., :unknowns] - half_turn(back[..., unknowns:])
    for b in range(boxes):
        parts = [
            jnp.concatenate([own[b, s, t * group : (t + 1) * group] for s in range(groups)], axis=0)
            for t in range(2)
        ]
        out[b] = jnp.concatenate(parts, axis=1) + near[b]


def down(pieces, near, radiate, interp, cosine, sine, groups, slices):
    boxes, excite, both = near.shape
    return pl.pallas_call(
        lambda *refs: down_body(*refs, groups=groups, slices=slices),
        out_shape=jax.ShapeDtypeStruct(near.shape, f32),
        scratch_shapes=[pltpu.VMEM((boxes * excite * 2, interp.shape[1]), f32)],
        name="down",
    )(pieces, near, radiate, interp, cosine, sine)


def is_even(axis):
    return lax.rem(lax.axis_index(axis), 2) == 0


def coefficients(kinds, mat_real, mat_loss, base):
    diagonal = jnp.full(kinds.shape, 6.0, f32)
    loss = jnp.zeros(kinds.shape, f32)
    for k in range(mat_real.shape[0]):
        present = kinds == k + base
        diagonal = jnp.where(present, 6.0 + mat_real[k], diagonal)
        loss = jnp.where(present, mat_loss[k], loss)
    a = relaxation / diagonal
    if base > 0:
        a = jnp.where(kinds < base, 0.0, a)
    return a, a * loss


def along_z(v):
    lanes = v.shape[-1]
    lane = lax.broadcasted_iota(jnp.int32, v.shape, v.ndim - 1)
    lower = jnp.where(lane == 0, 0.0, pltpu.roll(v, 1, v.ndim - 1))
    upper = jnp.where(lane == lanes - 1, 0.0, pltpu.roll(v, lanes - 1, v.ndim - 1))
    return lower + upper


def along_y(v, low, high):
    rows = v.shape[0]
    row = lax.broadcasted_iota(jnp.int32, v.shape, 0)
    lower = jnp.where(row == 0, low, pltpu.roll(v, 1, 0))
    upper = jnp.where(row == rows - 1, high, pltpu.roll(v, rows - 1, 0))
    return lower + upper


def relaxed(v, total, a, b):
    keep = 1.0 - relaxation
    return (
        keep * v[0] + a * total[0] + b * v[1],
        keep * v[1] + a * total[1] - b * v[0],
    )


def edge_body(field, source, kinds, first, second, *, cx, cy):
    total = field.shape[0] // cy
    even = is_even("shard")

    def face(inner, outer):
        def layer(ref, y):
            return jnp.concatenate(
                [ref[pl.ds(r * cy + y, 8, stride=cy), :] for r in range(0, total, 8)], axis=0
            )

        kind = kinds[pl.ds(outer, cx, stride=cy), :].astype(f32) + 1.0
        kind = jnp.concatenate([kind] * (16 // cx), axis=0)
        return jnp.concatenate([layer(field, inner), layer(field, outer), layer(source, outer), kind], axis=0)

    high = face(cy - 2, cy - 1)
    low = face(1, 0)
    first[...] = jnp.where(even, high, low).astype(bf16)
    second[...] = jnp.where(even, low, high).astype(bf16)


def edges(field, source, kinds, cx, cy):
    rows = 3 * (field.shape[0] // cy) + 16
    message = jax.ShapeDtypeStruct((rows, field.shape[1]), bf16)
    return pl.pallas_call(
        lambda *refs: edge_body(*refs, cx=cx, cy=cy), out_shape=(message, message), name="edges"
    )(field, source, kinds)


def first_body(
    mat_real, mat_loss, field, source, kinds, got_first, got_second,
    sweep, columns, column_a, to_first, to_second, near, *, cx, cy
):
    total = field.shape[0] // cy
    channels = total // cx
    excite = channels // 2
    even_y = is_even("shard")
    a, b = coefficients(kinds[...], mat_real, mat_loss, 0)
    row = lax.broadcasted_iota(jnp.int32, (8, field.shape[1]), 0) & (cx - 1)
    one = got_first[...].astype(f32)
    two = got_second[...].astype(f32)
    for side, own_y in ((0, 0), (1, cy - 1)):
        halo = jnp.where(even_y, two, one) if side == 0 else jnp.where(even_y, one, two)
        kind = halo[3 * total : 3 * total + 8].astype(jnp.int32)
        col_a, col_b = coefficients(kind, mat_real, mat_loss, 1)
        column_a[side] = col_a
        near[side] = halo[total : 2 * total]
        for j in range(0, total // 2, 8):
            v, sums = [], []
            for part in range(2):
                at = part * (total // 2) + j
                beside = halo[total + at : total + at + 8]
                nbr = halo[at : at + 8] + halo[2 * total + at : 2 * total + at + 8] + along_z(beside)
                nbr = nbr + field[pl.ds(at * cy + own_y, 8, stride=cy), :]
                nbr = nbr + jnp.where(row == 0, 0.0, pltpu.roll(beside, 1, 0))
                nbr = nbr + jnp.where(row == cx - 1, 0.0, pltpu.roll(beside, 7, 0))
                v.append(beside)
                sums.append(nbr)
            new = relaxed(v, sums, col_a, col_b)
            for part in range(2):
                at = part * (total // 2) + j
                columns[side, at : at + 8] = new[part]
    for e in range(excite):
        v = [
            [field[at * cy : (at + 1) * cy, :] for at in range((p * excite + e) * cx, (p * excite + e + 1) * cx)]
            for p in range(2)
        ]
        for x in range(cx):
            sums = []
            for p in range(2):
                at = (p * excite + e) * cx + x
                n = source[at * cy : (at + 1) * cy, :] + along_z(v[p][x])
                n = n + along_y(v[p][x], near[0, at : at + 1, :], near[1, at : at + 1, :])
                if x > 0:
                    n = n + v[p][x - 1]
                if x < cx - 1:
                    n = n + v[p][x + 1]
                sums.append(n)
            new = relaxed((v[0][x], v[1][x]), sums, a[x * cy : (x + 1) * cy], b[x * cy : (x + 1) * cy])
            for p in range(2):
                at = (p * excite + e) * cx + x
                sweep[at * cy : (at + 1) * cy, :] = new[p]
    even_x = is_even("space")
    plane = channels * cy
    for message, x in ((to_first, jnp.where(even_x, cx - 1, 0)), (to_second, jnp.where(even_x, 0, cx - 1))):
        for c in range(channels):
            rows = pl.ds(pl.multiple_of((c * cx + x) * cy, cy), cy)
            message[c * cy : (c + 1) * cy, :] = field[rows, :].astype(bf16)
            message[plane + c * cy : plane + (c + 1) * cy, :] = sweep[rows, :].astype(bf16)
        for side in range(2):
            corner = jnp.concatenate(
                [near.at[side][pl.ds(c * cx + x, 8, stride=cx), :] for c in range(0, channels, 8)], axis=0
            )
            at = 2 * plane + side * channels
            message[at : at + channels, :] = corner.astype(bf16)
        at = 2 * plane + 2 * channels
        kind = kinds[pl.ds(pl.multiple_of(x * cy, cy), cy), :].astype(f32) + 1.0
        message[at : at + cy, :] = kind.astype(bf16)


def first_sweep(mat_real, mat_loss, field, source, kinds, got_first, got_second, cx, cy):
    total, nz = field.shape[0] // cy, field.shape[1]
    channels = total // cx
    smem = pl.BlockSpec(memory_space=pltpu.SMEM)
    vmem = pl.BlockSpec(memory_space=pltpu.VMEM)
    message = jax.ShapeDtypeStruct((2 * channels * cy + 2 * channels + cy, nz), bf16)
    return pl.pallas_call(
        lambda *refs: first_body(*refs, cx=cx, cy=cy),
        out_shape=(
            jax.ShapeDtypeStruct(field.shape, f32),
            jax.ShapeDtypeStruct((2, total, nz), f32),
            jax.ShapeDtypeStruct((2, 8, nz), f32),
            message,
            message,
        ),
        in_specs=[smem, smem] + [vmem] * 5,
        out_specs=(vmem,) * 5,
        scratch_shapes=[pltpu.VMEM((2, total, nz), f32)],
        name="first_sweep",
    )(mat_real, mat_loss, field, source, kinds, got_first, got_second)


def shards(
    volume_field,
    source,
    material,
    mat_real,
    mat_loss,
    surface_map,
    near_boxes,
    near_blocks,
    radiate,
    interp,
    phase_angle,
    far_parents,
    far_kind,
    translate,
):
    every = ("space", "shard")
    groups = lax.axis_size("space")
    slices = lax.axis_size("shard")
    excite, cells_x, cells_y, cells_z = volume_field.shape[1:]
    cosine = jnp.cos(phase_angle)
    sine = jnp.sin(phase_angle)
    weights = radiate.reshape(2 * radiate.shape[1], radiate.shape[2])
    field = volume_field.reshape(-1, cells_z)
    flat_source = source.reshape(-1, cells_z)
    kinds = material.reshape(-1, cells_z)
    got_y = swap(*edges(field, flat_source, kinds, cells_x, cells_y), "shard")
    sweep, columns, column_a, *to_x = first_sweep(
        mat_real, mat_loss, field, flat_source, kinds, *got_y, cells_x, cells_y
    )
    got_x = swap(*to_x, "space")
    current, currents, pieces = up(
        (mat_real, mat_loss, field, sweep, columns, column_a, flat_source, kinds, *got_x),
        surface_map,
        weights,
        interp,
        cosine,
        sine,
        cells_x,
        cells_y,
        groups,
        slices,
    )
    directed = lax.all_to_all(pieces, every, split_axis=0, concat_axis=0, tiled=True)
    combined = far_combine(far_parents, far_kind, directed, translate)
    incoming = lax.all_to_all(combined, every, split_axis=0, concat_axis=0, tiled=True)

    shard = lax.axis_index("shard")
    rank = lax.axis_index("space") * slices + shard
    boxes = near_boxes.shape[0]
    first, second = swap(currents, currents, "shard")
    offset = near_boxes - rank * boxes
    even = shard % 2 == 0
    above = jnp.where(even, 0, boxes)
    below = jnp.where(even, 2 * boxes, boxes) + boxes
    spots = offset + jnp.where(offset < 0, below, jnp.where(offset < boxes, 0, above))
    near = near_force(spots, currents, first, second, near_blocks)
    forcing = down(incoming, near, weights, interp, cosine, sine, groups, slices)
    return (current.reshape(volume_field.shape), forcing)


def solution(mesh):
    return jax.shard_map(
        shards,
        mesh=mesh,
        in_specs=(
            P(None, None, "space", "shard", None),
            P(None, None, "space", "shard", None),
            P("space", "shard", None),
            P(),
            P(),
            P(("space", "shard"), None),
            P(("space", "shard"), None),
            P(),
            P(),
            P(),
            P(),
            P(),
            P(),
            P(None, None, "shard"),
        ),
        out_specs=(P(None, None, "space", "shard", None), P(("space", "shard"), None, None)),
        check_vma=False,
    )
```

```python
import jax
import jax.numpy as jnp
from jax import lax
from jax.experimental import pallas as pl
from jax.experimental.pallas import tpu as pltpu
from jax.sharding import PartitionSpec as P

relaxation = 0.8
f32 = jnp.float32
bf16 = jnp.bfloat16
CHILDREN = 8


def held(*arrays):
    return [pltpu.with_memory_space_constraint(a, pltpu.VMEM) for a in arrays]


def left(*arrays):
    return [pltpu.with_memory_space_constraint(a, pltpu.HBM) for a in arrays]


def params(mib):
    return pltpu.CompilerParams(vmem_limit_bytes=mib << 20)


def dot(a, b):
    return jnp.dot(a, b, preferred_element_type=f32)


def dot_t(a, b):
    return lax.dot_general(a, b, (((1,), (1,)), ((), ())), preferred_element_type=f32)


def half_turn(v):
    half = v.shape[-2] // 2
    rows = lax.broadcasted_iota(jnp.int32, v.shape, v.ndim - 2)
    swapped = pltpu.roll(v, half, v.ndim - 2)
    return jnp.where(rows < half, -swapped, swapped)


def log2(n):
    assert n & (n - 1) == 0
    return n.bit_length() - 1


def prepare(angle, smap, cx, cy, nz):
    boxes, unknowns = smap.shape

    def body(angle, smap, cosine, sine, chosen, depth):
        cosine[...] = jnp.cos(angle[...])
        sine[...] = jnp.sin(angle[...])
        level = lax.broadcasted_iota(jnp.int32, (nz, unknowns), 0)
        for b in range(boxes):
            key = smap[b : b + 1, :]
            key_z = key & (nz - 1)
            key_x = key >> (log2(nz) + log2(cy))
            lanes = slice(b * unknowns, (b + 1) * unknowns)
            for x in range(cx):
                hit = level == jnp.where(key_x == x, key_z, -1)
                chosen[x * nz : (x + 1) * nz, lanes] = jnp.where(hit, 1.0, 0.0).astype(bf16)
            depth[:, lanes] = jnp.broadcast_to((key >> log2(nz)) & (cy - 1), (8, unknowns))

    shape = pltpu.VMEM(angle.shape, f32)
    return pl.pallas_call(
        body,
        out_shape=(
            shape,
            shape,
            pltpu.VMEM((cx * nz, boxes * unknowns), bf16),
            pltpu.VMEM((8, boxes * unknowns), jnp.int32),
        ),
        compiler_params=params(6),
        name="prepare",
    )(*held(angle, smap))


def swap_pairs(n, first):
    pairs = []
    for i in range(first, n - 1, 2):
        pairs += [(i, i + 1), (i + 1, i)]
    return pairs


def swap(for_even, for_odd, axis):
    n = lax.axis_size(axis)
    far = lax.ppermute(for_odd, axis, swap_pairs(n, 1))
    return lax.ppermute(for_even, axis, swap_pairs(n, 0)), far


def second_sweep(mat_real, mat_loss, field, sweep, columns, column_a, source, kinds, got_first, got_second, out, beside, store, cx, cy):
    total = field.shape[0] // cy
    channels = total // cx
    excite = channels // 2
    plane = channels * cy
    even = is_even("space")
    a, b = coefficients(kinds[...], mat_real, mat_loss, 0)

    def halo(side, start, size):
        one = got_first[start : start + size, :].astype(f32)
        two = got_second[start : start + size, :].astype(f32)
        return jnp.where(even, two, one) if side == 0 else jnp.where(even, one, two)

    faces = (0, cx - 1)
    for y_side in range(2):
        beside[y_side] = columns[y_side]
        for x_side, x in enumerate(faces):
            corner = halo(x_side, 2 * plane + y_side * channels, channels)
            factor = column_a[y_side, x : x + 1, :]
            for c in range(0, channels, 8):
                rows = pl.ds(c * cx + x, 8, stride=cx)
                beside.at[y_side][rows, :] = beside.at[y_side][rows, :] + factor * corner[c : c + 8]
    face_a = []
    for x_side in range(2):
        kind = halo(x_side, 2 * plane + 2 * channels, cy).astype(jnp.int32)
        face_a.append(coefficients(kind, mat_real, mat_loss, 1)[0])
    for e in range(excite):
        v = []
        for p in range(2):
            c = p * excite + e
            own = [sweep[(c * cx + x) * cy : (c * cx + x + 1) * cy, :] for x in range(cx)]
            outer = []
            for x_side, x in enumerate(faces):
                own[x] = own[x] + a[x * cy : (x + 1) * cy] * halo(x_side, c * cy, cy)
                before = field[(c * cx + x) * cy : (c * cx + x + 1) * cy, :]
                outer.append(halo(x_side, plane + c * cy, cy) + face_a[x_side] * before)
            v.append([outer[0]] + own + [outer[1]])
        for x in range(cx):
            sums = []
            for p in range(2):
                at = (p * excite + e) * cx + x
                w = v[p][x + 1]
                n = source[at * cy : (at + 1) * cy, :] + along_z(w)
                n = n + along_y(w, beside[0, at : at + 1, :], beside[1, at : at + 1, :])
                sums.append(n + v[p][x] + v[p][x + 2])
            new = relaxed((v[0][x + 1], v[1][x + 1]), sums, a[x * cy : (x + 1) * cy], b[x * cy : (x + 1) * cy])
            for p in range(2):
                at = (p * excite + e) * cx + x
                out[at * cy : (at + 1) * cy, :] = new[p]
                store(p, e, x, new[p])


def up_body(
    mat_real, mat_loss, field, sweep, columns, column_a, source, kinds, got_first, got_second,
    chosen, depth, radiate, interp, cosine, sine, volume, cur, out, beside, cells, rows, fresh, sem,
    *, cx, cy, groups, slices
):
    nz = field.shape[1]
    channels = field.shape[0] // (cx * cy)
    excite = channels // 2
    group = excite // groups
    boxes = cur.shape[0]
    unknowns = depth.shape[1] // boxes

    def store(t, e, x, value):
        place = (e // group) * 2 * group + t * group + e % group
        for y in range(0, cy, 8):
            cells.at[x][pl.ds(y * channels + place, 8, stride=channels), :] = value[y : y + 8]

    second_sweep(
        mat_real, mat_loss, field, sweep, columns, column_a, source, kinds, got_first, got_second,
        fresh, beside, store, cx, cy
    )
    leaving = pltpu.make_async_copy(fresh, volume, sem)
    leaving.start()
    lhs = jnp.concatenate([cells[x].astype(bf16) for x in range(cx)], axis=1)
    pair = 2
    for b in range(0, boxes, pair):
        lanes = slice(b * unknowns, (b + pair) * unknowns)
        picked = dot(lhs, chosen[:, lanes])
        key_y = jnp.concatenate([depth[:, lanes]] * (channels // 8), axis=0)
        found = jnp.zeros((channels, pair * unknowns), f32)
        for y in range(cy):
            found = jnp.where(key_y == y, picked[y * channels : (y + 1) * channels], found)
        for j in range(pair):
            own = found[:, j * unknowns : (j + 1) * unknowns].reshape(groups, 2 * group, unknowns)
            turned = half_turn(own)
            both = jnp.concatenate([own, turned], axis=2).reshape(channels, 2 * unknowns)
            rows[(b + j) * channels : (b + j + 1) * channels, :] = both.astype(bf16)
            parts = [
                jnp.concatenate([own[s, t * group : (t + 1) * group] for s in range(groups)], axis=0)
                for t in range(2)
            ]
            cur[b + j] = jnp.concatenate(parts, axis=1).astype(bf16)
    leaf = dot(rows[...], radiate[...]).astype(bf16)
    directions = interp.shape[1]
    width = directions // slices
    tile = max(width, 256)
    parents = boxes // CHILDREN
    for n in range(0, directions, tile):
        spread = dot(leaf, interp[:, n : n + tile]).reshape(parents, CHILDREN, groups, 2 * group, tile)
        along = jnp.zeros((parents, groups, 2 * group, tile), f32)
        across = jnp.zeros((parents, groups, 2 * group, tile), f32)
        for child in range(CHILDREN):
            along = along + cosine[child : child + 1, n : n + tile] * spread[:, child]
            across = across + sine[child : child + 1, n : n + tile] * spread[:, child]
        whole = (along + half_turn(across)).astype(bf16)
        for s in range(groups):
            piece = jnp.concatenate([whole[p, s] for p in range(parents)], axis=0)
            for k in range(tile // width):
                out[s * slices + n // width + k] = piece[:, k * width : (k + 1) * width]
    leaving.wait()


def up(volume_args, chosen, depth, boxes, radiate, interp, cosine, sine, cx, cy, groups, slices):
    field = volume_args[2]
    nz = field.shape[1]
    total = field.shape[0] // cy
    channels = total // cx
    unknowns = depth.shape[1] // boxes
    width = interp.shape[1] // slices
    piece_rows = boxes // CHILDREN * (channels // groups)
    smem = pl.BlockSpec(memory_space=pltpu.SMEM)
    vmem = pl.BlockSpec(memory_space=pltpu.VMEM)
    return pl.pallas_call(
        lambda *refs: up_body(*refs, cx=cx, cy=cy, groups=groups, slices=slices),
        out_shape=(
            pltpu.HBM(field.shape, f32),
            pltpu.VMEM((boxes, channels // 2, 2 * unknowns), bf16),
            pltpu.VMEM((groups * slices, piece_rows, width), bf16),
        ),
        in_specs=[smem, smem] + [vmem] * 14,
        out_specs=(pl.BlockSpec(memory_space=pltpu.HBM), vmem, vmem),
        scratch_shapes=[
            pltpu.VMEM((2, total, nz), f32),
            pltpu.VMEM((cx, cy * channels, nz), f32),
            pltpu.VMEM((boxes * channels, 2 * unknowns), bf16),
            pltpu.VMEM(field.shape, f32),
            pltpu.SemaphoreType.DMA(()),
        ],
        compiler_params=params(16), name="up",
    )(*volume_args[:2], *held(*volume_args[2:], chosen, depth, radiate, interp, cosine, sine))


def far_body(lists, kinds, sources, translate, out, plain, turned):
    far, targets = lists.shape
    devices, piece_rows, width = sources.shape
    per = targets // devices
    tile = piece_rows // per
    wide = sources[...].astype(f32).reshape(targets, tile, width)
    plain[...] = wide
    turned[...] = half_turn(wide)

    def one(d, _):
        results = []
        for j in range(per):
            t = d * per + j
            total = jnp.zeros((tile, width), f32)
            for f in range(far):
                p = lists[f, t]
                k = kinds[f, t]
                factor = translate[k]
                total = total + factor[0:1] * plain[p] + factor[1:2] * turned[p]
            results.append(total)
        out[d] = jnp.concatenate(results, axis=0).astype(bf16)
        return 0

    lax.fori_loop(0, devices, one, 0)


def far_combine(lists, kinds, sources, translate):
    targets = lists.shape[1]
    devices, piece_rows, width = sources.shape
    tile = piece_rows // (targets // devices)
    smem = pl.BlockSpec(memory_space=pltpu.SMEM)
    vmem = pl.BlockSpec(memory_space=pltpu.VMEM)
    return pl.pallas_call(
        far_body,
        out_shape=pltpu.VMEM(sources.shape, bf16),
        in_specs=[smem, smem, vmem, vmem],
        out_specs=vmem,
        scratch_shapes=[pltpu.VMEM((targets, tile, width), f32)] * 2,
        compiler_params=params(8), name="far",
    )(lists, kinds, *held(sources, translate))


def near_body(lists, own, first, second, blocks, angle, out, cosine, sine, boxes_all, rows):
    cosine[...] = jnp.cos(angle[...])
    sine[...] = jnp.sin(angle[...])
    boxes, excite, k = own.shape
    slots = lists.shape[0]
    shard = lax.axis_index("shard")
    base = (lax.axis_index("space") * lax.axis_size("shard") + shard) * boxes
    even = lax.rem(shard, 2) == 0
    above = jnp.where(even, 0, boxes)
    below = jnp.where(even, 3 * boxes, 2 * boxes)
    boxes_all[0:boxes] = own[...]
    boxes_all[boxes : 2 * boxes] = first[...]
    boxes_all[2 * boxes : 3 * boxes] = second[...]
    for b in range(boxes):
        for s in range(slots):
            away = lists[s, b] - base
            spot = away + jnp.where(away < 0, below, jnp.where(away < boxes, 0, above))
            rows[b * excite : (b + 1) * excite, s * k : (s + 1) * k] = boxes_all[spot]
    out[...] = dot(rows[...], blocks[...]).reshape(out.shape)


def near_force(lists, own, first, second, blocks, angle):
    boxes, excite, k = own.shape
    slots = lists.shape[0]
    smem = pl.BlockSpec(memory_space=pltpu.SMEM)
    vmem = pl.BlockSpec(memory_space=pltpu.VMEM)
    return pl.pallas_call(
        near_body,
        out_shape=(pltpu.VMEM((boxes, excite, k), f32),) + (pltpu.VMEM(angle.shape, f32),) * 2,
        in_specs=[smem] + [vmem] * 5,
        out_specs=(vmem,) * 3,
        scratch_shapes=[
            pltpu.VMEM((3 * boxes, excite, k), bf16),
            pltpu.VMEM((boxes * excite, slots * k), bf16),
        ],
        compiler_params=params(6), name="near",
    )(lists, *held(own, first, second, blocks.reshape(slots * k, k), angle))


def down_body(pieces, near, radiate, interp, cosine, sine, out, shifted, *, groups, slices):
    _, piece_rows, width = pieces.shape
    boxes, excite, both = out.shape
    unknowns = both // 2
    group = excite // groups
    tile = 2 * group
    parents = boxes // CHILDREN
    for h in range(slices):
        lanes = slice(h * width, (h + 1) * width)
        for s in range(groups):
            incoming = pieces[s * slices + h].astype(f32).reshape(parents, tile, width)
            turned = half_turn(incoming)
            for p in range(parents):
                for child in range(0, CHILDREN):
                    row = ((p * CHILDREN + child) * groups + s) * tile
                    value = cosine[child : child + 1, lanes] * incoming[p] - sine[child : child + 1, lanes] * turned[p]
                    shifted[row : row + tile, lanes] = value
    leaf_in = dot_t(shifted[...].astype(bf16), interp[...]).astype(bf16)
    back = dot_t(leaf_in, radiate[...]).reshape(boxes, groups, tile, both)
    own = back[..., :unknowns] - half_turn(back[..., unknowns:])
    for b in range(boxes):
        parts = [
            jnp.concatenate([own[b, s, t * group : (t + 1) * group] for s in range(groups)], axis=0)
            for t in range(2)
        ]
        out[b] = jnp.concatenate(parts, axis=1) + near[b]


def down(pieces, near, radiate, interp, cosine, sine, groups, slices):
    boxes, excite, both = near.shape
    return pl.pallas_call(
        lambda *refs: down_body(*refs, groups=groups, slices=slices),
        out_shape=jax.ShapeDtypeStruct(near.shape, f32),
        scratch_shapes=[pltpu.VMEM((boxes * excite * 2, interp.shape[1]), f32)],
        compiler_params=params(16), name="down",
    )(*held(pieces, near, radiate, interp, cosine, sine))


def is_even(axis):
    return lax.rem(lax.axis_index(axis), 2) == 0


def coefficients(kinds, mat_real, mat_loss, base):
    diagonal = jnp.full(kinds.shape, 6.0, f32)
    loss = jnp.zeros(kinds.shape, f32)
    for k in range(mat_real.shape[0]):
        present = kinds == k + base
        diagonal = jnp.where(present, 6.0 + mat_real[k], diagonal)
        loss = jnp.where(present, mat_loss[k], loss)
    a = relaxation / diagonal
    if base > 0:
        a = jnp.where(kinds < base, 0.0, a)
    return a, a * loss


def along_z(v):
    lanes = v.shape[-1]
    lane = lax.broadcasted_iota(jnp.int32, v.shape, v.ndim - 1)
    lower = jnp.where(lane == 0, 0.0, pltpu.roll(v, 1, v.ndim - 1))
    upper = jnp.where(lane == lanes - 1, 0.0, pltpu.roll(v, lanes - 1, v.ndim - 1))
    return lower + upper


def along_y(v, low, high):
    rows = v.shape[0]
    row = lax.broadcasted_iota(jnp.int32, v.shape, 0)
    lower = jnp.where(row == 0, low, pltpu.roll(v, 1, 0))
    upper = jnp.where(row == rows - 1, high, pltpu.roll(v, rows - 1, 0))
    return lower + upper


def relaxed(v, total, a, b):
    keep = 1.0 - relaxation
    return (
        keep * v[0] + a * total[0] + b * v[1],
        keep * v[1] + a * total[1] - b * v[0],
    )


def edge_body(field, source, kinds, first, second, layers, kind_rows, sem, kind_sem):
    total, cy, _ = field.shape
    cx = kinds.shape[0]
    even = is_even("shard")
    faces = ((cy - 2, cy - 1), (1, 0))
    copies = []
    for i, (inner, outer) in enumerate(faces):
        for k, (ref, y) in enumerate(((field, inner), (field, outer), (source, outer))):
            copies.append(pltpu.make_async_copy(ref.at[:, y], layers.at[i, k], sem.at[i, k]))
        copies.append(pltpu.make_async_copy(kinds.at[:, outer], kind_rows.at[i], kind_sem.at[i]))
    for copy in copies:
        copy.start()
    for copy in copies:
        copy.wait()
    for k in range(3):
        rows = slice(k * total, (k + 1) * total)
        first[rows, :] = jnp.where(even, layers[0, k], layers[1, k]).astype(bf16)
        second[rows, :] = jnp.where(even, layers[1, k], layers[0, k]).astype(bf16)
    kind = [jnp.concatenate([kind_rows[i].astype(f32) + 1.0] * (16 // cx), axis=0) for i in range(2)]
    first[3 * total :, :] = jnp.where(even, kind[0], kind[1]).astype(bf16)
    second[3 * total :, :] = jnp.where(even, kind[1], kind[0]).astype(bf16)


def edges(field, source, kinds):
    total, _, nz = field.shape
    cx = kinds.shape[0]
    message = pltpu.VMEM((3 * total + 16, nz), bf16)
    anywhere = pl.BlockSpec(memory_space=pl.ANY)
    return pl.pallas_call(
        edge_body,
        out_shape=(message, message),
        in_specs=[anywhere] * 3,
        scratch_shapes=[
            pltpu.VMEM((2, 3, total, nz), f32),
            pltpu.VMEM((2, cx, nz), jnp.int32),
            pltpu.SemaphoreType.DMA((2, 3)),
            pltpu.SemaphoreType.DMA((2,)),
        ],
        compiler_params=params(6),
        name="edges",
    )(*left(field, source, kinds))


def first_body(
    mat_real, mat_loss, field, source, kinds, got_first, got_second,
    sweep, columns, column_a, to_first, to_second, near, *, cx, cy
):
    total = field.shape[0] // cy
    channels = total // cx
    excite = channels // 2
    even_y = is_even("shard")
    a, b = coefficients(kinds[...], mat_real, mat_loss, 0)
    row = lax.broadcasted_iota(jnp.int32, (8, field.shape[1]), 0) & (cx - 1)
    one = got_first[...].astype(f32)
    two = got_second[...].astype(f32)
    for side, own_y in ((0, 0), (1, cy - 1)):
        halo = jnp.where(even_y, two, one) if side == 0 else jnp.where(even_y, one, two)
        kind = halo[3 * total : 3 * total + 8].astype(jnp.int32)
        col_a, col_b = coefficients(kind, mat_real, mat_loss, 1)
        column_a[side] = col_a
        near[side] = halo[total : 2 * total]
        for j in range(0, total // 2, 8):
            v, sums = [], []
            for part in range(2):
                at = part * (total // 2) + j
                beside = halo[total + at : total + at + 8]
                nbr = halo[at : at + 8] + halo[2 * total + at : 2 * total + at + 8] + along_z(beside)
                nbr = nbr + field[pl.ds(at * cy + own_y, 8, stride=cy), :]
                nbr = nbr + jnp.where(row == 0, 0.0, pltpu.roll(beside, 1, 0))
                nbr = nbr + jnp.where(row == cx - 1, 0.0, pltpu.roll(beside, 7, 0))
                v.append(beside)
                sums.append(nbr)
            new = relaxed(v, sums, col_a, col_b)
            for part in range(2):
                at = part * (total // 2) + j
                columns[side, at : at + 8] = new[part]
    for e in range(excite):
        v = [
            [field[at * cy : (at + 1) * cy, :] for at in range((p * excite + e) * cx, (p * excite + e + 1) * cx)]
            for p in range(2)
        ]
        for x in range(cx):
            sums = []
            for p in range(2):
                at = (p * excite + e) * cx + x
                n = source[at * cy : (at + 1) * cy, :] + along_z(v[p][x])
                n = n + along_y(v[p][x], near[0, at : at + 1, :], near[1, at : at + 1, :])
                if x > 0:
                    n = n + v[p][x - 1]
                if x < cx - 1:
                    n = n + v[p][x + 1]
                sums.append(n)
            new = relaxed((v[0][x], v[1][x]), sums, a[x * cy : (x + 1) * cy], b[x * cy : (x + 1) * cy])
            for p in range(2):
                at = (p * excite + e) * cx + x
                sweep[at * cy : (at + 1) * cy, :] = new[p]
    even_x = is_even("space")
    plane = channels * cy
    for message, x in ((to_first, jnp.where(even_x, cx - 1, 0)), (to_second, jnp.where(even_x, 0, cx - 1))):
        for c in range(channels):
            rows = pl.ds(pl.multiple_of((c * cx + x) * cy, cy), cy)
            message[c * cy : (c + 1) * cy, :] = field[rows, :].astype(bf16)
            message[plane + c * cy : plane + (c + 1) * cy, :] = sweep[rows, :].astype(bf16)
        for side in range(2):
            corner = jnp.concatenate(
                [near.at[side][pl.ds(c * cx + x, 8, stride=cx), :] for c in range(0, channels, 8)], axis=0
            )
            at = 2 * plane + side * channels
            message[at : at + channels, :] = corner.astype(bf16)
        at = 2 * plane + 2 * channels
        kind = kinds[pl.ds(pl.multiple_of(x * cy, cy), cy), :].astype(f32) + 1.0
        message[at : at + cy, :] = kind.astype(bf16)


def first_sweep(mat_real, mat_loss, field, source, kinds, got_first, got_second, cx, cy):
    total, nz = field.shape[0] // cy, field.shape[1]
    channels = total // cx
    smem = pl.BlockSpec(memory_space=pltpu.SMEM)
    vmem = pl.BlockSpec(memory_space=pltpu.VMEM)
    message = pltpu.VMEM((2 * channels * cy + 2 * channels + cy, nz), bf16)
    return pl.pallas_call(
        lambda *refs: first_body(*refs, cx=cx, cy=cy),
        out_shape=(
            pltpu.VMEM(field.shape, f32),
            pltpu.VMEM((2, total, nz), f32),
            pltpu.VMEM((2, 8, nz), f32),
            message,
            message,
        ),
        in_specs=[smem, smem] + [vmem] * 5,
        out_specs=(vmem,) * 5,
        scratch_shapes=[pltpu.VMEM((2, total, nz), f32)],
        compiler_params=params(8), name="first_sweep",
    )(mat_real, mat_loss, *held(field, source, kinds, got_first, got_second))


def shards(
    volume_field,
    source,
    material,
    mat_real,
    mat_loss,
    surface_map,
    near_boxes,
    near_blocks,
    radiate,
    interp,
    phase_angle,
    far_parents,
    far_kind,
    translate,
):
    every = ("space", "shard")
    groups = lax.axis_size("space")
    slices = lax.axis_size("shard")
    excite, cells_x, cells_y, cells_z = volume_field.shape[1:]
    cosine, sine, chosen, depth = prepare(phase_angle, surface_map, cells_x, cells_y, cells_z)
    weights = radiate.reshape(2 * radiate.shape[1], radiate.shape[2])
    field = volume_field.reshape(-1, cells_z)
    flat_source = source.reshape(-1, cells_z)
    kinds = material.reshape(-1, cells_z)
    bricks = (-1, cells_y, cells_z)
    got_y = swap(*edges(volume_field.reshape(bricks), source.reshape(bricks), material), "shard")
    sweep, columns, column_a, *to_x = first_sweep(
        mat_real, mat_loss, field, flat_source, kinds, *got_y, cells_x, cells_y
    )
    got_x = swap(*to_x, "space")
    current, currents, pieces = up(
        (mat_real, mat_loss, field, sweep, columns, column_a, flat_source, kinds, *got_x),
        chosen,
        depth,
        near_boxes.shape[0],
        weights,
        interp,
        cosine,
        sine,
        cells_x,
        cells_y,
        groups,
        slices,
    )
    directed = lax.all_to_all(pieces, every, split_axis=0, concat_axis=0, tiled=True)
    first, second = swap(currents, currents, "shard")
    directed, first, second = lax.optimization_barrier((directed, first, second))
    combined = far_combine(far_parents.T, far_kind.T, directed, translate)
    incoming = lax.all_to_all(combined, every, split_axis=0, concat_axis=0, tiled=True)
    near, cosine, sine = near_force(near_boxes.T, currents, first, second, near_blocks, phase_angle)
    forcing = down(incoming, near, weights, interp, cosine, sine, groups, slices)
    return (current.reshape(volume_field.shape), forcing)


def solution(mesh):
    return jax.shard_map(
        shards,
        mesh=mesh,
        in_specs=(
            P(None, None, "space", "shard", None),
            P(None, None, "space", "shard", None),
            P("space", "shard", None),
            P(),
            P(),
            P(("space", "shard"), None),
            P(("space", "shard"), None),
            P(),
            P(),
            P(),
            P(),
            P(),
            P(),
            P(None, None, "shard"),
        ),
        out_specs=(P(None, None, "space", "shard", None), P(("space", "shard"), None, None)),
        check_vma=False,
    )
```

```python
import jax
import jax.numpy as jnp
from jax import lax
from jax.experimental import pallas as pl
from jax.experimental.pallas import tpu as pltpu
from jax.sharding import PartitionSpec as P


relaxation = 0.8
f32 = jnp.float32
bf16 = jnp.bfloat16
CHILDREN = 8


def held(*arrays):
    return [pltpu.with_memory_space_constraint(a, pltpu.VMEM) for a in arrays]


def left(*arrays):
    return [pltpu.with_memory_space_constraint(a, pltpu.HBM) for a in arrays]


def params(mib):
    return pltpu.CompilerParams(vmem_limit_bytes=mib << 20)


def dot(a, b):
    return jnp.dot(a, b, preferred_element_type=f32)


def dot_t(a, b):
    return lax.dot_general(a, b, (((1,), (1,)), ((), ())), preferred_element_type=f32)


def half_turn(v):
    half = v.shape[-2] // 2
    rows = lax.broadcasted_iota(jnp.int32, v.shape, v.ndim - 2)
    swapped = pltpu.roll(v, half, v.ndim - 2)
    return jnp.where(rows < half, -swapped, swapped)


def log2(n):
    assert n & (n - 1) == 0
    return n.bit_length() - 1


def prepare(angle, smap, cx, cy, nz):
    boxes, unknowns = smap.shape

    def body(angle, smap, cosine, sine, chosen, depth):
        cosine[...] = jnp.cos(angle[...])
        sine[...] = jnp.sin(angle[...])
        level = lax.broadcasted_iota(jnp.int32, (nz, unknowns), 0)
        for b in range(boxes):
            key = smap[b : b + 1, :]
            key_z = key & (nz - 1)
            key_x = key >> (log2(nz) + log2(cy))
            lanes = slice(b * unknowns, (b + 1) * unknowns)
            for x in range(cx):
                hit = level == jnp.where(key_x == x, key_z, -1)
                chosen[x * nz : (x + 1) * nz, lanes] = jnp.where(hit, 1.0, 0.0).astype(bf16)
            depth[:, lanes] = jnp.broadcast_to((key >> log2(nz)) & (cy - 1), (8, unknowns))

    shape = pltpu.VMEM(angle.shape, f32)
    return pl.pallas_call(
        body,
        out_shape=(
            shape,
            shape,
            pltpu.VMEM((cx * nz, boxes * unknowns), bf16),
            pltpu.VMEM((8, boxes * unknowns), jnp.int32),
        ),
        compiler_params=params(6),
        name="prepare",
    )(*held(angle, smap))


def swap_pairs(n, first):
    pairs = []
    for i in range(first, n - 1, 2):
        pairs += [(i, i + 1), (i + 1, i)]
    return pairs


def swap(for_even, for_odd, axis):
    n = lax.axis_size(axis)
    received = []
    for k, value in enumerate((for_even, for_odd)):
        received.append(lax.ppermute(value, axis, swap_pairs(n, k)))
    return received


def second_sweep(mat_real, mat_loss, field, sweep, columns, column_a, source, kinds, got_first, got_second, out, beside, store, cx, cy):
    total = field.shape[0] // cy
    channels = total // cx
    excite = channels // 2
    plane = channels * cy
    even = is_even("space")
    a, b = coefficients(kinds[...], mat_real, mat_loss, 0)

    def halo(side, start, size):
        one = got_first[start : start + size, :].astype(f32)
        two = got_second[start : start + size, :].astype(f32)
        return jnp.where(even, two, one) if side == 0 else jnp.where(even, one, two)

    faces = (0, cx - 1)
    for y_side in range(2):
        beside[y_side] = columns[y_side]
        for x_side, x in enumerate(faces):
            corner = halo(x_side, 2 * plane + y_side * channels, channels)
            factor = column_a[y_side, x : x + 1, :]
            for c in range(0, channels, 8):
                rows = pl.ds(c * cx + x, 8, stride=cx)
                beside.at[y_side][rows, :] = beside.at[y_side][rows, :] + factor * corner[c : c + 8]
    face_a = []
    for x_side in range(2):
        kind = halo(x_side, 2 * plane + 2 * channels, cy).astype(jnp.int32)
        face_a.append(coefficients(kind, mat_real, mat_loss, 1)[0])
    for e in range(excite):
        v = []
        for p in range(2):
            c = p * excite + e
            own = [sweep[(c * cx + x) * cy : (c * cx + x + 1) * cy, :] for x in range(cx)]
            outer = []
            for x_side, x in enumerate(faces):
                own[x] = own[x] + a[x * cy : (x + 1) * cy] * halo(x_side, c * cy, cy)
                before = field[(c * cx + x) * cy : (c * cx + x + 1) * cy, :]
                outer.append(halo(x_side, plane + c * cy, cy) + face_a[x_side] * before)
            v.append([outer[0]] + own + [outer[1]])
        for x in range(cx):
            sums = []
            for p in range(2):
                at = (p * excite + e) * cx + x
                w = v[p][x + 1]
                n = source[at * cy : (at + 1) * cy, :] + along_z(w)
                n = n + along_y(w, beside[0, at : at + 1, :], beside[1, at : at + 1, :])
                sums.append(n + v[p][x] + v[p][x + 2])
            new = relaxed((v[0][x + 1], v[1][x + 1]), sums, a[x * cy : (x + 1) * cy], b[x * cy : (x + 1) * cy])
            for p in range(2):
                at = (p * excite + e) * cx + x
                out[at * cy : (at + 1) * cy, :] = new[p]
                store(p, e, x, new[p])


def up_body(
    mat_real, mat_loss, field, sweep, columns, column_a, source, kinds, got_first, got_second,
    chosen, depth, radiate, interp, cosine, sine, volume, cur, out, beside, cells, rows, fresh, sem,
    *, cx, cy, groups, slices
):
    channels = field.shape[0] // (cx * cy)
    excite = channels // 2
    group = excite // groups
    boxes = cur.shape[0]
    unknowns = depth.shape[1] // boxes

    def store(t, e, x, value):
        place = (e // group) * 2 * group + t * group + e % group
        for y in range(0, cy, 8):
            cells.at[x][pl.ds(y * channels + place, 8, stride=channels), :] = value[y : y + 8]

    second_sweep(
        mat_real, mat_loss, field, sweep, columns, column_a, source, kinds, got_first, got_second,
        fresh, beside, store, cx, cy
    )
    leaving = pltpu.make_async_copy(fresh, volume, sem)
    leaving.start()
    lhs = jnp.concatenate([cells[x].astype(bf16) for x in range(cx)], axis=1)
    pair = 2
    for b in range(0, boxes, pair):
        lanes = slice(b * unknowns, (b + pair) * unknowns)
        picked = dot(lhs, chosen[:, lanes])
        key_y = jnp.concatenate([depth[:, lanes]] * (channels // 8), axis=0)
        found = jnp.zeros((channels, pair * unknowns), f32)
        for y in range(cy):
            found = jnp.where(key_y == y, picked[y * channels : (y + 1) * channels], found)
        for j in range(pair):
            own = found[:, j * unknowns : (j + 1) * unknowns].reshape(groups, 2 * group, unknowns)
            turned = half_turn(own)
            both = jnp.concatenate([own, turned], axis=2).reshape(channels, 2 * unknowns)
            rows[(b + j) * channels : (b + j + 1) * channels, :] = both.astype(bf16)
            parts = [
                jnp.concatenate([own[s, t * group : (t + 1) * group] for s in range(groups)], axis=0)
                for t in range(2)
            ]
            cur[b + j] = jnp.concatenate(parts, axis=1).astype(bf16)
    leaf = dot(rows[...], radiate[...]).astype(bf16)
    directions = interp.shape[1]
    width = directions // slices
    tile = max(width, 256)
    parents = boxes // CHILDREN
    for n in range(0, directions, tile):
        spread = dot(leaf, interp[:, n : n + tile]).reshape(parents, CHILDREN, groups, 2 * group, tile)
        along = jnp.zeros((parents, groups, 2 * group, tile), f32)
        across = jnp.zeros((parents, groups, 2 * group, tile), f32)
        for child in range(CHILDREN):
            along = along + cosine[child : child + 1, n : n + tile] * spread[:, child]
            across = across + sine[child : child + 1, n : n + tile] * spread[:, child]
        whole = (along + half_turn(across)).astype(bf16)
        for s in range(groups):
            piece = jnp.concatenate([whole[p, s] for p in range(parents)], axis=0)
            for k in range(tile // width):
                out[s * slices + n // width + k] = piece[:, k * width : (k + 1) * width]
    leaving.wait()


def up(volume_args, chosen, depth, boxes, radiate, interp, cosine, sine, cx, cy, groups, slices):
    field = volume_args[2]
    nz = field.shape[1]
    total = field.shape[0] // cy
    channels = total // cx
    unknowns = depth.shape[1] // boxes
    width = interp.shape[1] // slices
    piece_rows = boxes // CHILDREN * (channels // groups)
    smem = pl.BlockSpec(memory_space=pltpu.SMEM)
    vmem = pl.BlockSpec(memory_space=pltpu.VMEM)
    return pl.pallas_call(
        lambda *refs: up_body(*refs, cx=cx, cy=cy, groups=groups, slices=slices),
        out_shape=(
            pltpu.HBM(field.shape, f32),
            pltpu.VMEM((boxes, channels // 2, 2 * unknowns), bf16),
            pltpu.VMEM((groups * slices, piece_rows, width), bf16),
        ),
        in_specs=[smem, smem] + [vmem] * 14,
        out_specs=(pl.BlockSpec(memory_space=pltpu.HBM), vmem, vmem),
        scratch_shapes=[
            pltpu.VMEM((2, total, nz), f32),
            pltpu.VMEM((cx, cy * channels, nz), f32),
            pltpu.VMEM((boxes * channels, 2 * unknowns), bf16),
            pltpu.VMEM(field.shape, f32),
            pltpu.SemaphoreType.DMA(()),
        ],
        compiler_params=params(16), name="up",
    )(*volume_args[:2], *held(*volume_args[2:], chosen, depth, radiate, interp, cosine, sine))


def far_body(lists, kinds, sources, translate, out, plain):
    far, targets = lists.shape
    devices, piece_rows, width = sources.shape
    per = targets // devices
    tile = piece_rows // per
    plain[...] = sources[...].astype(f32).reshape(targets, tile, width)

    def one(d, _):
        results = []
        for j in range(per):
            t = d * per + j
            along = jnp.zeros((tile, width), f32)
            across = jnp.zeros((tile, width), f32)
            for f in range(far):
                source = plain[lists[f, t]]
                factor = translate[kinds[f, t]]
                along = along + factor[0:1] * source
                across = across + factor[1:2] * source
            results.append(along + half_turn(across))
        out[d] = jnp.concatenate(results, axis=0).astype(bf16)
        return 0

    lax.fori_loop(0, devices, one, 0, unroll=4)


def far_combine(lists, kinds, sources, translate):
    targets = lists.shape[1]
    devices, piece_rows, width = sources.shape
    tile = piece_rows // (targets // devices)
    smem = pl.BlockSpec(memory_space=pltpu.SMEM)
    vmem = pl.BlockSpec(memory_space=pltpu.VMEM)
    return pl.pallas_call(
        far_body,
        out_shape=pltpu.VMEM(sources.shape, bf16),
        in_specs=[smem, smem, vmem, vmem],
        out_specs=vmem,
        scratch_shapes=[pltpu.VMEM((targets, tile, width), f32)],
        compiler_params=params(8),
        name="far",
    )(lists, kinds, *held(sources, translate))


def near_body(lists, own, first, second, blocks, angle, out, cosine, sine, boxes_all, rows):
    cosine[...] = jnp.cos(angle[...])
    sine[...] = jnp.sin(angle[...])
    boxes, excite, k = own.shape
    slots = lists.shape[0]
    shard = lax.axis_index("shard")
    base = (lax.axis_index("space") * lax.axis_size("shard") + shard) * boxes
    even = lax.rem(shard, 2) == 0
    above = jnp.where(even, 0, boxes)
    below = jnp.where(even, 3 * boxes, 2 * boxes)
    boxes_all[0:boxes] = own[...]
    boxes_all[boxes : 2 * boxes] = first[...]
    boxes_all[2 * boxes : 3 * boxes] = second[...]
    for b in range(boxes):
        for s in range(slots):
            away = lists[s, b] - base
            spot = away + jnp.where(away < 0, below, jnp.where(away < boxes, 0, above))
            rows[b * excite : (b + 1) * excite, s * k : (s + 1) * k] = boxes_all[spot]
    out[...] = dot(rows[...], blocks[...]).reshape(out.shape)


def near_force(lists, own, first, second, blocks, angle):
    boxes, excite, k = own.shape
    slots = lists.shape[0]
    smem = pl.BlockSpec(memory_space=pltpu.SMEM)
    vmem = pl.BlockSpec(memory_space=pltpu.VMEM)
    return pl.pallas_call(
        near_body,
        out_shape=(pltpu.VMEM((boxes, excite, k), f32),) + (pltpu.VMEM(angle.shape, f32),) * 2,
        in_specs=[smem] + [vmem] * 5,
        out_specs=(vmem,) * 3,
        scratch_shapes=[
            pltpu.VMEM((3 * boxes, excite, k), bf16),
            pltpu.VMEM((boxes * excite, slots * k), bf16),
        ],
        compiler_params=params(6), name="near",
    )(lists, *held(own, first, second, blocks.reshape(slots * k, k), angle))


def down_body(pieces, near, radiate, interp, cosine, sine, out, shifted, *, groups, slices):
    _, _, width = pieces.shape
    boxes, excite, both = out.shape
    unknowns = both // 2
    group = excite // groups
    tile = 2 * group
    parents = boxes // CHILDREN
    for h in range(slices):
        lanes = slice(h * width, (h + 1) * width)
        for s in range(groups):
            incoming = pieces[s * slices + h].astype(f32).reshape(parents, tile, width)
            turned = half_turn(incoming)
            for p in range(parents):
                for child in range(0, CHILDREN):
                    row = ((p * CHILDREN + child) * groups + s) * tile
                    value = cosine[child : child + 1, lanes] * incoming[p] - sine[child : child + 1, lanes] * turned[p]
                    shifted[row : row + tile, lanes] = value
    leaf_in = dot_t(shifted[...].astype(bf16), interp[...]).astype(bf16)
    back = dot_t(leaf_in, radiate[...]).reshape(boxes, groups, tile, both)
    own = back[..., :unknowns] - half_turn(back[..., unknowns:])
    for b in range(boxes):
        parts = [
            jnp.concatenate([own[b, s, t * group : (t + 1) * group] for s in range(groups)], axis=0)
            for t in range(2)
        ]
        out[b] = jnp.concatenate(parts, axis=1) + near[b]


def down(pieces, near, radiate, interp, cosine, sine, groups, slices):
    boxes, excite, _ = near.shape
    return pl.pallas_call(
        lambda *refs: down_body(*refs, groups=groups, slices=slices),
        out_shape=jax.ShapeDtypeStruct(near.shape, f32),
        scratch_shapes=[pltpu.VMEM((boxes * excite * 2, interp.shape[1]), f32)],
        compiler_params=params(16), name="down",
    )(*held(pieces, near, radiate, interp, cosine, sine))


def is_even(axis):
    return lax.rem(lax.axis_index(axis), 2) == 0


def coefficients(kinds, mat_real, mat_loss, base):
    diagonal = jnp.full(kinds.shape, 6.0, f32)
    loss = jnp.zeros(kinds.shape, f32)
    for k in range(mat_real.shape[0]):
        present = kinds == k + base
        diagonal = jnp.where(present, 6.0 + mat_real[k], diagonal)
        loss = jnp.where(present, mat_loss[k], loss)
    a = relaxation / diagonal
    if base > 0:
        a = jnp.where(kinds < base, 0.0, a)
    return a, a * loss


def along_z(v):
    lanes = v.shape[-1]
    lane = lax.broadcasted_iota(jnp.int32, v.shape, v.ndim - 1)
    lower = jnp.where(lane == 0, 0.0, pltpu.roll(v, 1, v.ndim - 1))
    upper = jnp.where(lane == lanes - 1, 0.0, pltpu.roll(v, lanes - 1, v.ndim - 1))
    return lower + upper


def along_y(v, low, high):
    rows = v.shape[0]
    row = lax.broadcasted_iota(jnp.int32, v.shape, 0)
    lower = jnp.where(row == 0, low, pltpu.roll(v, 1, 0))
    upper = jnp.where(row == rows - 1, high, pltpu.roll(v, rows - 1, 0))
    return lower + upper


def relaxed(v, total, a, b):
    keep = 1.0 - relaxation
    return (
        keep * v[0] + a * total[0] + b * v[1],
        keep * v[1] + a * total[1] - b * v[0],
    )


def edge_body(field, source, kinds, first, second, layers, kind_rows, sem, kind_sem):
    total, cy, _ = field.shape
    cx = kinds.shape[0]
    even = is_even("shard")
    faces = ((cy - 2, cy - 1), (1, 0))
    copies = []
    for i, (inner, outer) in enumerate(faces):
        for k, (ref, y) in enumerate(((field, inner), (field, outer), (source, outer))):
            copies.append(pltpu.make_async_copy(ref.at[:, y], layers.at[i, k], sem.at[i, k]))
        copies.append(pltpu.make_async_copy(kinds.at[:, outer], kind_rows.at[i], kind_sem.at[i]))
    for copy in copies:
        copy.start()
    for copy in copies:
        copy.wait()
    for k in range(3):
        rows = slice(k * total, (k + 1) * total)
        first[rows, :] = jnp.where(even, layers[0, k], layers[1, k]).astype(bf16)
        second[rows, :] = jnp.where(even, layers[1, k], layers[0, k]).astype(bf16)
    kind = [jnp.concatenate([kind_rows[i].astype(f32) + 1.0] * (16 // cx), axis=0) for i in range(2)]
    first[3 * total :, :] = jnp.where(even, kind[0], kind[1]).astype(bf16)
    second[3 * total :, :] = jnp.where(even, kind[1], kind[0]).astype(bf16)


def edges(field, source, kinds):
    total, _, nz = field.shape
    cx = kinds.shape[0]
    message = pltpu.VMEM((3 * total + 16, nz), bf16)
    anywhere = pl.BlockSpec(memory_space=pl.ANY)
    return pl.pallas_call(
        edge_body,
        out_shape=(message, message),
        in_specs=[anywhere] * 3,
        scratch_shapes=[
            pltpu.VMEM((2, 3, total, nz), f32),
            pltpu.VMEM((2, cx, nz), jnp.int32),
            pltpu.SemaphoreType.DMA((2, 3)),
            pltpu.SemaphoreType.DMA((2,)),
        ],
        compiler_params=params(6),
        name="edges",
    )(*left(field, source, kinds))


def first_body(
    mat_real, mat_loss, field, source, kinds, got_first, got_second,
    sweep, columns, column_a, to_first, to_second, near, *, cx, cy
):
    total = field.shape[0] // cy
    channels = total // cx
    excite = channels // 2
    even_y = is_even("shard")
    a, b = coefficients(kinds[...], mat_real, mat_loss, 0)
    row = lax.broadcasted_iota(jnp.int32, (8, field.shape[1]), 0) & (cx - 1)
    one = got_first[...].astype(f32)
    two = got_second[...].astype(f32)
    for side, own_y in ((0, 0), (1, cy - 1)):
        halo = jnp.where(even_y, two, one) if side == 0 else jnp.where(even_y, one, two)
        kind = halo[3 * total : 3 * total + 8].astype(jnp.int32)
        col_a, col_b = coefficients(kind, mat_real, mat_loss, 1)
        column_a[side] = col_a
        near[side] = halo[total : 2 * total]
        for j in range(0, total // 2, 8):
            v, sums = [], []
            for part in range(2):
                at = part * (total // 2) + j
                beside = halo[total + at : total + at + 8]
                nbr = halo[at : at + 8] + halo[2 * total + at : 2 * total + at + 8] + along_z(beside)
                nbr = nbr + field[pl.ds(at * cy + own_y, 8, stride=cy), :]
                nbr = nbr + jnp.where(row == 0, 0.0, pltpu.roll(beside, 1, 0))
                nbr = nbr + jnp.where(row == cx - 1, 0.0, pltpu.roll(beside, 7, 0))
                v.append(beside)
                sums.append(nbr)
            new = relaxed(v, sums, col_a, col_b)
            for part in range(2):
                at = part * (total // 2) + j
                columns[side, at : at + 8] = new[part]
    for e in range(excite):
        v = [
            [field[at * cy : (at + 1) * cy, :] for at in range((p * excite + e) * cx, (p * excite + e + 1) * cx)]
            for p in range(2)
        ]
        for x in range(cx):
            sums = []
            for p in range(2):
                at = (p * excite + e) * cx + x
                n = source[at * cy : (at + 1) * cy, :] + along_z(v[p][x])
                n = n + along_y(v[p][x], near[0, at : at + 1, :], near[1, at : at + 1, :])
                if x > 0:
                    n = n + v[p][x - 1]
                if x < cx - 1:
                    n = n + v[p][x + 1]
                sums.append(n)
            new = relaxed((v[0][x], v[1][x]), sums, a[x * cy : (x + 1) * cy], b[x * cy : (x + 1) * cy])
            for p in range(2):
                at = (p * excite + e) * cx + x
                sweep[at * cy : (at + 1) * cy, :] = new[p]
    even_x = is_even("space")
    plane = channels * cy
    for message, x in ((to_first, jnp.where(even_x, cx - 1, 0)), (to_second, jnp.where(even_x, 0, cx - 1))):
        for c in range(channels):
            rows = pl.ds(pl.multiple_of((c * cx + x) * cy, cy), cy)
            message[c * cy : (c + 1) * cy, :] = field[rows, :].astype(bf16)
            message[plane + c * cy : plane + (c + 1) * cy, :] = sweep[rows, :].astype(bf16)
        for side in range(2):
            corner = jnp.concatenate(
                [near.at[side][pl.ds(c * cx + x, 8, stride=cx), :] for c in range(0, channels, 8)], axis=0
            )
            at = 2 * plane + side * channels
            message[at : at + channels, :] = corner.astype(bf16)
        at = 2 * plane + 2 * channels
        kind = kinds[pl.ds(pl.multiple_of(x * cy, cy), cy), :].astype(f32) + 1.0
        message[at : at + cy, :] = kind.astype(bf16)


def first_sweep(mat_real, mat_loss, field, source, kinds, got_first, got_second, cx, cy):
    total, nz = field.shape[0] // cy, field.shape[1]
    channels = total // cx
    smem = pl.BlockSpec(memory_space=pltpu.SMEM)
    vmem = pl.BlockSpec(memory_space=pltpu.VMEM)
    message = pltpu.VMEM((2 * channels * cy + 2 * channels + cy, nz), bf16)
    return pl.pallas_call(
        lambda *refs: first_body(*refs, cx=cx, cy=cy),
        out_shape=(
            pltpu.VMEM(field.shape, f32),
            pltpu.VMEM((2, total, nz), f32),
            pltpu.VMEM((2, 8, nz), f32),
            message,
            message,
        ),
        in_specs=[smem, smem] + [vmem] * 5,
        out_specs=(vmem,) * 5,
        scratch_shapes=[pltpu.VMEM((2, total, nz), f32)],
        compiler_params=params(8), name="first_sweep",
    )(mat_real, mat_loss, *held(field, source, kinds, got_first, got_second))


def steps(
    volume_field,
    source,
    material,
    mat_real,
    mat_loss,
    surface_map,
    near_boxes,
    near_blocks,
    radiate,
    interp,
    phase_angle,
    far_parents,
    far_kind,
    translate,
):
    every = ("space", "shard")
    groups = lax.axis_size("space")
    slices = lax.axis_size("shard")
    _, cells_x, cells_y, cells_z = volume_field.shape[1:]
    cosine, sine, chosen, depth = prepare(phase_angle, surface_map, cells_x, cells_y, cells_z)
    weights = radiate.reshape(2 * radiate.shape[1], radiate.shape[2])
    field = volume_field.reshape(-1, cells_z)
    flat_source = source.reshape(-1, cells_z)
    kinds = material.reshape(-1, cells_z)
    bricks = (-1, cells_y, cells_z)
    got_y = swap(*edges(volume_field.reshape(bricks), source.reshape(bricks), material), "shard")
    sweep, columns, column_a, *to_x = first_sweep(
        mat_real, mat_loss, field, flat_source, kinds, *got_y, cells_x, cells_y
    )
    got_x = swap(*to_x, "space")
    current, currents, pieces = up(
        (mat_real, mat_loss, field, sweep, columns, column_a, flat_source, kinds, *got_x),
        chosen,
        depth,
        near_boxes.shape[0],
        weights,
        interp,
        cosine,
        sine,
        cells_x,
        cells_y,
        groups,
        slices,
    )
    directed = lax.all_to_all(pieces, every, split_axis=0, concat_axis=0, tiled=True)
    first, second = swap(currents, currents, "shard")
    combined = far_combine(far_parents.T, far_kind.T, directed, translate)
    incoming = lax.all_to_all(combined, every, split_axis=0, concat_axis=0, tiled=True)
    near, cosine, sine = near_force(near_boxes.T, currents, first, second, near_blocks, phase_angle)
    forcing = down(incoming, near, weights, interp, cosine, sine, groups, slices)
    return (current.reshape(volume_field.shape), forcing)


def solution(mesh):
    return jax.shard_map(
        steps,
        mesh=mesh,
        in_specs=(
            P(None, None, "space", "shard", None),
            P(None, None, "space", "shard", None),
            P("space", "shard", None),
            P(),
            P(),
            P(("space", "shard"), None),
            P(("space", "shard"), None),
            P(),
            P(),
            P(),
            P(),
            P(),
            P(),
            P(None, None, "shard"),
        ),
        out_specs=(P(None, None, "space", "shard", None), P(("space", "shard"), None, None)),
        check_vma=False,
    )
```

```python
import jax
import jax.numpy as jnp
from jax import lax
from jax.experimental import pallas as pl
from jax.experimental.pallas import tpu as pltpu
from jax.sharding import PartitionSpec as P


relaxation = 0.8
f32 = jnp.float32
bf16 = jnp.bfloat16
CHILDREN = 8


def held(*arrays):
    return [pltpu.with_memory_space_constraint(a, pltpu.VMEM) for a in arrays]


def left(*arrays):
    return [pltpu.with_memory_space_constraint(a, pltpu.HBM) for a in arrays]


def params(mib):
    return pltpu.CompilerParams(vmem_limit_bytes=mib << 20)


def dot(a, b):
    return jnp.dot(a, b, preferred_element_type=f32)


def dot_t(a, b):
    return lax.dot_general(a, b, (((1,), (1,)), ((), ())), preferred_element_type=f32)


def half_turn(v):
    half = v.shape[-2] // 2
    rows = lax.broadcasted_iota(jnp.int32, v.shape, v.ndim - 2)
    swapped = pltpu.roll(v, half, v.ndim - 2)
    return jnp.where(rows < half, -swapped, swapped)


def log2(n):
    assert n & (n - 1) == 0
    return n.bit_length() - 1


def prepare(angle, smap, cx, cy, nz):
    boxes, unknowns = smap.shape

    def body(angle, smap, cosine, sine, chosen, depth):
        cosine[...] = jnp.cos(angle[...])
        sine[...] = jnp.sin(angle[...])
        level = lax.broadcasted_iota(jnp.int32, (nz, unknowns), 0)
        for b in range(boxes):
            key = smap[b : b + 1, :]
            key_z = key & (nz - 1)
            key_x = key >> (log2(nz) + log2(cy))
            lanes = slice(b * unknowns, (b + 1) * unknowns)
            for x in range(cx):
                hit = level == jnp.where(key_x == x, key_z, -1)
                chosen[x * nz : (x + 1) * nz, lanes] = jnp.where(hit, 1.0, 0.0).astype(bf16)
            depth[:, lanes] = jnp.broadcast_to((key >> log2(nz)) & (cy - 1), (8, unknowns))

    shape = pltpu.VMEM(angle.shape, f32)
    return pl.pallas_call(
        body,
        out_shape=(
            shape,
            shape,
            pltpu.VMEM((cx * nz, boxes * unknowns), bf16),
            pltpu.VMEM((8, boxes * unknowns), jnp.int32),
        ),
        compiler_params=params(6),
        name="prepare",
    )(*held(angle, smap))


def swap_pairs(n, first):
    pairs = []
    for i in range(first, n - 1, 2):
        pairs += [(i, i + 1), (i + 1, i)]
    return pairs


def swap(for_even, for_odd, axis):
    n = lax.axis_size(axis)
    received = []
    for k, value in enumerate((for_even, for_odd)):
        received.append(lax.ppermute(value, axis, swap_pairs(n, k)))
    return received


def second_sweep(
    mat_real, mat_loss, field, sweep, columns, column_a, source, kinds, early_first, early_second,
    late_first, late_second, out, beside, a_all, b_all, store, cx, cy
):
    total = field.shape[0] // cy
    channels = total // cx
    excite = channels // 2
    plane = channels * cy
    a_all[...], b_all[...] = coefficients(kinds[...], mat_real, mat_loss, 0)
    ends = (0, cx - 1)

    def run(*got):
        for y_side in range(2):
            beside[y_side] = columns[y_side]
            for x_side, x in enumerate(ends):
                at = plane + y_side * channels
                corner = got[x_side][1][at : at + channels, :].astype(f32)
                factor = column_a[y_side, x : x + 1, :]
                for c in range(0, channels, 8):
                    rows = pl.ds(c * cx + x, 8, stride=cx)
                    beside.at[y_side][rows, :] = beside.at[y_side][rows, :] + factor * corner[c : c + 8]
        face_a = [
            coefficients(got[side][0][plane:, :].astype(f32).astype(jnp.int32), mat_real, mat_loss, 1)[0]
            for side in range(2)
        ]

        def one(e, _):
            values = []
            for p in range(2):
                c = p * excite + e
                own = [tiles_at(sweep, (c * cx + x) * cy, cy) for x in range(cx)]
                outer = []
                for side, x in enumerate(ends):
                    raw = wide_tiles_at(got[side][0], c * cy, cy)
                    own[x] = [
                        t + a_all[x * cy + i * 8 : x * cy + i * 8 + 8, :] * h
                        for i, (t, h) in enumerate(zip(own[x], raw))
                    ]
                    part = wide_tiles_at(got[side][1], c * cy, cy)
                    before = tiles_at(field, (c * cx + x) * cy, cy)
                    outer.append(
                        [q + face_a[side][i * 8 : i * 8 + 8] * t for i, (q, t) in enumerate(zip(part, before))]
                    )
                values.append([outer[0]] + own + [outer[1]])

            def emit(p, x, i, value):
                at = ((p * excite + e) * cx + x) * cy + i
                out[pl.ds(pl.multiple_of(at, 8), 8), :] = value
                store(p, e, x, i, value)

            sweep_brick(values, e, excite, cx, cy, source, beside, a_all, b_all, emit)
            return 0

        lax.fori_loop(0, excite, one, 0)

    by_parity("space", run, (early_first, late_first), (early_second, late_second))


def up_body(
    mat_real, mat_loss, field, sweep, columns, column_a, source, kinds, early_first, early_second,
    late_first, late_second, chosen, depth, radiate, interp, cosine, sine, volume, cur, out,
    beside, cells, rows, fresh, a_all, b_all, sem,
    *, cx, cy, groups, slices
):
    channels = field.shape[0] // (cx * cy)
    excite = channels // 2
    group = excite // groups
    boxes = cur.shape[0]
    unknowns = depth.shape[1] // boxes

    def store(t, e, x, y, value):
        place = (e // group) * 2 * group + t * group + e % group
        cells.at[x][pl.ds(y * channels + place, 8, stride=channels), :] = value

    second_sweep(
        mat_real, mat_loss, field, sweep, columns, column_a, source, kinds, early_first, early_second,
        late_first, late_second, fresh, beside, a_all, b_all, store, cx, cy
    )
    leaving = pltpu.make_async_copy(fresh, volume, sem)
    leaving.start()
    lhs = jnp.concatenate([cells[x].astype(bf16) for x in range(cx)], axis=1)
    pair = 2
    for b in range(0, boxes, pair):
        lanes = slice(b * unknowns, (b + pair) * unknowns)
        picked = dot(lhs, chosen[:, lanes])
        key_y = jnp.concatenate([depth[:, lanes]] * (channels // 8), axis=0)
        found = jnp.zeros((channels, pair * unknowns), f32)
        for y in range(cy):
            found = jnp.where(key_y == y, picked[y * channels : (y + 1) * channels], found)
        for j in range(pair):
            own = found[:, j * unknowns : (j + 1) * unknowns].reshape(groups, 2 * group, unknowns)
            turned = half_turn(own)
            both = jnp.concatenate([own, turned], axis=2).reshape(channels, 2 * unknowns)
            rows[(b + j) * channels : (b + j + 1) * channels, :] = both.astype(bf16)
            parts = [
                jnp.concatenate([own[s, t * group : (t + 1) * group] for s in range(groups)], axis=0)
                for t in range(2)
            ]
            cur[b + j] = jnp.concatenate(parts, axis=1).astype(bf16)
    leaf = dot(rows[...], radiate[...]).astype(bf16)
    directions = interp.shape[1]
    width = directions // slices
    tile = max(width, 256)
    parents = boxes // CHILDREN
    for n in range(0, directions, tile):
        spread = dot(leaf, interp[:, n : n + tile]).reshape(parents, CHILDREN, groups, 2 * group, tile)
        along = jnp.zeros((parents, groups, 2 * group, tile), f32)
        across = jnp.zeros((parents, groups, 2 * group, tile), f32)
        for child in range(CHILDREN):
            along = along + cosine[child : child + 1, n : n + tile] * spread[:, child]
            across = across + sine[child : child + 1, n : n + tile] * spread[:, child]
        whole = (along + half_turn(across)).astype(bf16)
        for s in range(groups):
            piece = jnp.concatenate([whole[p, s] for p in range(parents)], axis=0)
            for k in range(tile // width):
                out[s * slices + n // width + k] = piece[:, k * width : (k + 1) * width]
    leaving.wait()


def up(volume_args, chosen, depth, boxes, radiate, interp, cosine, sine, cx, cy, groups, slices):
    field = volume_args[2]
    nz = field.shape[1]
    total = field.shape[0] // cy
    channels = total // cx
    unknowns = depth.shape[1] // boxes
    width = interp.shape[1] // slices
    piece_rows = boxes // CHILDREN * (channels // groups)
    smem = pl.BlockSpec(memory_space=pltpu.SMEM)
    vmem = pl.BlockSpec(memory_space=pltpu.VMEM)
    return pl.pallas_call(
        lambda *refs: up_body(*refs, cx=cx, cy=cy, groups=groups, slices=slices),
        out_shape=(
            pltpu.HBM(field.shape, f32),
            pltpu.VMEM((boxes, channels // 2, 2 * unknowns), bf16),
            pltpu.VMEM((groups * slices, piece_rows, width), bf16),
        ),
        in_specs=[smem, smem] + [vmem] * 16,
        out_specs=(pl.BlockSpec(memory_space=pltpu.HBM), vmem, vmem),
        scratch_shapes=[
            pltpu.VMEM((2, total, nz), f32),
            pltpu.VMEM((cx, cy * channels, nz), f32),
            pltpu.VMEM((boxes * channels, 2 * unknowns), bf16),
            pltpu.VMEM(field.shape, f32),
            pltpu.VMEM((cx * cy, nz), f32),
            pltpu.VMEM((cx * cy, nz), f32),
            pltpu.SemaphoreType.DMA(()),
        ],
        compiler_params=params(16), name="up",
    )(*volume_args[:2], *held(*volume_args[2:], chosen, depth, radiate, interp, cosine, sine))


def tables(lists, kinds, translate):
    far, targets = lists.shape

    def body(lists, kinds, translate, factors, order):
        def one(t, _):
            for f in range(far):
                order[t * far + f] = lists[f, t]
                factors[t * far + f] = translate[kinds[f, t]]
            return 0

        lax.fori_loop(0, targets, one, 0, unroll=2)

    smem = pl.BlockSpec(memory_space=pltpu.SMEM)
    vmem = pl.BlockSpec(memory_space=pltpu.VMEM)
    return pl.pallas_call(
        body,
        out_shape=(
            pltpu.VMEM((targets * far,) + translate.shape[1:], f32),
            jax.ShapeDtypeStruct((targets * far,), jnp.int32),
        ),
        in_specs=[smem, smem, vmem],
        out_specs=(vmem, smem),
        compiler_params=params(8),
        name="tables",
    )(lists, kinds, *held(translate))


def far_body(order, sources, factors, out, plain, *, targets):
    devices, piece_rows, width = sources.shape
    far = order.shape[0] // targets
    per = targets // devices
    tile = piece_rows // per
    plain[...] = sources[...].astype(f32).reshape(targets, tile, width)

    def one(d, _):
        results = []
        for j in range(per):
            along = jnp.zeros((tile, width), f32)
            across = jnp.zeros((tile, width), f32)
            for f in range(far):
                pair = d * (per * far) + (j * far + f)
                source = plain[order[pair]]
                factor = factors[pair]
                along = along + factor[0:1] * source
                across = across + factor[1:2] * source
            results.append(along + half_turn(across))
        out[d] = jnp.concatenate(results, axis=0).astype(bf16)
        return 0

    lax.fori_loop(0, devices, one, 0, unroll=4)


def far_combine(order, sources, factors, targets):
    devices, piece_rows, width = sources.shape
    tile = piece_rows // (targets // devices)
    smem = pl.BlockSpec(memory_space=pltpu.SMEM)
    vmem = pl.BlockSpec(memory_space=pltpu.VMEM)
    return pl.pallas_call(
        lambda *refs: far_body(*refs, targets=targets),
        out_shape=pltpu.VMEM(sources.shape, bf16),
        in_specs=[smem, vmem, vmem],
        out_specs=vmem,
        scratch_shapes=[pltpu.VMEM((targets, tile, width), f32)],
        compiler_params=params(8),
        name="far",
    )(order, *held(sources, factors))


def near_body(lists, own, first, second, blocks, angle, out, cosine, sine, boxes_all, rows):
    cosine[...] = jnp.cos(angle[...])
    sine[...] = jnp.sin(angle[...])
    boxes, excite, k = own.shape
    slots = lists.shape[0]
    shard = lax.axis_index("shard")
    base = (lax.axis_index("space") * lax.axis_size("shard") + shard) * boxes
    even = lax.rem(shard, 2) == 0
    above = jnp.where(even, 0, boxes)
    below = jnp.where(even, 3 * boxes, 2 * boxes)
    boxes_all[0:boxes] = own[...]
    boxes_all[boxes : 2 * boxes] = first[...]
    boxes_all[2 * boxes : 3 * boxes] = second[...]
    for b in range(boxes):
        for s in range(slots):
            away = lists[s, b] - base
            spot = away + jnp.where(away < 0, below, jnp.where(away < boxes, 0, above))
            rows[b * excite : (b + 1) * excite, s * k : (s + 1) * k] = boxes_all[spot]
    out[...] = dot(rows[...], blocks[...]).reshape(out.shape)


def near_force(lists, own, first, second, blocks, angle):
    boxes, excite, k = own.shape
    slots = lists.shape[0]
    smem = pl.BlockSpec(memory_space=pltpu.SMEM)
    vmem = pl.BlockSpec(memory_space=pltpu.VMEM)
    return pl.pallas_call(
        near_body,
        out_shape=(pltpu.VMEM((boxes, excite, k), f32),) + (pltpu.VMEM(angle.shape, f32),) * 2,
        in_specs=[smem] + [vmem] * 5,
        out_specs=(vmem,) * 3,
        scratch_shapes=[
            pltpu.VMEM((3 * boxes, excite, k), bf16),
            pltpu.VMEM((boxes * excite, slots * k), bf16),
        ],
        compiler_params=params(6), name="near",
    )(lists, *held(own, first, second, blocks.reshape(slots * k, k), angle))


def down_body(pieces, near, radiate, interp, cosine, sine, out, shifted, *, groups, slices):
    _, _, width = pieces.shape
    boxes, excite, both = out.shape
    unknowns = both // 2
    group = excite // groups
    tile = 2 * group
    parents = boxes // CHILDREN
    for h in range(slices):
        lanes = slice(h * width, (h + 1) * width)
        for s in range(0, groups, 2):
            pair = [pieces[(s + k) * slices + h].astype(f32) for k in range(2)]
            for p in range(parents):
                incoming = jnp.concatenate([v[p * tile : (p + 1) * tile] for v in pair], axis=0)
                turned = half_turn(incoming.reshape(2, tile, width)).reshape(2 * tile, width)
                for child in range(CHILDREN):
                    row = ((p * CHILDREN + child) * groups + s) * tile
                    value = cosine[child : child + 1, lanes] * incoming - sine[child : child + 1, lanes] * turned
                    shifted[row : row + 2 * tile, lanes] = value.astype(bf16)
    leaf_in = dot_t(shifted[...], interp[...]).astype(bf16)
    back = dot_t(leaf_in, radiate[...]).reshape(boxes, groups, tile, both)
    own = back[..., :unknowns] - half_turn(back[..., unknowns:])
    for b in range(boxes):
        parts = [
            jnp.concatenate([own[b, s, t * group : (t + 1) * group] for s in range(groups)], axis=0)
            for t in range(2)
        ]
        out[b] = jnp.concatenate(parts, axis=1) + near[b]


def down(pieces, near, radiate, interp, cosine, sine, groups, slices):
    boxes, excite, _ = near.shape
    return pl.pallas_call(
        lambda *refs: down_body(*refs, groups=groups, slices=slices),
        out_shape=jax.ShapeDtypeStruct(near.shape, f32),
        scratch_shapes=[pltpu.VMEM((boxes * excite * 2, interp.shape[1]), bf16)],
        compiler_params=params(16), name="down",
    )(*held(pieces, near, radiate, interp, cosine, sine))


def is_even(axis):
    return lax.rem(lax.axis_index(axis), 2) == 0


def coefficients(kinds, mat_real, mat_loss, base):
    diagonal = jnp.full(kinds.shape, 6.0, f32)
    loss = jnp.zeros(kinds.shape, f32)
    for k in range(mat_real.shape[0]):
        present = kinds == k + base
        diagonal = jnp.where(present, 6.0 + mat_real[k], diagonal)
        loss = jnp.where(present, mat_loss[k], loss)
    a = relaxation / diagonal
    if base > 0:
        a = jnp.where(kinds < base, 0.0, a)
    return a, a * loss


def along_z(v):
    lanes = v.shape[-1]
    lane = lax.broadcasted_iota(jnp.int32, v.shape, v.ndim - 1)
    lower = jnp.where(lane == 0, 0.0, pltpu.roll(v, 1, v.ndim - 1))
    upper = jnp.where(lane == lanes - 1, 0.0, pltpu.roll(v, lanes - 1, v.ndim - 1))
    return lower + upper


def along_y(tiles, low, high):
    row = lax.broadcasted_iota(jnp.int32, tiles[0].shape, 0)
    lower = [low] + [pltpu.roll(t, 1, 0) for t in tiles]
    upper = [pltpu.roll(t, 7, 0) for t in tiles] + [high]
    return [
        jnp.where(row == 0, lower[i], lower[i + 1]) + jnp.where(row == 7, upper[i + 1], upper[i])
        for i in range(len(tiles))
    ]


def relaxed(v, total, a, b):
    keep = 1.0 - relaxation
    return (
        keep * v[0] + a * total[0] + b * v[1],
        keep * v[1] + a * total[1] - b * v[0],
    )


def tiles_at(ref, at, rows):
    return [ref[pl.ds(pl.multiple_of(at + i, 8), 8), :] for i in range(0, rows, 8)]


def wide_tiles_at(ref, at, rows):
    wide = ref[pl.ds(pl.multiple_of(at, 16), rows), :].astype(f32)
    return [wide[i : i + 8] for i in range(0, rows, 8)]


def sweep_brick(values, e, excite, cx, cy, source, beside, a, b, emit):
    for x in range(cx):
        sums = []
        for p in range(2):
            at = (p * excite + e) * cx + x
            edge = [jnp.broadcast_to(beside[side, pl.ds(at, 1), :], (8, source.shape[1])) for side in range(2)]
            here = values[p][x + 1]
            total = [n + along_z(t) + y for n, t, y in zip(tiles_at(source, at * cy, cy), here, along_y(here, *edge))]
            for other in (values[p][x], values[p][x + 2]):
                if other is not None:
                    total = [n + t for n, t in zip(total, other)]
            sums.append(total)
        for i in range(cy // 8):
            rows = slice(x * cy + i * 8, x * cy + i * 8 + 8)
            new = relaxed(
                (values[0][x + 1][i], values[1][x + 1][i]), (sums[0][i], sums[1][i]), a[rows, :], b[rows, :]
            )
            for p in range(2):
                emit(p, x, i * 8, new[p])


def by_parity(axis, run, first, second):
    even = is_even(axis)

    @pl.when(even)
    def _():
        run(second, first)

    @pl.when(jnp.logical_not(even))
    def _():
        run(first, second)


def edge_body(
    mat_real, mat_loss, field, source, kinds, first, second, layers, kind_rows, sem, kind_sem
):
    total, cy, nz = field.shape
    cx = kinds.shape[0]
    even = is_even("shard")
    faces = ((cy - 2, cy - 1), (1, 0))
    copies = []
    for i, (inner, outer) in enumerate(faces):
        for k, (ref, y) in enumerate(((field, inner), (field, outer), (source, outer))):
            copies.append(pltpu.make_async_copy(ref.at[:, y], layers.at[i, k], sem.at[i, k]))
        for k in range(2):
            copies.append(
                pltpu.make_async_copy(kinds.at[:, outer], kind_rows.at[i, pl.ds(k * cx, cx)], kind_sem.at[i, k])
            )
    for copy in copies:
        copy.start()
    for copy in copies:
        copy.wait()
    row = lax.broadcasted_iota(jnp.int32, (8, nz), 0) & (cx - 1)
    for i in range(2):
        a, b = coefficients(kind_rows[i], mat_real, mat_loss, 0)
        for j in range(0, total // 2, 8):
            v, sums = [], []
            for part in range(2):
                rows = slice(part * (total // 2) + j, part * (total // 2) + j + 8)
                here = layers[i, 1, rows, :]
                n = layers[i, 0, rows, :] + layers[i, 2, rows, :] + along_z(here)
                n = n + jnp.where(row == 0, 0.0, pltpu.roll(here, 1, 0))
                n = n + jnp.where(row == cx - 1, 0.0, pltpu.roll(here, 7, 0))
                v.append(here)
                sums.append(n)
            new = relaxed(v, sums, a, b)
            for part in range(2):
                layers[i, 2, part * (total // 2) + j : part * (total // 2) + j + 8, :] = new[part]
    for place, k in ((0, 1), (1, 2)):
        rows = slice(place * total, (place + 1) * total)
        first[rows, :] = jnp.where(even, layers[0, k], layers[1, k]).astype(bf16)
        second[rows, :] = jnp.where(even, layers[1, k], layers[0, k]).astype(bf16)
    kind = [jnp.concatenate([kind_rows[i].astype(f32) + 1.0] * 2, axis=0) for i in range(2)]
    first[2 * total :, :] = jnp.where(even, kind[0], kind[1]).astype(bf16)
    second[2 * total :, :] = jnp.where(even, kind[1], kind[0]).astype(bf16)


def edges(mat_real, mat_loss, field, source, kinds):
    total, _, nz = field.shape
    assert 2 * kinds.shape[0] == 8
    message = pltpu.VMEM((2 * total + 16, nz), bf16)
    anywhere = pl.BlockSpec(memory_space=pl.ANY)
    smem = pl.BlockSpec(memory_space=pltpu.SMEM)
    return pl.pallas_call(
        edge_body,
        out_shape=(message, message),
        in_specs=[smem, smem] + [anywhere] * 3,
        scratch_shapes=[
            pltpu.VMEM((2, 3, total, nz), f32),
            pltpu.VMEM((2, 8, nz), jnp.int32),
            pltpu.SemaphoreType.DMA((2, 3)),
            pltpu.SemaphoreType.DMA((2, 2)),
        ],
        compiler_params=params(6),
        name="edges",
    )(mat_real, mat_loss, *left(field, source, kinds))


def faces(field, kinds, cx, cy):
    channels = field.shape[0] // (cx * cy)

    def body(field, kinds, first, second):
        even = is_even("space")
        for message, x in ((first, jnp.where(even, cx - 1, 0)), (second, jnp.where(even, 0, cx - 1))):
            for c in range(channels):
                rows = pl.ds(pl.multiple_of((c * cx + x) * cy, cy), cy)
                message[c * cy : (c + 1) * cy, :] = field[rows, :].astype(bf16)
            kind = kinds[pl.ds(pl.multiple_of(x * cy, cy), cy), :].astype(f32) + 1.0
            message[channels * cy :, :] = kind.astype(bf16)

    message = pltpu.VMEM((channels * cy + cy, field.shape[1]), bf16)
    return pl.pallas_call(body, out_shape=(message, message), compiler_params=params(6), name="faces")(
        *held(field, kinds)
    )


def first_body(
    mat_real, mat_loss, field, source, kinds, got_first, got_second,
    sweep, columns, column_a, to_first, to_second, near, a_all, b_all, *, cx, cy
):
    total = field.shape[0] // cy
    channels = total // cx
    excite = channels // 2
    a_all[...], b_all[...] = coefficients(kinds[...], mat_real, mat_loss, 0)

    def columns_from(*got):
        for side, own_y in ((0, 0), (1, cy - 1)):
            halo = got[side]
            kind = halo[2 * total :, :].astype(f32)[0:8].astype(jnp.int32)
            col_a = coefficients(kind, mat_real, mat_loss, 1)[0]
            column_a[side] = col_a
            near[side] = halo[0:total, :].astype(f32)
            part = halo[total : 2 * total, :].astype(f32)
            for j in range(0, total, 8):
                own = field[pl.ds(j * cy + own_y, 8, stride=cy), :]
                columns[side, j : j + 8] = part[j : j + 8] + col_a * own

    by_parity("shard", columns_from, got_first, got_second)

    def one(e, _):
        values = [
            [None] + [tiles_at(field, ((p * excite + e) * cx + x) * cy, cy) for x in range(cx)] + [None]
            for p in range(2)
        ]

        def emit(p, x, i, value):
            at = ((p * excite + e) * cx + x) * cy + i
            sweep[pl.ds(pl.multiple_of(at, 8), 8), :] = value

        sweep_brick(values, e, excite, cx, cy, source, near, a_all, b_all, emit)
        return 0

    lax.fori_loop(0, excite, one, 0, unroll=2)
    even_x = is_even("space")
    plane = channels * cy
    for message, x in ((to_first, jnp.where(even_x, cx - 1, 0)), (to_second, jnp.where(even_x, 0, cx - 1))):
        for c in range(channels):
            rows = pl.ds(pl.multiple_of((c * cx + x) * cy, cy), cy)
            message[c * cy : (c + 1) * cy, :] = sweep[rows, :].astype(bf16)
        for side in range(2):
            corner = jnp.concatenate(
                [near.at[side][pl.ds(c * cx + x, 8, stride=cx), :] for c in range(0, channels, 8)], axis=0
            )
            at = plane + side * channels
            message[at : at + channels, :] = corner.astype(bf16)


def first_sweep(mat_real, mat_loss, field, source, kinds, got_first, got_second, cx, cy):
    total, nz = field.shape[0] // cy, field.shape[1]
    channels = total // cx
    smem = pl.BlockSpec(memory_space=pltpu.SMEM)
    vmem = pl.BlockSpec(memory_space=pltpu.VMEM)
    message = pltpu.VMEM((channels * cy + 2 * channels, nz), bf16)
    return pl.pallas_call(
        lambda *refs: first_body(*refs, cx=cx, cy=cy),
        out_shape=(
            pltpu.VMEM(field.shape, f32),
            pltpu.VMEM((2, total, nz), f32),
            pltpu.VMEM((2, 8, nz), f32),
            message,
            message,
        ),
        in_specs=[smem, smem] + [vmem] * 5,
        out_specs=(vmem,) * 5,
        scratch_shapes=[pltpu.VMEM((2, total, nz), f32)] + [pltpu.VMEM((cx * cy, nz), f32)] * 2,
        compiler_params=params(8),
        name="first_sweep",
    )(mat_real, mat_loss, *held(field, source, kinds, got_first, got_second))


def steps(
    volume_field,
    source,
    material,
    mat_real,
    mat_loss,
    surface_map,
    near_boxes,
    near_blocks,
    radiate,
    interp,
    phase_angle,
    far_parents,
    far_kind,
    translate,
):
    every = ("space", "shard")
    groups = lax.axis_size("space")
    slices = lax.axis_size("shard")
    _, cells_x, cells_y, cells_z = volume_field.shape[1:]
    cosine, sine, chosen, depth = prepare(phase_angle, surface_map, cells_x, cells_y, cells_z)
    weights = radiate.reshape(2 * radiate.shape[1], radiate.shape[2])
    field = volume_field.reshape(-1, cells_z)
    flat_source = source.reshape(-1, cells_z)
    kinds = material.reshape(-1, cells_z)
    bricks = (-1, cells_y, cells_z)
    to_y = edges(mat_real, mat_loss, volume_field.reshape(bricks), source.reshape(bricks), material)
    got_y = swap(*to_y, "shard")
    got_early = swap(*faces(field, kinds, cells_x, cells_y), "space")
    sweep, columns, column_a, *to_x = first_sweep(
        mat_real, mat_loss, field, flat_source, kinds, *got_y, cells_x, cells_y
    )
    got_late = swap(*to_x, "space")
    current, currents, pieces = up(
        (mat_real, mat_loss, field, sweep, columns, column_a, flat_source, kinds, *got_early, *got_late),
        chosen,
        depth,
        near_boxes.shape[0],
        weights,
        interp,
        cosine,
        sine,
        cells_x,
        cells_y,
        groups,
        slices,
    )
    directed = lax.all_to_all(pieces, every, split_axis=0, concat_axis=0, tiled=True)
    first, second = swap(currents, currents, "shard")
    factors, order = tables(far_parents.T, far_kind.T, translate)
    combined = far_combine(order, directed, factors, far_parents.shape[0])
    incoming = lax.all_to_all(combined, every, split_axis=0, concat_axis=0, tiled=True)
    near, cosine, sine = near_force(near_boxes.T, currents, first, second, near_blocks, phase_angle)
    forcing = down(incoming, near, weights, interp, cosine, sine, groups, slices)
    return (current.reshape(volume_field.shape), forcing)


def solution(mesh):
    return jax.shard_map(
        steps,
        mesh=mesh,
        in_specs=(
            P(None, None, "space", "shard", None),
            P(None, None, "space", "shard", None),
            P("space", "shard", None),
            P(),
            P(),
            P(("space", "shard"), None),
            P(("space", "shard"), None),
            P(),
            P(),
            P(),
            P(),
            P(),
            P(),
            P(None, None, "shard"),
        ),
        out_specs=(P(None, None, "space", "shard", None), P(("space", "shard"), None, None)),
        check_vma=False,
    )
```

```python
import jax
import jax.numpy as jnp
from jax import lax
from jax.experimental import pallas as pl
from jax.experimental.pallas import tpu as pltpu
from jax.sharding import PartitionSpec as P


relaxation = 0.8
f32 = jnp.float32
bf16 = jnp.bfloat16
CHILDREN = 8


def held(*arrays):
    return [pltpu.with_memory_space_constraint(a, pltpu.VMEM) for a in arrays]


def left(*arrays):
    return [pltpu.with_memory_space_constraint(a, pltpu.HBM) for a in arrays]


def params(mib):
    return pltpu.CompilerParams(vmem_limit_bytes=mib << 20)


def dot(a, b):
    return jnp.dot(a, b, preferred_element_type=f32)


def dot_t(a, b):
    return lax.dot_general(a, b, (((1,), (1,)), ((), ())), preferred_element_type=f32)


def half_turn(v):
    half = v.shape[-2] // 2
    rows = lax.broadcasted_iota(jnp.int32, v.shape, v.ndim - 2)
    swapped = pltpu.roll(v, half, v.ndim - 2)
    return jnp.where(rows < half, -swapped, swapped)


def log2(n):
    assert n & (n - 1) == 0
    return n.bit_length() - 1


def prepare(angle, smap, cx, cy, nz):
    boxes, unknowns = smap.shape

    def body(angle, smap, cosine, sine, chosen, depth):
        cosine[...] = jnp.cos(angle[...])
        sine[...] = jnp.sin(angle[...])
        level = lax.broadcasted_iota(jnp.int32, (nz, unknowns), 0)
        for b in range(boxes):
            key = smap[b : b + 1, :]
            key_z = key & (nz - 1)
            key_x = key >> (log2(nz) + log2(cy))
            lanes = slice(b * unknowns, (b + 1) * unknowns)
            for x in range(cx):
                hit = level == jnp.where(key_x == x, key_z, -1)
                chosen[x * nz : (x + 1) * nz, lanes] = jnp.where(hit, 1.0, 0.0).astype(bf16)
            depth[:, lanes] = jnp.broadcast_to((key >> log2(nz)) & (cy - 1), (8, unknowns))

    shape = pltpu.VMEM(angle.shape, f32)
    return pl.pallas_call(
        body,
        out_shape=(
            shape,
            shape,
            pltpu.VMEM((cx * nz, boxes * unknowns), bf16),
            pltpu.VMEM((8, boxes * unknowns), jnp.int32),
        ),
        compiler_params=params(6),
        name="prepare",
    )(*held(angle, smap))


def swap_pairs(n, first):
    pairs = []
    for i in range(first, n - 1, 2):
        pairs += [(i, i + 1), (i + 1, i)]
    return pairs


def swap(for_even, for_odd, axis):
    n = lax.axis_size(axis)
    received = []
    for k, value in enumerate((for_even, for_odd)):
        received.append(lax.ppermute(value, axis, swap_pairs(n, k)))
    return received


def second_sweep(
    mat_real, mat_loss, field, sweep, columns, column_a, source, kinds, got_first, got_second,
    out, beside, a_all, b_all, store, cx, cy
):
    total = field.shape[0] // cy
    channels = total // cx
    excite = channels // 2
    plane = channels * cy
    a_all[...], b_all[...] = coefficients(kinds[...], mat_real, mat_loss, 0)
    got = below_above("space", got_first, got_second)
    ends = (0, cx - 1)
    for y_side in range(2):
        beside[y_side] = columns[y_side]
        for x_side, x in enumerate(ends):
            corner = got[x_side](2 * plane + y_side * channels, channels)
            factor = column_a[y_side, x : x + 1, :]
            for c in range(0, channels, 8):
                rows = pl.ds(c * cx + x, 8, stride=cx)
                beside.at[y_side][rows, :] = beside.at[y_side][rows, :] + factor * corner[c : c + 8]
    face_a = [
        coefficients(got[side](2 * plane + 2 * channels, cy).astype(jnp.int32), mat_real, mat_loss, 1)[0]
        for side in range(2)
    ]
    for e in range(excite):
        values = []
        for p in range(2):
            c = p * excite + e
            own = [tiles_at(sweep, (c * cx + x) * cy, cy) for x in range(cx)]
            outer = []
            for side, x in enumerate(ends):
                raw = tiles_of(got[side](c * cy, cy))
                factors = tiles_at(a_all, x * cy, cy)
                own[x] = [t + f * h for t, f, h in zip(own[x], factors, raw)]
                part = tiles_of(got[side](plane + c * cy, cy))
                before = tiles_at(field, (c * cx + x) * cy, cy)
                outer.append([q + f * t for q, f, t in zip(part, tiles_of(face_a[side]), before)])
            values.append([outer[0]] + own + [outer[1]])

        def emit(p, x, new, e=e):
            at = ((p * excite + e) * cx + x) * cy
            whole = jnp.concatenate(new, axis=0)
            out[at : at + cy, :] = whole
            store(p * excite + e, x, whole)

        sweep_brick(values, e, excite, cx, cy, source, beside, a_all, b_all, emit)


def gather_rows(parts):
    row = lax.broadcasted_iota(jnp.int32, parts[0].shape, 0)
    upper = row < 4
    fours = [
        jnp.where(upper, parts[r], parts[r + 4]) + pltpu.roll(jnp.where(upper, parts[r + 4], parts[r]), 4, 0)
        for r in range(4)
    ]
    second = (row & 2) == 0
    twos = [
        jnp.where(second, fours[r] + pltpu.roll(fours[r], 6, 0), fours[r + 2] + pltpu.roll(fours[r + 2], 2, 0))
        for r in range(2)
    ]
    first = (row & 1) == 0
    return jnp.where(first, twos[0] + pltpu.roll(twos[0], 7, 0), twos[1] + pltpu.roll(twos[1], 1, 0))


def up_body(
    mat_real, mat_loss, field, sweep, columns, column_a, source, kinds, got_first, got_second,
    chosen, depth, radiate, interp, cosine, sine, volume, cur, out,
    beside, cells, rows, fresh, a_all, b_all, sem, *, cx, cy, groups, slices
):
    nz = field.shape[1]
    channels = field.shape[0] // (cx * cy)
    excite = channels // 2
    group = excite // groups
    assert 2 * group == 8 and cy % 8 == 0
    boxes = cur.shape[0]
    unknowns = depth.shape[1] // boxes

    def store(c, x, value):
        cells[c * cy : (c + 1) * cy, x * nz : (x + 1) * nz] = value.astype(bf16)

    second_sweep(
        mat_real, mat_loss, field, sweep, columns, column_a, source, kinds, got_first, got_second,
        fresh, beside, a_all, b_all, store, cx, cy
    )
    leaving = pltpu.make_async_copy(fresh, volume, sem)
    leaving.start()
    pair = 2
    for b in range(0, boxes, pair):
        lanes = slice(b * unknowns, (b + pair) * unknowns)
        picked = dot(cells[...], chosen[:, lanes])
        key_y = depth[:, lanes]
        row = lax.broadcasted_iota(jnp.int32, key_y.shape, 0)
        hits = [key_y == row + y for y in range(0, cy, 8)]
        found = []
        for s in range(groups):
            parts = []
            for r in range(2 * group):
                c = (r // group) * excite + s * group + r % group
                kept = jnp.zeros(key_y.shape, f32)
                for i, hit in enumerate(hits):
                    kept = jnp.where(hit, picked[c * cy + i * 8 : c * cy + i * 8 + 8], kept)
                parts.append(kept)
            found.append(gather_rows(parts))
        found = jnp.concatenate(found, axis=0)
        for j in range(pair):
            own = found[:, j * unknowns : (j + 1) * unknowns].reshape(groups, 2 * group, unknowns)
            turned = half_turn(own)
            both = jnp.concatenate([own, turned], axis=2).reshape(channels, 2 * unknowns)
            rows[(b + j) * channels : (b + j + 1) * channels, :] = both.astype(bf16)
            parts = [
                jnp.concatenate([own[s, t * group : (t + 1) * group] for s in range(groups)], axis=0)
                for t in range(2)
            ]
            cur[b + j] = jnp.concatenate(parts, axis=1).astype(bf16)
    leaf = dot(rows[...], radiate[...]).astype(bf16)
    directions = interp.shape[1]
    width = directions // slices
    tile = max(width, 256)
    parents = boxes // CHILDREN
    for n in range(0, directions, tile):
        spread = dot(leaf, interp[:, n : n + tile]).reshape(parents, CHILDREN, groups, 2 * group, tile)
        along = jnp.zeros((parents, groups, 2 * group, tile), f32)
        across = jnp.zeros((parents, groups, 2 * group, tile), f32)
        for child in range(CHILDREN):
            along = along + cosine[child : child + 1, n : n + tile] * spread[:, child]
            across = across + sine[child : child + 1, n : n + tile] * spread[:, child]
        whole = (along + half_turn(across)).astype(bf16)
        for s in range(groups):
            piece = jnp.concatenate([whole[p, s] for p in range(parents)], axis=0)
            for k in range(tile // width):
                out[s * slices + n // width + k] = piece[:, k * width : (k + 1) * width]
    leaving.wait()


def up(volume_args, chosen, depth, boxes, radiate, interp, cosine, sine, cx, cy, groups, slices):
    field = volume_args[2]
    nz = field.shape[1]
    total = field.shape[0] // cy
    channels = total // cx
    unknowns = depth.shape[1] // boxes
    width = interp.shape[1] // slices
    piece_rows = boxes // CHILDREN * (channels // groups)
    smem = pl.BlockSpec(memory_space=pltpu.SMEM)
    vmem = pl.BlockSpec(memory_space=pltpu.VMEM)
    return pl.pallas_call(
        lambda *refs: up_body(*refs, cx=cx, cy=cy, groups=groups, slices=slices),
        out_shape=(
            pltpu.HBM(field.shape, f32),
            pltpu.VMEM((boxes, channels // 2, 2 * unknowns), bf16),
            jax.ShapeDtypeStruct((groups * slices, piece_rows, width), bf16),
        ),
        in_specs=[smem, smem] + [vmem] * 14,
        out_specs=(pl.BlockSpec(memory_space=pltpu.HBM), vmem, vmem),
        scratch_shapes=[
            pltpu.VMEM((2, total, nz), f32),
            pltpu.VMEM((channels * cy, cx * nz), bf16),
            pltpu.VMEM((boxes * channels, 2 * unknowns), bf16),
            pltpu.VMEM(field.shape, f32),
            pltpu.VMEM((cx * cy, nz), f32),
            pltpu.VMEM((cx * cy, nz), f32),
            pltpu.SemaphoreType.DMA(()),
        ],
        compiler_params=params(16), name="up",
    )(*volume_args[:2], *held(*volume_args[2:], chosen, depth, radiate, interp, cosine, sine))


def tables(lists, kinds, translate, angle):
    far, targets = lists.shape

    def body(lists, kinds, translate, angle, factors, order, cosine, sine):
        cosine[...] = jnp.cos(angle[...])
        sine[...] = jnp.sin(angle[...])

        def one(t, _):
            for f in range(far):
                order[t * far + f] = lists[f, t]
                factors[t * far + f] = translate[kinds[f, t]]
            return 0

        lax.fori_loop(0, targets, one, 0, unroll=2)

    smem = pl.BlockSpec(memory_space=pltpu.SMEM)
    vmem = pl.BlockSpec(memory_space=pltpu.VMEM)
    return pl.pallas_call(
        body,
        out_shape=(
            pltpu.VMEM((targets * far,) + translate.shape[1:], f32),
            jax.ShapeDtypeStruct((targets * far,), jnp.int32),
            pltpu.VMEM(angle.shape, f32),
            pltpu.VMEM(angle.shape, f32),
        ),
        in_specs=[smem, smem, vmem, vmem],
        out_specs=(vmem, smem, vmem, vmem),
        compiler_params=params(8),
        name="tables",
    )(lists, kinds, *held(translate, angle))


def far_body(order, sources, factors, out, plain, *, targets):
    devices, piece_rows, width = sources.shape
    far = order.shape[0] // targets
    per = targets // devices
    tile = piece_rows // per
    plain[...] = sources[...].astype(f32).reshape(targets, tile, width)

    def one(d, _):
        results = []
        for j in range(per):
            along = jnp.zeros((tile, width), f32)
            across = jnp.zeros((tile, width), f32)
            for f in range(far):
                pair = d * (per * far) + (j * far + f)
                source = plain[order[pair]]
                factor = factors[pair]
                along = along + factor[0:1] * source
                across = across + factor[1:2] * source
            results.append(along + half_turn(across))
        out[d] = jnp.concatenate(results, axis=0).astype(bf16)
        return 0

    lax.fori_loop(0, devices, one, 0, unroll=4)


def far_combine(order, sources, factors, targets):
    devices, piece_rows, width = sources.shape
    tile = piece_rows // (targets // devices)
    smem = pl.BlockSpec(memory_space=pltpu.SMEM)
    vmem = pl.BlockSpec(memory_space=pltpu.VMEM)
    return pl.pallas_call(
        lambda *refs: far_body(*refs, targets=targets),
        out_shape=jax.ShapeDtypeStruct(sources.shape, bf16),
        in_specs=[smem, vmem, vmem],
        out_specs=vmem,
        scratch_shapes=[pltpu.VMEM((targets, tile, width), f32)],
        compiler_params=params(8),
        name="far",
    )(order, *held(sources, factors))


def near_body(lists, own, first, second, blocks, out, boxes_all, rows):
    boxes, excite, k = own.shape
    slots = lists.shape[0]
    shard = lax.axis_index("shard")
    base = (lax.axis_index("space") * lax.axis_size("shard") + shard) * boxes
    even = lax.rem(shard, 2) == 0
    above = jnp.where(even, 0, boxes)
    below = jnp.where(even, 3 * boxes, 2 * boxes)
    boxes_all[0:boxes] = own[...]
    boxes_all[boxes : 2 * boxes] = first[...]
    boxes_all[2 * boxes : 3 * boxes] = second[...]
    for b in range(boxes):
        for s in range(slots):
            away = lists[s, b] - base
            spot = away + jnp.where(away < 0, below, jnp.where(away < boxes, 0, above))
            rows[b * excite : (b + 1) * excite, s * k : (s + 1) * k] = boxes_all[spot]
    out[...] = dot(rows[...], blocks[...]).reshape(out.shape)


def near_force(lists, own, first, second, blocks):
    boxes, excite, k = own.shape
    slots = lists.shape[0]
    smem = pl.BlockSpec(memory_space=pltpu.SMEM)
    vmem = pl.BlockSpec(memory_space=pltpu.VMEM)
    return pl.pallas_call(
        near_body,
        out_shape=pltpu.VMEM((boxes, excite, k), f32),
        in_specs=[smem] + [vmem] * 4,
        out_specs=vmem,
        scratch_shapes=[
            pltpu.VMEM((3 * boxes, excite, k), bf16),
            pltpu.VMEM((boxes * excite, slots * k), bf16),
        ],
        compiler_params=params(6), name="near",
    )(lists, *held(own, first, second, blocks.reshape(slots * k, k)))


def down_body(pieces, near, radiate, interp, cosine, sine, out, shifted, *, groups, slices):
    _, _, width = pieces.shape
    boxes, excite, both = out.shape
    unknowns = both // 2
    group = excite // groups
    tile = 2 * group
    parents = boxes // CHILDREN
    for h in range(slices):
        lanes = slice(h * width, (h + 1) * width)
        for s in range(0, groups, 2):
            pair = [pieces[(s + k) * slices + h].astype(f32) for k in range(2)]
            for p in range(parents):
                incoming = jnp.concatenate([v[p * tile : (p + 1) * tile] for v in pair], axis=0)
                turned = half_turn(incoming.reshape(2, tile, width)).reshape(2 * tile, width)
                for child in range(CHILDREN):
                    row = ((p * CHILDREN + child) * groups + s) * tile
                    value = cosine[child : child + 1, lanes] * incoming - sine[child : child + 1, lanes] * turned
                    shifted[row : row + 2 * tile, lanes] = value.astype(bf16)
    leaf_in = dot_t(shifted[...], interp[...]).astype(bf16)
    back = dot_t(leaf_in, radiate[...]).reshape(boxes, groups, tile, both)
    own = back[..., :unknowns] - half_turn(back[..., unknowns:])
    for b in range(boxes):
        parts = [
            jnp.concatenate([own[b, s, t * group : (t + 1) * group] for s in range(groups)], axis=0)
            for t in range(2)
        ]
        out[b] = jnp.concatenate(parts, axis=1) + near[b]


def down(pieces, near, radiate, interp, cosine, sine, groups, slices):
    boxes, excite, _ = near.shape
    return pl.pallas_call(
        lambda *refs: down_body(*refs, groups=groups, slices=slices),
        out_shape=jax.ShapeDtypeStruct(near.shape, f32),
        scratch_shapes=[pltpu.VMEM((boxes * excite * 2, interp.shape[1]), bf16)],
        compiler_params=params(16), name="down",
    )(*held(pieces, near, radiate, interp, cosine, sine))


def is_even(axis):
    return lax.rem(lax.axis_index(axis), 2) == 0


def coefficients(kinds, mat_real, mat_loss, base):
    diagonal = jnp.full(kinds.shape, 6.0, f32)
    loss = jnp.zeros(kinds.shape, f32)
    for k in range(mat_real.shape[0]):
        present = kinds == k + base
        diagonal = jnp.where(present, 6.0 + mat_real[k], diagonal)
        loss = jnp.where(present, mat_loss[k], loss)
    a = relaxation / diagonal
    if base > 0:
        a = jnp.where(kinds < base, 0.0, a)
    return a, a * loss


def along_z(v):
    lanes = v.shape[-1]
    lane = lax.broadcasted_iota(jnp.int32, v.shape, v.ndim - 1)
    lower = jnp.where(lane == 0, 0.0, pltpu.roll(v, 1, v.ndim - 1))
    upper = jnp.where(lane == lanes - 1, 0.0, pltpu.roll(v, lanes - 1, v.ndim - 1))
    return lower + upper


def along_y(tiles, low, high):
    row = lax.broadcasted_iota(jnp.int32, tiles[0].shape, 0)
    lower = [low] + [pltpu.roll(t, 1, 0) for t in tiles]
    upper = [pltpu.roll(t, 7, 0) for t in tiles] + [high]
    return [
        jnp.where(row == 0, lower[i], lower[i + 1]) + jnp.where(row == 7, upper[i + 1], upper[i])
        for i in range(len(tiles))
    ]


def relaxed(v, total, a, b):
    keep = 1.0 - relaxation
    return (
        keep * v[0] + a * total[0] + b * v[1],
        keep * v[1] + a * total[1] - b * v[0],
    )


def tiles_of(value):
    return [value[i : i + 8] for i in range(0, value.shape[0], 8)]


def tiles_at(ref, at, rows):
    return [ref[i : i + 8, :] for i in range(at, at + rows, 8)]


def sweep_brick(values, e, excite, cx, cy, source, beside, a, b, emit):
    for x in range(cx):
        sums = []
        for p in range(2):
            at = (p * excite + e) * cx + x
            edge = [jnp.broadcast_to(beside[side, at : at + 1, :], (8, source.shape[1])) for side in range(2)]
            here = values[p][x + 1]
            total = [n + along_z(t) + y for n, t, y in zip(tiles_at(source, at * cy, cy), here, along_y(here, *edge))]
            for other in (values[p][x], values[p][x + 2]):
                if other is not None:
                    total = [n + t for n, t in zip(total, other)]
            sums.append(total)
        new = []
        for i in range(cy // 8):
            rows = slice(x * cy + i * 8, x * cy + i * 8 + 8)
            new.append(
                relaxed((values[0][x + 1][i], values[1][x + 1][i]), (sums[0][i], sums[1][i]), a[rows, :], b[rows, :])
            )
        for p in range(2):
            emit(p, x, [pair[p] for pair in new])


def below_above(axis, first, second):
    even = is_even(axis)

    def pick(one, two):
        def rows(at, size):
            return jnp.where(even, one[at : at + size, :].astype(f32), two[at : at + size, :].astype(f32))

        return rows

    return pick(second, first), pick(first, second)


def edge_body(
    real_table, loss_table, field, source, kinds, first, second, layers, kind_rows, mat_real, mat_loss,
    sem, kind_sem, table_sem
):
    total, cy, nz = field.shape
    cx = kinds.shape[0]
    even = is_even("shard")
    faces = ((cy - 2, cy - 1), (1, 0))
    copies = [
        pltpu.make_async_copy(real_table, mat_real, table_sem.at[0]),
        pltpu.make_async_copy(loss_table, mat_loss, table_sem.at[1]),
    ]
    for i, (inner, outer) in enumerate(faces):
        for k, (ref, y) in enumerate(((field, inner), (field, outer), (source, outer))):
            copies.append(pltpu.make_async_copy(ref.at[:, y], layers.at[i, k], sem.at[i, k]))
        for k in range(2):
            copies.append(
                pltpu.make_async_copy(kinds.at[:, outer], kind_rows.at[i, pl.ds(k * cx, cx)], kind_sem.at[i, k])
            )
    for copy in copies:
        copy.start()
    for copy in copies:
        copy.wait()
    row = lax.broadcasted_iota(jnp.int32, (8, nz), 0) & (cx - 1)
    for i in range(2):
        a, b = coefficients(kind_rows[i], mat_real, mat_loss, 0)
        for j in range(0, total // 2, 8):
            v, sums = [], []
            for part in range(2):
                rows = slice(part * (total // 2) + j, part * (total // 2) + j + 8)
                here = layers[i, 1, rows, :]
                n = layers[i, 0, rows, :] + layers[i, 2, rows, :] + along_z(here)
                n = n + jnp.where(row == 0, 0.0, pltpu.roll(here, 1, 0))
                n = n + jnp.where(row == cx - 1, 0.0, pltpu.roll(here, 7, 0))
                v.append(here)
                sums.append(n)
            new = relaxed(v, sums, a, b)
            for part in range(2):
                layers[i, 2, part * (total // 2) + j : part * (total // 2) + j + 8, :] = new[part]
    for place, k in ((0, 1), (1, 2)):
        rows = slice(place * total, (place + 1) * total)
        first[rows, :] = jnp.where(even, layers[0, k], layers[1, k]).astype(bf16)
        second[rows, :] = jnp.where(even, layers[1, k], layers[0, k]).astype(bf16)
    kind = [jnp.concatenate([kind_rows[i].astype(f32) + 1.0] * 2, axis=0) for i in range(2)]
    first[2 * total :, :] = jnp.where(even, kind[0], kind[1]).astype(bf16)
    second[2 * total :, :] = jnp.where(even, kind[1], kind[0]).astype(bf16)


def edges(mat_real, mat_loss, field, source, kinds):
    total, _, nz = field.shape
    assert 2 * kinds.shape[0] == 8
    message = pltpu.VMEM((2 * total + 16, nz), bf16)
    anywhere = pl.BlockSpec(memory_space=pl.ANY)
    return pl.pallas_call(
        edge_body,
        out_shape=(message, message),
        in_specs=[anywhere] * 5,
        scratch_shapes=[
            pltpu.VMEM((2, 3, total, nz), f32),
            pltpu.VMEM((2, 8, nz), jnp.int32),
            pltpu.SMEM(mat_real.shape, f32),
            pltpu.SMEM(mat_loss.shape, f32),
            pltpu.SemaphoreType.DMA((2, 3)),
            pltpu.SemaphoreType.DMA((2, 2)),
            pltpu.SemaphoreType.DMA((2,)),
        ],
        compiler_params=params(6),
        name="edges",
    )(*left(mat_real, mat_loss, field, source, kinds))


def first_body(
    mat_real, mat_loss, field, source, kinds, got_first, got_second,
    sweep, columns, column_a, to_first, to_second, near, a_all, b_all, *, cx, cy
):
    total = field.shape[0] // cy
    channels = total // cx
    excite = channels // 2
    a_all[...], b_all[...] = coefficients(kinds[...], mat_real, mat_loss, 0)

    for side, (halo, own_y) in enumerate(zip(below_above("shard", got_first, got_second), (0, cy - 1))):
        kind = halo(2 * total, 16)[0:8].astype(jnp.int32)
        col_a = coefficients(kind, mat_real, mat_loss, 1)[0]
        column_a[side] = col_a
        near[side] = halo(0, total)
        for j in range(0, total, 16):
            part = halo(total + j, 16)
            for k in (0, 8):
                own = field[pl.ds((j + k) * cy + own_y, 8, stride=cy), :]
                columns[side, j + k : j + k + 8] = part[k : k + 8] + col_a * own
    for e in range(excite):
        values = [
            [None] + [tiles_at(field, ((p * excite + e) * cx + x) * cy, cy) for x in range(cx)] + [None]
            for p in range(2)
        ]

        def emit(p, x, new, e=e):
            at = ((p * excite + e) * cx + x) * cy
            sweep[at : at + cy, :] = jnp.concatenate(new, axis=0)

        sweep_brick(values, e, excite, cx, cy, source, near, a_all, b_all, emit)
    even_x = is_even("space")
    plane = channels * cy
    for message, x in ((to_first, jnp.where(even_x, cx - 1, 0)), (to_second, jnp.where(even_x, 0, cx - 1))):
        for c in range(channels):
            rows = pl.ds(pl.multiple_of((c * cx + x) * cy, cy), cy)
            message[c * cy : (c + 1) * cy, :] = field[rows, :].astype(bf16)
            message[plane + c * cy : plane + (c + 1) * cy, :] = sweep[rows, :].astype(bf16)
        for side in range(2):
            corner = jnp.concatenate(
                [near.at[side][pl.ds(c * cx + x, 8, stride=cx), :] for c in range(0, channels, 8)], axis=0
            )
            at = 2 * plane + side * channels
            message[at : at + channels, :] = corner.astype(bf16)
        kind = kinds[pl.ds(pl.multiple_of(x * cy, cy), cy), :].astype(f32) + 1.0
        message[2 * plane + 2 * channels :, :] = kind.astype(bf16)


def first_sweep(mat_real, mat_loss, field, source, kinds, got_first, got_second, cx, cy):
    total, nz = field.shape[0] // cy, field.shape[1]
    channels = total // cx
    smem = pl.BlockSpec(memory_space=pltpu.SMEM)
    vmem = pl.BlockSpec(memory_space=pltpu.VMEM)
    message = pltpu.VMEM((2 * channels * cy + 2 * channels + cy, nz), bf16)
    return pl.pallas_call(
        lambda *refs: first_body(*refs, cx=cx, cy=cy),
        out_shape=(
            pltpu.VMEM(field.shape, f32),
            pltpu.VMEM((2, total, nz), f32),
            pltpu.VMEM((2, 8, nz), f32),
            message,
            message,
        ),
        in_specs=[smem, smem] + [vmem] * 5,
        out_specs=(vmem,) * 5,
        scratch_shapes=[pltpu.VMEM((2, total, nz), f32)] + [pltpu.VMEM((cx * cy, nz), f32)] * 2,
        compiler_params=params(8),
        name="first_sweep",
    )(mat_real, mat_loss, *held(field, source, kinds, got_first, got_second))


def steps(
    volume_field,
    source,
    material,
    mat_real,
    mat_loss,
    surface_map,
    near_boxes,
    near_blocks,
    radiate,
    interp,
    phase_angle,
    far_parents,
    far_kind,
    translate,
):
    every = ("space", "shard")
    groups = lax.axis_size("space")
    slices = lax.axis_size("shard")
    _, cells_x, cells_y, cells_z = volume_field.shape[1:]
    cosine, sine, chosen, depth = prepare(phase_angle, surface_map, cells_x, cells_y, cells_z)
    weights = radiate.reshape(2 * radiate.shape[1], radiate.shape[2])
    field = volume_field.reshape(-1, cells_z)
    flat_source = source.reshape(-1, cells_z)
    kinds = material.reshape(-1, cells_z)
    bricks = (-1, cells_y, cells_z)
    to_y = edges(mat_real, mat_loss, volume_field.reshape(bricks), source.reshape(bricks), material)
    got_y = swap(*to_y, "shard")
    sweep, columns, column_a, *to_x = first_sweep(
        mat_real, mat_loss, field, flat_source, kinds, *got_y, cells_x, cells_y
    )
    got_x = swap(*to_x, "space")
    current, currents, pieces = up(
        (mat_real, mat_loss, field, sweep, columns, column_a, flat_source, kinds, *got_x),
        chosen,
        depth,
        near_boxes.shape[0],
        weights,
        interp,
        cosine,
        sine,
        cells_x,
        cells_y,
        groups,
        slices,
    )
    directed = lax.all_to_all(pieces, every, split_axis=0, concat_axis=0, tiled=True)
    first, second = swap(currents, currents, "shard")
    factors, order, cosine, sine = tables(far_parents.T, far_kind.T, translate, phase_angle)
    combined = far_combine(order, directed, factors, far_parents.shape[0])
    incoming = lax.all_to_all(combined, every, split_axis=0, concat_axis=0, tiled=True)
    near = near_force(near_boxes.T, currents, first, second, near_blocks)
    forcing = down(incoming, near, weights, interp, cosine, sine, groups, slices)
    return (current.reshape(volume_field.shape), forcing)


def solution(mesh):
    return jax.shard_map(
        steps,
        mesh=mesh,
        in_specs=(
            P(None, None, "space", "shard", None),
            P(None, None, "space", "shard", None),
            P("space", "shard", None),
            P(),
            P(),
            P(("space", "shard"), None),
            P(("space", "shard"), None),
            P(),
            P(),
            P(),
            P(),
            P(),
            P(),
            P(None, None, "shard"),
        ),
        out_specs=(P(None, None, "space", "shard", None), P(("space", "shard"), None, None)),
        check_vma=False,
    )
```

```python
import jax
import jax.numpy as jnp
from jax import lax
from jax.experimental import pallas as pl
from jax.experimental.pallas import tpu as pltpu
from jax.sharding import PartitionSpec as P


relaxation = 0.8
f32 = jnp.float32
bf16 = jnp.bfloat16
CHILDREN = 8


def held(*arrays):
    return [pltpu.with_memory_space_constraint(a, pltpu.VMEM) for a in arrays]


def left(*arrays):
    return [pltpu.with_memory_space_constraint(a, pltpu.HBM) for a in arrays]


def params(mib):
    return pltpu.CompilerParams(vmem_limit_bytes=mib << 20)


def dot(a, b):
    return jnp.dot(a, b, preferred_element_type=f32)


def dot_t(a, b):
    return lax.dot_general(a, b, (((1,), (1,)), ((), ())), preferred_element_type=f32)


def half_turn(v):
    half = v.shape[-2] // 2
    rows = lax.broadcasted_iota(jnp.int32, v.shape, v.ndim - 2)
    swapped = pltpu.roll(v, half, v.ndim - 2)
    return jnp.where(rows < half, -swapped, swapped)


def log2(n):
    assert n & (n - 1) == 0
    return n.bit_length() - 1


def prepare(angle, smap, cx, cy, nz):
    boxes, unknowns = smap.shape

    def body(angle, smap, cosine, sine, chosen, depth):
        cosine[...] = jnp.cos(angle[...])
        sine[...] = jnp.sin(angle[...])
        level = lax.broadcasted_iota(jnp.int32, (nz, unknowns), 0)
        for b in range(boxes):
            key = smap[b : b + 1, :]
            key_z = key & (nz - 1)
            key_x = key >> (log2(nz) + log2(cy))
            lanes = slice(b * unknowns, (b + 1) * unknowns)
            for x in range(cx):
                hit = level == jnp.where(key_x == x, key_z, -1)
                chosen[x * nz : (x + 1) * nz, lanes] = jnp.where(hit, 1.0, 0.0).astype(bf16)
            depth[:, lanes] = jnp.broadcast_to((key >> log2(nz)) & (cy - 1), (8, unknowns))

    shape = pltpu.VMEM(angle.shape, f32)
    return pl.pallas_call(
        body,
        out_shape=(
            shape,
            shape,
            pltpu.VMEM((cx * nz, boxes * unknowns), bf16),
            pltpu.VMEM((8, boxes * unknowns), jnp.int32),
        ),
        compiler_params=params(6),
        name="prepare",
    )(*held(angle, smap))


def swap_pairs(n, first):
    pairs = []
    for i in range(first, n - 1, 2):
        pairs += [(i, i + 1), (i + 1, i)]
    return pairs


def swap(for_even, for_odd, axis):
    n = lax.axis_size(axis)
    received = []
    for k, value in enumerate((for_even, for_odd)):
        received.append(lax.ppermute(value, axis, swap_pairs(n, k)))
    return received


def second_sweep(
    table, field, sweep, columns, column_a, source, kinds, got_first, got_second,
    out, beside, a_all, b_all, store, cx, cy
):
    total = field.shape[0] // cy
    channels = total // cx
    excite = channels // 2
    plane = channels * cy
    a_all[...], b_all[...] = coefficients(kinds[...], table, 0)
    got = below_above("space", got_first, got_second)
    ends = (0, cx - 1)
    for y_side in range(2):
        beside[y_side] = columns[y_side]
        for x_side, x in enumerate(ends):
            corner = got[x_side](2 * plane + y_side * channels, channels)
            factor = column_a[y_side, x : x + 1, :]
            for c in range(0, channels, 8):
                rows = pl.ds(c * cx + x, 8, stride=cx)
                beside.at[y_side][rows, :] = beside.at[y_side][rows, :] + factor * corner[c : c + 8]
    face_a = [
        coefficients(got[side](2 * plane + 2 * channels, cy).astype(jnp.int32), table, 1)[0]
        for side in range(2)
    ]
    for e in range(excite):
        values = []
        for p in range(2):
            c = p * excite + e
            own = [tiles_at(sweep, (c * cx + x) * cy, cy) for x in range(cx)]
            outer = []
            for side, x in enumerate(ends):
                raw = tiles_of(got[side](c * cy, cy))
                factors = tiles_at(a_all, x * cy, cy)
                own[x] = [t + f * h for t, f, h in zip(own[x], factors, raw)]
                part = tiles_of(got[side](plane + c * cy, cy))
                before = tiles_at(field, (c * cx + x) * cy, cy)
                outer.append([q + f * t for q, f, t in zip(part, tiles_of(face_a[side]), before)])
            values.append([outer[0]] + own + [outer[1]])

        def emit(p, x, new, e=e):
            at = ((p * excite + e) * cx + x) * cy
            whole = jnp.concatenate(new, axis=0)
            out[at : at + cy, :] = whole
            store(p * excite + e, x, whole)

        sweep_brick(values, e, excite, cx, cy, source, beside, a_all, b_all, emit)


def gather_rows(parts):
    row = lax.broadcasted_iota(jnp.int32, parts[0].shape, 0)
    upper = row < 4
    fours = [
        jnp.where(upper, parts[r], parts[r + 4]) + pltpu.roll(jnp.where(upper, parts[r + 4], parts[r]), 4, 0)
        for r in range(4)
    ]
    second = (row & 2) == 0
    twos = [
        jnp.where(second, fours[r] + pltpu.roll(fours[r], 6, 0), fours[r + 2] + pltpu.roll(fours[r + 2], 2, 0))
        for r in range(2)
    ]
    first = (row & 1) == 0
    return jnp.where(first, twos[0] + pltpu.roll(twos[0], 7, 0), twos[1] + pltpu.roll(twos[1], 1, 0))


def up_body(
    table, field, sweep, columns, column_a, source, kinds, got_first, got_second,
    chosen, depth, radiate, interp, cosine, sine, volume, cur, out,
    beside, cells, rows, fresh, a_all, b_all, sem, *, cx, cy, groups, slices
):
    nz = field.shape[1]
    channels = field.shape[0] // (cx * cy)
    excite = channels // 2
    group = excite // groups
    assert 2 * group == 8 and cy % 8 == 0
    boxes = cur.shape[0]
    unknowns = depth.shape[1] // boxes

    def store(c, x, value):
        cells[c * cy : (c + 1) * cy, x * nz : (x + 1) * nz] = value.astype(bf16)

    second_sweep(
        table, field, sweep, columns, column_a, source, kinds, got_first, got_second,
        fresh, beside, a_all, b_all, store, cx, cy
    )
    leaving = pltpu.make_async_copy(fresh, volume, sem)
    leaving.start()
    pair = 2
    for b in range(0, boxes, pair):
        lanes = slice(b * unknowns, (b + pair) * unknowns)
        picked = dot(cells[...], chosen[:, lanes])
        key_y = depth[:, lanes]
        row = lax.broadcasted_iota(jnp.int32, key_y.shape, 0)
        hits = [key_y == row + y for y in range(0, cy, 8)]
        found = []
        for s in range(groups):
            parts = []
            for r in range(2 * group):
                c = (r // group) * excite + s * group + r % group
                kept = jnp.zeros(key_y.shape, f32)
                for i, hit in enumerate(hits):
                    kept = jnp.where(hit, picked[c * cy + i * 8 : c * cy + i * 8 + 8], kept)
                parts.append(kept)
            found.append(gather_rows(parts))
        found = jnp.concatenate(found, axis=0)
        for j in range(pair):
            own = found[:, j * unknowns : (j + 1) * unknowns].reshape(groups, 2 * group, unknowns)
            turned = half_turn(own)
            both = jnp.concatenate([own, turned], axis=2).reshape(channels, 2 * unknowns)
            rows[(b + j) * channels : (b + j + 1) * channels, :] = both.astype(bf16)
            parts = [
                jnp.concatenate([own[s, t * group : (t + 1) * group] for s in range(groups)], axis=0)
                for t in range(2)
            ]
            cur[b + j] = jnp.concatenate(parts, axis=1).astype(bf16)
    leaf = dot(rows[...], radiate[...]).astype(bf16)
    directions = interp.shape[1]
    width = directions // slices
    tile = max(width, 256)
    parents = boxes // CHILDREN
    for n in range(0, directions, tile):
        spread = dot(leaf, interp[:, n : n + tile]).reshape(parents, CHILDREN, groups, 2 * group, tile)
        along = jnp.zeros((parents, groups, 2 * group, tile), f32)
        across = jnp.zeros((parents, groups, 2 * group, tile), f32)
        for child in range(CHILDREN):
            along = along + cosine[child : child + 1, n : n + tile] * spread[:, child]
            across = across + sine[child : child + 1, n : n + tile] * spread[:, child]
        whole = (along + half_turn(across)).astype(bf16)
        for s in range(groups):
            piece = jnp.concatenate([whole[p, s] for p in range(parents)], axis=0)
            for k in range(tile // width):
                out[s * slices + n // width + k] = piece[:, k * width : (k + 1) * width]
    leaving.wait()


def up(volume_args, chosen, depth, boxes, radiate, interp, cosine, sine, cx, cy, groups, slices):
    field = volume_args[1]
    nz = field.shape[1]
    total = field.shape[0] // cy
    channels = total // cx
    unknowns = depth.shape[1] // boxes
    width = interp.shape[1] // slices
    piece_rows = boxes // CHILDREN * (channels // groups)
    vmem = pl.BlockSpec(memory_space=pltpu.VMEM)
    return pl.pallas_call(
        lambda *refs: up_body(*refs, cx=cx, cy=cy, groups=groups, slices=slices),
        out_shape=(
            pltpu.HBM(field.shape, f32),
            pltpu.VMEM((boxes, channels // 2, 2 * unknowns), bf16),
            pltpu.HBM((groups * slices, piece_rows, width), bf16),
        ),
        in_specs=[vmem] * 15,
        out_specs=(pl.BlockSpec(memory_space=pltpu.HBM), vmem, vmem),
        scratch_shapes=[
            pltpu.VMEM((2, total, nz), f32),
            pltpu.VMEM((channels * cy, cx * nz), bf16),
            pltpu.VMEM((boxes * channels, 2 * unknowns), bf16),
            pltpu.VMEM(field.shape, f32),
            pltpu.VMEM((cx * cy, nz), f32),
            pltpu.VMEM((cx * cy, nz), f32),
            pltpu.SemaphoreType.DMA(()),
        ],
        compiler_params=params(16), name="up",
    )(*held(*volume_args, chosen, depth, radiate, interp, cosine, sine))


def tables(lists, kinds, translate):
    far, targets = lists.shape

    def body(lists, kinds, translate, factors, order):
        def one(t, _):
            for f in range(far):
                order[t * far + f] = lists[f, t]
                factors[t * far + f] = translate[kinds[f, t]]
            return 0

        lax.fori_loop(0, targets, one, 0, unroll=2)

    smem = pl.BlockSpec(memory_space=pltpu.SMEM)
    vmem = pl.BlockSpec(memory_space=pltpu.VMEM)
    return pl.pallas_call(
        body,
        out_shape=(
            pltpu.VMEM((targets * far,) + translate.shape[1:], f32),
            jax.ShapeDtypeStruct((targets * far,), jnp.int32),
        ),
        in_specs=[smem, smem, vmem],
        out_specs=(vmem, smem),
        compiler_params=params(8),
        name="tables",
    )(lists, kinds, *held(translate))


def far_body(order, sources, factors, out, plain, *, targets):
    devices, piece_rows, width = sources.shape
    far = order.shape[0] // targets
    per = targets // devices
    tile = piece_rows // per
    plain[...] = sources[...].astype(f32).reshape(targets, tile, width)

    def one(d, _):
        results = []
        for j in range(per):
            along = jnp.zeros((tile, width), f32)
            across = jnp.zeros((tile, width), f32)
            for f in range(far):
                pair = d * (per * far) + (j * far + f)
                source = plain[order[pair]]
                factor = factors[pair]
                along = along + factor[0:1] * source
                across = across + factor[1:2] * source
            results.append(along + half_turn(across))
        out[d] = jnp.concatenate(results, axis=0).astype(bf16)
        return 0

    lax.fori_loop(0, devices, one, 0, unroll=4)


def far_combine(order, sources, factors, targets):
    devices, piece_rows, width = sources.shape
    tile = piece_rows // (targets // devices)
    smem = pl.BlockSpec(memory_space=pltpu.SMEM)
    vmem = pl.BlockSpec(memory_space=pltpu.VMEM)
    return pl.pallas_call(
        lambda *refs: far_body(*refs, targets=targets),
        out_shape=pltpu.HBM(sources.shape, bf16),
        in_specs=[smem, vmem, vmem],
        out_specs=vmem,
        scratch_shapes=[pltpu.VMEM((targets, tile, width), f32)],
        compiler_params=params(8),
        name="far",
    )(order, *held(sources, factors))


def near_body(lists, own, first, second, blocks, angle, out, cosine, sine, boxes_all, rows):
    cosine[...] = jnp.cos(angle[...])
    sine[...] = jnp.sin(angle[...])
    boxes, excite, k = own.shape
    slots = lists.shape[0]
    shard = lax.axis_index("shard")
    base = (lax.axis_index("space") * lax.axis_size("shard") + shard) * boxes
    even = lax.rem(shard, 2) == 0
    above = jnp.where(even, 0, boxes)
    below = jnp.where(even, 3 * boxes, 2 * boxes)
    boxes_all[0:boxes] = own[...]
    boxes_all[boxes : 2 * boxes] = first[...]
    boxes_all[2 * boxes : 3 * boxes] = second[...]
    for b in range(boxes):
        for s in range(slots):
            away = lists[s, b] - base
            spot = away + jnp.where(away < 0, below, jnp.where(away < boxes, 0, above))
            rows[b * excite : (b + 1) * excite, s * k : (s + 1) * k] = boxes_all[spot]
    out[...] = dot(rows[...], blocks[...]).reshape(out.shape)


def near_force(lists, own, first, second, blocks, angle):
    boxes, excite, k = own.shape
    slots = lists.shape[0]
    smem = pl.BlockSpec(memory_space=pltpu.SMEM)
    vmem = pl.BlockSpec(memory_space=pltpu.VMEM)
    return pl.pallas_call(
        near_body,
        out_shape=(pltpu.VMEM((boxes, excite, k), f32),) + (pltpu.VMEM(angle.shape, f32),) * 2,
        in_specs=[smem] + [vmem] * 5,
        out_specs=(vmem,) * 3,
        scratch_shapes=[
            pltpu.VMEM((3 * boxes, excite, k), bf16),
            pltpu.VMEM((boxes * excite, slots * k), bf16),
        ],
        compiler_params=params(6), name="near",
    )(lists, *held(own, first, second, blocks.reshape(slots * k, k), angle))


def down_body(pieces, near, radiate, interp, cosine, sine, out, shifted, *, groups, slices):
    _, _, width = pieces.shape
    boxes, excite, both = out.shape
    unknowns = both // 2
    group = excite // groups
    tile = 2 * group
    parents = boxes // CHILDREN
    for h in range(slices):
        lanes = slice(h * width, (h + 1) * width)
        for s in range(0, groups, 2):
            pair = [pieces[(s + k) * slices + h].astype(f32) for k in range(2)]
            for p in range(parents):
                incoming = jnp.concatenate([v[p * tile : (p + 1) * tile] for v in pair], axis=0)
                turned = half_turn(incoming.reshape(2, tile, width)).reshape(2 * tile, width)
                for child in range(CHILDREN):
                    row = ((p * CHILDREN + child) * groups + s) * tile
                    value = cosine[child : child + 1, lanes] * incoming - sine[child : child + 1, lanes] * turned
                    shifted[row : row + 2 * tile, lanes] = value.astype(bf16)
    leaf_in = dot_t(shifted[...], interp[...]).astype(bf16)
    back = dot_t(leaf_in, radiate[...]).reshape(boxes, groups, tile, both)
    own = back[..., :unknowns] - half_turn(back[..., unknowns:])
    for b in range(boxes):
        parts = [
            jnp.concatenate([own[b, s, t * group : (t + 1) * group] for s in range(groups)], axis=0)
            for t in range(2)
        ]
        out[b] = jnp.concatenate(parts, axis=1) + near[b]


def down(pieces, near, radiate, interp, cosine, sine, groups, slices):
    boxes, excite, _ = near.shape
    return pl.pallas_call(
        lambda *refs: down_body(*refs, groups=groups, slices=slices),
        out_shape=jax.ShapeDtypeStruct(near.shape, f32),
        scratch_shapes=[pltpu.VMEM((boxes * excite * 2, interp.shape[1]), bf16)],
        compiler_params=params(16), name="down",
    )(*held(pieces, near, radiate, interp, cosine, sine))


def is_even(axis):
    return lax.rem(lax.axis_index(axis), 2) == 0


def coefficients(kinds, table, base):
    mats = table.shape[0] // 2
    diagonal = jnp.full(kinds.shape, 6.0, f32)
    loss = jnp.zeros(kinds.shape, f32)
    for k in range(mats):
        present = kinds == k + base
        diagonal = jnp.where(present, 6.0 + table[k : k + 1, :], diagonal)
        loss = jnp.where(present, table[mats + k : mats + k + 1, :], loss)
    a = relaxation / diagonal
    if base > 0:
        a = jnp.where(kinds < base, 0.0, a)
    return a, a * loss


def along_z(v):
    lanes = v.shape[-1]
    lane = lax.broadcasted_iota(jnp.int32, v.shape, v.ndim - 1)
    lower = jnp.where(lane == 0, 0.0, pltpu.roll(v, 1, v.ndim - 1))
    upper = jnp.where(lane == lanes - 1, 0.0, pltpu.roll(v, lanes - 1, v.ndim - 1))
    return lower + upper


def along_y(tiles, low, high):
    row = lax.broadcasted_iota(jnp.int32, tiles[0].shape, 0)
    lower = [low] + [pltpu.roll(t, 1, 0) for t in tiles]
    upper = [pltpu.roll(t, 7, 0) for t in tiles] + [high]
    return [
        jnp.where(row == 0, lower[i], lower[i + 1]) + jnp.where(row == 7, upper[i + 1], upper[i])
        for i in range(len(tiles))
    ]


def relaxed(v, total, a, b):
    keep = 1.0 - relaxation
    return (
        keep * v[0] + a * total[0] + b * v[1],
        keep * v[1] + a * total[1] - b * v[0],
    )


def tiles_of(value):
    return [value[i : i + 8] for i in range(0, value.shape[0], 8)]


def tiles_at(ref, at, rows):
    return [ref[i : i + 8, :] for i in range(at, at + rows, 8)]


def sweep_brick(values, e, excite, cx, cy, source, beside, a, b, emit):
    for x in range(cx):
        sums = []
        for p in range(2):
            at = (p * excite + e) * cx + x
            edge = [jnp.broadcast_to(beside[side, at : at + 1, :], (8, source.shape[1])) for side in range(2)]
            here = values[p][x + 1]
            total = [n + along_z(t) + y for n, t, y in zip(tiles_at(source, at * cy, cy), here, along_y(here, *edge))]
            for other in (values[p][x], values[p][x + 2]):
                if other is not None:
                    total = [n + t for n, t in zip(total, other)]
            sums.append(total)
        new = []
        for i in range(cy // 8):
            rows = slice(x * cy + i * 8, x * cy + i * 8 + 8)
            new.append(
                relaxed((values[0][x + 1][i], values[1][x + 1][i]), (sums[0][i], sums[1][i]), a[rows, :], b[rows, :])
            )
        for p in range(2):
            emit(p, x, [pair[p] for pair in new])


def below_above(axis, first, second):
    even = is_even(axis)

    def pick(one, two):
        def rows(at, size):
            return jnp.where(even, one[at : at + size, :].astype(f32), two[at : at + size, :].astype(f32))

        return rows

    return pick(second, first), pick(first, second)


def edge_body(
    real_table, loss_table, field, source, kinds, first, second, table, layers, kind_rows, mat_real, mat_loss,
    sem, kind_sem, table_sem
):
    total, cy, nz = field.shape
    cx = kinds.shape[0]
    even = is_even("shard")
    faces = ((cy - 2, cy - 1), (1, 0))
    copies = [
        pltpu.make_async_copy(real_table, mat_real, table_sem.at[0]),
        pltpu.make_async_copy(loss_table, mat_loss, table_sem.at[1]),
    ]
    for i, (inner, outer) in enumerate(faces):
        for k, (ref, y) in enumerate(((field, inner), (field, outer), (source, outer))):
            copies.append(pltpu.make_async_copy(ref.at[:, y], layers.at[i, k], sem.at[i, k]))
        for k in range(2):
            copies.append(
                pltpu.make_async_copy(kinds.at[:, outer], kind_rows.at[i, pl.ds(k * cx, cx)], kind_sem.at[i, k])
            )
    for copy in copies:
        copy.start()
    for copy in copies:
        copy.wait()
    for k in range(mat_real.shape[0]):
        table[k : k + 1, :] = jnp.full((1, nz), mat_real[k], f32)
        table[mat_real.shape[0] + k : mat_real.shape[0] + k + 1, :] = jnp.full((1, nz), mat_loss[k], f32)
    row = lax.broadcasted_iota(jnp.int32, (8, nz), 0) & (cx - 1)
    for i in range(2):
        a, b = coefficients(kind_rows[i], table, 0)
        for j in range(0, total // 2, 8):
            v, sums = [], []
            for part in range(2):
                rows = slice(part * (total // 2) + j, part * (total // 2) + j + 8)
                here = layers[i, 1, rows, :]
                n = layers[i, 0, rows, :] + layers[i, 2, rows, :] + along_z(here)
                n = n + jnp.where(row == 0, 0.0, pltpu.roll(here, 1, 0))
                n = n + jnp.where(row == cx - 1, 0.0, pltpu.roll(here, 7, 0))
                v.append(here)
                sums.append(n)
            new = relaxed(v, sums, a, b)
            for part in range(2):
                layers[i, 2, part * (total // 2) + j : part * (total // 2) + j + 8, :] = new[part]
    for place, k in ((0, 1), (1, 2)):
        rows = slice(place * total, (place + 1) * total)
        first[rows, :] = jnp.where(even, layers[0, k], layers[1, k]).astype(bf16)
        second[rows, :] = jnp.where(even, layers[1, k], layers[0, k]).astype(bf16)
    kind = [jnp.concatenate([kind_rows[i].astype(f32) + 1.0] * 2, axis=0) for i in range(2)]
    first[2 * total :, :] = jnp.where(even, kind[0], kind[1]).astype(bf16)
    second[2 * total :, :] = jnp.where(even, kind[1], kind[0]).astype(bf16)


def edges(mat_real, mat_loss, field, source, kinds):
    total, _, nz = field.shape
    assert 2 * kinds.shape[0] == 8
    message = pltpu.VMEM((2 * total + 16, nz), bf16)
    anywhere = pl.BlockSpec(memory_space=pl.ANY)
    return pl.pallas_call(
        edge_body,
        out_shape=(message, message, pltpu.VMEM((2 * mat_real.shape[0], nz), f32)),
        in_specs=[anywhere] * 5,
        scratch_shapes=[
            pltpu.VMEM((2, 3, total, nz), f32),
            pltpu.VMEM((2, 8, nz), jnp.int32),
            pltpu.SMEM(mat_real.shape, f32),
            pltpu.SMEM(mat_loss.shape, f32),
            pltpu.SemaphoreType.DMA((2, 3)),
            pltpu.SemaphoreType.DMA((2, 2)),
            pltpu.SemaphoreType.DMA((2,)),
        ],
        compiler_params=params(6),
        name="edges",
    )(*left(mat_real, mat_loss, field, source, kinds))


def first_body(
    table, field, source, kinds, got_first, got_second,
    sweep, columns, column_a, to_first, to_second, near, a_all, b_all, *, cx, cy
):
    total = field.shape[0] // cy
    channels = total // cx
    excite = channels // 2
    a_all[...], b_all[...] = coefficients(kinds[...], table, 0)

    for side, (halo, own_y) in enumerate(zip(below_above("shard", got_first, got_second), (0, cy - 1))):
        kind = halo(2 * total, 16)[0:8].astype(jnp.int32)
        col_a = coefficients(kind, table, 1)[0]
        column_a[side] = col_a
        near[side] = halo(0, total)
        for j in range(0, total, 16):
            part = halo(total + j, 16)
            for k in (0, 8):
                own = field[pl.ds((j + k) * cy + own_y, 8, stride=cy), :]
                columns[side, j + k : j + k + 8] = part[k : k + 8] + col_a * own
    for e in range(excite):
        values = [
            [None] + [tiles_at(field, ((p * excite + e) * cx + x) * cy, cy) for x in range(cx)] + [None]
            for p in range(2)
        ]

        def emit(p, x, new, e=e):
            at = ((p * excite + e) * cx + x) * cy
            sweep[at : at + cy, :] = jnp.concatenate(new, axis=0)

        sweep_brick(values, e, excite, cx, cy, source, near, a_all, b_all, emit)
    even_x = is_even("space")
    plane = channels * cy
    for message, x in ((to_first, jnp.where(even_x, cx - 1, 0)), (to_second, jnp.where(even_x, 0, cx - 1))):
        for c in range(channels):
            rows = pl.ds(pl.multiple_of((c * cx + x) * cy, cy), cy)
            message[c * cy : (c + 1) * cy, :] = field[rows, :].astype(bf16)
            message[plane + c * cy : plane + (c + 1) * cy, :] = sweep[rows, :].astype(bf16)
        for side in range(2):
            corner = jnp.concatenate(
                [near.at[side][pl.ds(c * cx + x, 8, stride=cx), :] for c in range(0, channels, 8)], axis=0
            )
            at = 2 * plane + side * channels
            message[at : at + channels, :] = corner.astype(bf16)
        kind = kinds[pl.ds(pl.multiple_of(x * cy, cy), cy), :].astype(f32) + 1.0
        message[2 * plane + 2 * channels :, :] = kind.astype(bf16)


def first_sweep(table, field, source, kinds, got_first, got_second, cx, cy):
    total, nz = field.shape[0] // cy, field.shape[1]
    channels = total // cx
    vmem = pl.BlockSpec(memory_space=pltpu.VMEM)
    message = pltpu.VMEM((2 * channels * cy + 2 * channels + cy, nz), bf16)
    return pl.pallas_call(
        lambda *refs: first_body(*refs, cx=cx, cy=cy),
        out_shape=(
            pltpu.VMEM(field.shape, f32),
            pltpu.VMEM((2, total, nz), f32),
            pltpu.VMEM((2, 8, nz), f32),
            message,
            message,
        ),
        in_specs=[vmem] * 6,
        out_specs=(vmem,) * 5,
        scratch_shapes=[pltpu.VMEM((2, total, nz), f32)] + [pltpu.VMEM((cx * cy, nz), f32)] * 2,
        compiler_params=params(8),
        name="first_sweep",
    )(*held(table, field, source, kinds, got_first, got_second))


def steps(
    volume_field,
    source,
    material,
    mat_real,
    mat_loss,
    surface_map,
    near_boxes,
    near_blocks,
    radiate,
    interp,
    phase_angle,
    far_parents,
    far_kind,
    translate,
):
    every = ("space", "shard")
    groups = lax.axis_size("space")
    slices = lax.axis_size("shard")
    _, cells_x, cells_y, cells_z = volume_field.shape[1:]
    cosine, sine, chosen, depth = prepare(phase_angle, surface_map, cells_x, cells_y, cells_z)
    weights = radiate.reshape(2 * radiate.shape[1], radiate.shape[2])
    field = volume_field.reshape(-1, cells_z)
    flat_source = source.reshape(-1, cells_z)
    kinds = material.reshape(-1, cells_z)
    bricks = (-1, cells_y, cells_z)
    *to_y, table = edges(mat_real, mat_loss, volume_field.reshape(bricks), source.reshape(bricks), material)
    got_y = swap(*to_y, "shard")
    sweep, columns, column_a, *to_x = first_sweep(
        table, field, flat_source, kinds, *got_y, cells_x, cells_y
    )
    got_x = swap(*to_x, "space")
    current, currents, pieces = up(
        (table, field, sweep, columns, column_a, flat_source, kinds, *got_x),
        chosen,
        depth,
        near_boxes.shape[0],
        weights,
        interp,
        cosine,
        sine,
        cells_x,
        cells_y,
        groups,
        slices,
    )
    directed = lax.all_to_all(pieces, every, split_axis=0, concat_axis=0, tiled=True)
    first, second = swap(currents, currents, "shard")
    factors, order = tables(far_parents.T, far_kind.T, translate)
    combined = far_combine(order, directed, factors, far_parents.shape[0])
    incoming = lax.all_to_all(combined, every, split_axis=0, concat_axis=0, tiled=True)
    near, cosine, sine = near_force(near_boxes.T, currents, first, second, near_blocks, phase_angle)
    forcing = down(incoming, near, weights, interp, cosine, sine, groups, slices)
    return (current.reshape(volume_field.shape), forcing)


def solution(mesh):
    return jax.shard_map(
        steps,
        mesh=mesh,
        in_specs=(
            P(None, None, "space", "shard", None),
            P(None, None, "space", "shard", None),
            P("space", "shard", None),
            P(),
            P(),
            P(("space", "shard"), None),
            P(("space", "shard"), None),
            P(),
            P(),
            P(),
            P(),
            P(),
            P(),
            P(None, None, "shard"),
        ),
        out_specs=(P(None, None, "space", "shard", None), P(("space", "shard"), None, None)),
        check_vma=False,
    )
```

```python
import jax
import jax.numpy as jnp
from jax import lax
from jax.experimental import pallas as pl
from jax.experimental.pallas import tpu as pltpu
from jax.sharding import PartitionSpec as P


relaxation = 0.8
f32 = jnp.float32
bf16 = jnp.bfloat16
CHILDREN = 8


def held(*arrays):
    return [pltpu.with_memory_space_constraint(a, pltpu.VMEM) for a in arrays]


def left(*arrays):
    return [pltpu.with_memory_space_constraint(a, pltpu.HBM) for a in arrays]


def params(mib):
    return pltpu.CompilerParams(vmem_limit_bytes=mib << 20)


def dot(a, b):
    return jnp.dot(a, b, preferred_element_type=f32)


def dot_t(a, b):
    return lax.dot_general(a, b, (((1,), (1,)), ((), ())), preferred_element_type=f32)


def half_turn(v):
    half = v.shape[-2] // 2
    rows = lax.broadcasted_iota(jnp.int32, v.shape, v.ndim - 2)
    swapped = pltpu.roll(v, half, v.ndim - 2)
    return jnp.where(rows < half, -swapped, swapped)


def log2(n):
    assert n & (n - 1) == 0
    return n.bit_length() - 1


def prepare(angle, smap, cx, cy, nz):
    boxes, unknowns = smap.shape

    def body(angle, smap, cosine, sine, chosen, depth):
        cosine[...] = jnp.cos(angle[...])
        sine[...] = jnp.sin(angle[...])
        level = lax.broadcasted_iota(jnp.int32, (nz, unknowns), 0)
        for b in range(boxes):
            key = smap[b : b + 1, :]
            key_z = key & (nz - 1)
            key_x = key >> (log2(nz) + log2(cy))
            lanes = slice(b * unknowns, (b + 1) * unknowns)
            for x in range(cx):
                hit = level == jnp.where(key_x == x, key_z, -1)
                chosen[x * nz : (x + 1) * nz, lanes] = jnp.where(hit, 1.0, 0.0).astype(bf16)
            depth[:, lanes] = jnp.broadcast_to((key >> log2(nz)) & (cy - 1), (8, unknowns))

    shape = pltpu.VMEM(angle.shape, f32)
    return pl.pallas_call(
        body,
        out_shape=(
            shape,
            shape,
            pltpu.VMEM((cx * nz, boxes * unknowns), bf16),
            pltpu.VMEM((8, boxes * unknowns), jnp.int32),
        ),
        compiler_params=params(6),
        name="prepare",
    )(*held(angle, smap))


def swap_pairs(n, first):
    pairs = []
    for i in range(first, n - 1, 2):
        pairs += [(i, i + 1), (i + 1, i)]
    return pairs


def swap(for_even, for_odd, axis):
    n = lax.axis_size(axis)
    received = []
    for k, value in enumerate((for_even, for_odd)):
        received.append(lax.ppermute(value, axis, swap_pairs(n, k)))
    return received


def second_sweep(
    table, field, sweep, columns, column_a, source, kinds, early_first, early_second, late_first, late_second,
    out, beside, a_all, b_all, store, cx, cy
):
    total = field.shape[0] // cy
    channels = total // cx
    excite = channels // 2
    plane = channels * cy
    a_all[...], b_all[...] = coefficients(kinds[...], table, 0)
    early = below_above("space", early_first, early_second)
    late = below_above("space", late_first, late_second)
    ends = (0, cx - 1)
    for y_side in range(2):
        beside[y_side] = columns[y_side]
        for x_side, x in enumerate(ends):
            corner = late[x_side](plane + y_side * channels, channels)
            factor = column_a[y_side, x : x + 1, :]
            for c in range(0, channels, 8):
                rows = pl.ds(c * cx + x, 8, stride=cx)
                beside.at[y_side][rows, :] = beside.at[y_side][rows, :] + factor * corner[c : c + 8]
    face_a = [
        coefficients(early[side](plane, cy).astype(jnp.int32), table, 1)[0]
        for side in range(2)
    ]
    for e in range(excite):
        values = []
        for p in range(2):
            c = p * excite + e
            own = [tiles_at(sweep, (c * cx + x) * cy, cy) for x in range(cx)]
            outer = []
            for side, x in enumerate(ends):
                raw = tiles_of(early[side](c * cy, cy))
                factors = tiles_at(a_all, x * cy, cy)
                own[x] = [t + f * h for t, f, h in zip(own[x], factors, raw)]
                part = tiles_of(late[side](c * cy, cy))
                before = tiles_at(field, (c * cx + x) * cy, cy)
                outer.append([q + f * t for q, f, t in zip(part, tiles_of(face_a[side]), before)])
            values.append([outer[0]] + own + [outer[1]])

        def emit(p, x, new, e=e):
            at = ((p * excite + e) * cx + x) * cy
            whole = jnp.concatenate(new, axis=0)
            out[at : at + cy, :] = whole
            store(p * excite + e, x, whole)

        sweep_brick(values, e, excite, cx, cy, source, beside, a_all, b_all, emit)


def gather_rows(parts):
    row = lax.broadcasted_iota(jnp.int32, parts[0].shape, 0)
    upper = row < 4
    fours = [
        jnp.where(upper, parts[r], parts[r + 4]) + pltpu.roll(jnp.where(upper, parts[r + 4], parts[r]), 4, 0)
        for r in range(4)
    ]
    second = (row & 2) == 0
    twos = [
        jnp.where(second, fours[r] + pltpu.roll(fours[r], 6, 0), fours[r + 2] + pltpu.roll(fours[r + 2], 2, 0))
        for r in range(2)
    ]
    first = (row & 1) == 0
    return jnp.where(first, twos[0] + pltpu.roll(twos[0], 7, 0), twos[1] + pltpu.roll(twos[1], 1, 0))


def up_body(
    table, field, sweep, columns, column_a, source, kinds, early_first, early_second, late_first, late_second,
    chosen, depth, radiate, interp, cosine, sine, volume, cur, out,
    beside, cells, rows, fresh, a_all, b_all, sent, sem, sent_sem, *, cx, cy, groups, slices
):
    nz = field.shape[1]
    channels = field.shape[0] // (cx * cy)
    excite = channels // 2
    group = excite // groups
    assert 2 * group == 8 and cy % 8 == 0
    boxes = cur.shape[0]
    unknowns = depth.shape[1] // boxes

    def store(c, x, value):
        cells[c * cy : (c + 1) * cy, x * nz : (x + 1) * nz] = value.astype(bf16)

    second_sweep(
        table, field, sweep, columns, column_a, source, kinds, early_first, early_second, late_first, late_second,
        fresh, beside, a_all, b_all, store, cx, cy
    )
    leaving = pltpu.make_async_copy(fresh, volume, sem)
    leaving.start()
    moves = [leaving]
    pair = 2
    for b in range(0, boxes, pair):
        lanes = slice(b * unknowns, (b + pair) * unknowns)
        picked = dot(cells[...], chosen[:, lanes])
        key_y = depth[:, lanes]
        row = lax.broadcasted_iota(jnp.int32, key_y.shape, 0)
        hits = [key_y == row + y for y in range(0, cy, 8)]
        found = []
        for s in range(groups):
            parts = []
            for r in range(2 * group):
                c = (r // group) * excite + s * group + r % group
                kept = jnp.zeros(key_y.shape, f32)
                for i, hit in enumerate(hits):
                    kept = jnp.where(hit, picked[c * cy + i * 8 : c * cy + i * 8 + 8], kept)
                parts.append(kept)
            found.append(gather_rows(parts))
        found = jnp.concatenate(found, axis=0)
        for j in range(pair):
            own = found[:, j * unknowns : (j + 1) * unknowns].reshape(groups, 2 * group, unknowns)
            turned = half_turn(own)
            both = jnp.concatenate([own, turned], axis=2).reshape(channels, 2 * unknowns)
            rows[(b + j) * channels : (b + j + 1) * channels, :] = both.astype(bf16)
            parts = [
                jnp.concatenate([own[s, t * group : (t + 1) * group] for s in range(groups)], axis=0)
                for t in range(2)
            ]
            cur[b + j] = jnp.concatenate(parts, axis=1).astype(bf16)
    leaf = dot(rows[...], radiate[...]).astype(bf16)
    directions = interp.shape[1]
    width = directions // slices
    tile = max(width, 256)
    parents = boxes // CHILDREN
    for n in range(0, directions, tile):
        spread = dot(leaf, interp[:, n : n + tile]).reshape(parents, CHILDREN, groups, 2 * group, tile)
        along = jnp.zeros((parents, groups, 2 * group, tile), f32)
        across = jnp.zeros((parents, groups, 2 * group, tile), f32)
        for child in range(CHILDREN):
            along = along + cosine[child : child + 1, n : n + tile] * spread[:, child]
            across = across + sine[child : child + 1, n : n + tile] * spread[:, child]
        whole = (along + half_turn(across)).astype(bf16)
        for s in range(groups):
            piece = jnp.concatenate([whole[p, s] for p in range(parents)], axis=0)
            for k in range(tile // width):
                sent[s, n // width + k] = piece[:, k * width : (k + 1) * width]
        some = pl.ds(n // width, tile // width)
        moves.append(pltpu.make_async_copy(sent.at[:, some], out.at[:, some], sent_sem.at[n // tile]))
        moves[-1].start()
    for move in moves:
        move.wait()


def up(volume_args, chosen, depth, boxes, radiate, interp, cosine, sine, cx, cy, groups, slices):
    field = volume_args[1]
    nz = field.shape[1]
    total = field.shape[0] // cy
    channels = total // cx
    unknowns = depth.shape[1] // boxes
    width = interp.shape[1] // slices
    piece_rows = boxes // CHILDREN * (channels // groups)
    vmem = pl.BlockSpec(memory_space=pltpu.VMEM)
    hbm = pl.BlockSpec(memory_space=pltpu.HBM)
    return pl.pallas_call(
        lambda *refs: up_body(*refs, cx=cx, cy=cy, groups=groups, slices=slices),
        out_shape=(
            pltpu.HBM(field.shape, f32),
            pltpu.VMEM((boxes, channels // 2, 2 * unknowns), bf16),
            pltpu.HBM((groups, slices, piece_rows, width), bf16),
        ),
        in_specs=[vmem] * 17,
        out_specs=(hbm, vmem, hbm),
        scratch_shapes=[
            pltpu.VMEM((2, total, nz), f32),
            pltpu.VMEM((channels * cy, cx * nz), bf16),
            pltpu.VMEM((boxes * channels, 2 * unknowns), bf16),
            pltpu.VMEM(field.shape, f32),
            pltpu.VMEM((cx * cy, nz), f32),
            pltpu.VMEM((cx * cy, nz), f32),
            pltpu.VMEM((groups, slices, piece_rows, width), bf16),
            pltpu.SemaphoreType.DMA(()),
            pltpu.SemaphoreType.DMA((interp.shape[1] // max(width, 256),)),
        ],
        compiler_params=params(16), name="up",
    )(*held(*volume_args, chosen, depth, radiate, interp, cosine, sine))


def tables(lists, kinds, translate):
    far, targets = lists.shape

    def body(lists, kinds, translate, factors, order):
        def one(t, _):
            for f in range(far):
                order[t * far + f] = lists[f, t]
                factors[t * far + f] = translate[kinds[f, t]]
            return 0

        lax.fori_loop(0, targets, one, 0, unroll=2)

    smem = pl.BlockSpec(memory_space=pltpu.SMEM)
    vmem = pl.BlockSpec(memory_space=pltpu.VMEM)
    return pl.pallas_call(
        body,
        out_shape=(
            pltpu.VMEM((targets * far,) + translate.shape[1:], f32),
            jax.ShapeDtypeStruct((targets * far,), jnp.int32),
        ),
        in_specs=[smem, smem, vmem],
        out_specs=(vmem, smem),
        compiler_params=params(8),
        name="tables",
    )(lists, kinds, *held(translate))


def far_body(order, sources, factors, out, plain, sent, sem, *, targets):
    devices, piece_rows, width = sources.shape
    far = order.shape[0] // targets
    per = targets // devices
    tile = piece_rows // per
    plain[...] = sources[...].astype(f32).reshape(targets, tile, width)

    def one(d, _):
        results = []
        for j in range(per):
            along = jnp.zeros((tile, width), f32)
            across = jnp.zeros((tile, width), f32)
            for f in range(far):
                pair = d * (per * far) + (j * far + f)
                source = plain[order[pair]]
                factor = factors[pair]
                along = along + factor[0:1] * source
                across = across + factor[1:2] * source
            results.append(along + half_turn(across))
        sent[d] = jnp.concatenate(results, axis=0).astype(bf16)
        return 0

    parts = sem.shape[0]
    moves = []
    for part in range(parts):
        first = part * (devices // parts)
        lax.fori_loop(first, first + devices // parts, one, 0, unroll=4)
        some = pl.ds(first, devices // parts)
        moves.append(pltpu.make_async_copy(sent.at[some], out.at[some], sem.at[part]))
        moves[-1].start()
    for move in moves:
        move.wait()


def far_combine(order, sources, factors, targets):
    devices, piece_rows, width = sources.shape
    tile = piece_rows // (targets // devices)
    smem = pl.BlockSpec(memory_space=pltpu.SMEM)
    vmem = pl.BlockSpec(memory_space=pltpu.VMEM)
    return pl.pallas_call(
        lambda *refs: far_body(*refs, targets=targets),
        out_shape=pltpu.HBM(sources.shape, bf16),
        in_specs=[smem, vmem, vmem],
        out_specs=pl.BlockSpec(memory_space=pltpu.HBM),
        scratch_shapes=[
            pltpu.VMEM((targets, tile, width), f32),
            pltpu.VMEM(sources.shape, bf16),
            pltpu.SemaphoreType.DMA((4,)),
        ],
        compiler_params=params(8),
        name="far",
    )(order, *held(sources, factors))


def near_body(lists, own, first, second, blocks, angle, out, cosine, sine, boxes_all, rows):
    cosine[...] = jnp.cos(angle[...])
    sine[...] = jnp.sin(angle[...])
    boxes, excite, k = own.shape
    slots = lists.shape[0]
    shard = lax.axis_index("shard")
    base = (lax.axis_index("space") * lax.axis_size("shard") + shard) * boxes
    even = lax.rem(shard, 2) == 0
    above = jnp.where(even, 0, boxes)
    below = jnp.where(even, 3 * boxes, 2 * boxes)
    boxes_all[0:boxes] = own[...]
    boxes_all[boxes : 2 * boxes] = first[...]
    boxes_all[2 * boxes : 3 * boxes] = second[...]
    for b in range(boxes):
        for s in range(slots):
            away = lists[s, b] - base
            spot = away + jnp.where(away < 0, below, jnp.where(away < boxes, 0, above))
            rows[b * excite : (b + 1) * excite, s * k : (s + 1) * k] = boxes_all[spot]
    out[...] = dot(rows[...], blocks[...]).reshape(out.shape)


def near_force(lists, own, first, second, blocks, angle):
    boxes, excite, k = own.shape
    slots = lists.shape[0]
    smem = pl.BlockSpec(memory_space=pltpu.SMEM)
    vmem = pl.BlockSpec(memory_space=pltpu.VMEM)
    return pl.pallas_call(
        near_body,
        out_shape=(pltpu.VMEM((boxes, excite, k), f32),) + (pltpu.VMEM(angle.shape, f32),) * 2,
        in_specs=[smem] + [vmem] * 5,
        out_specs=(vmem,) * 3,
        scratch_shapes=[
            pltpu.VMEM((3 * boxes, excite, k), bf16),
            pltpu.VMEM((boxes * excite, slots * k), bf16),
        ],
        compiler_params=params(6), name="near",
    )(lists, *held(own, first, second, blocks.reshape(slots * k, k), angle))


def down_body(pieces, near, radiate, interp, cosine, sine, out, shifted, sent, sem, *, groups, slices):
    _, _, width = pieces.shape
    boxes, excite, both = out.shape
    unknowns = both // 2
    group = excite // groups
    tile = 2 * group
    parents = boxes // CHILDREN
    for h in range(slices):
        lanes = slice(h * width, (h + 1) * width)
        for s in range(0, groups, 2):
            pair = [pieces[(s + k) * slices + h].astype(f32) for k in range(2)]
            for p in range(parents):
                incoming = jnp.concatenate([v[p * tile : (p + 1) * tile] for v in pair], axis=0)
                turned = half_turn(incoming.reshape(2, tile, width)).reshape(2 * tile, width)
                for child in range(CHILDREN):
                    row = ((p * CHILDREN + child) * groups + s) * tile
                    value = cosine[child : child + 1, lanes] * incoming - sine[child : child + 1, lanes] * turned
                    shifted[row : row + 2 * tile, lanes] = value.astype(bf16)
    leaf_in = dot_t(shifted[...], interp[...]).astype(bf16)
    parts = sem.shape[0]
    count = boxes // parts
    box_rows = groups * tile
    moves = []
    for part in range(parts):
        first = part * count
        some = leaf_in[first * box_rows : (first + count) * box_rows]
        back = dot_t(some, radiate[...]).reshape(count, groups, tile, both)
        own = back[..., :unknowns] - half_turn(back[..., unknowns:])
        for b in range(count):
            halves = [
                jnp.concatenate([own[b, s, t * group : (t + 1) * group] for s in range(groups)], axis=0)
                for t in range(2)
            ]
            sent[first + b] = jnp.concatenate(halves, axis=1) + near[first + b]
        some = pl.ds(first, count)
        moves.append(pltpu.make_async_copy(sent.at[some], out.at[some], sem.at[part]))
        moves[-1].start()
    for move in moves:
        move.wait()


def down(pieces, near, radiate, interp, cosine, sine, groups, slices):
    boxes, excite, _ = near.shape
    vmem = pl.BlockSpec(memory_space=pltpu.VMEM)
    return pl.pallas_call(
        lambda *refs: down_body(*refs, groups=groups, slices=slices),
        out_shape=pltpu.HBM(near.shape, f32),
        in_specs=[vmem] * 6,
        out_specs=pl.BlockSpec(memory_space=pltpu.HBM),
        scratch_shapes=[
            pltpu.VMEM((boxes * excite * 2, interp.shape[1]), bf16),
            pltpu.VMEM(near.shape, f32),
            pltpu.SemaphoreType.DMA((4,)),
        ],
        compiler_params=params(16),
        name="down",
    )(*held(pieces, near, radiate, interp, cosine, sine))


def is_even(axis):
    return lax.rem(lax.axis_index(axis), 2) == 0


def coefficients(kinds, table, base):
    mats = table.shape[0] // 2
    diagonal = jnp.full(kinds.shape, 6.0, f32)
    loss = jnp.zeros(kinds.shape, f32)
    for k in range(mats):
        present = kinds == k + base
        diagonal = jnp.where(present, 6.0 + table[k : k + 1, :], diagonal)
        loss = jnp.where(present, table[mats + k : mats + k + 1, :], loss)
    a = relaxation / diagonal
    if base > 0:
        a = jnp.where(kinds < base, 0.0, a)
    return a, a * loss


def along_z(v):
    lanes = v.shape[-1]
    lane = lax.broadcasted_iota(jnp.int32, v.shape, v.ndim - 1)
    lower = jnp.where(lane == 0, 0.0, pltpu.roll(v, 1, v.ndim - 1))
    upper = jnp.where(lane == lanes - 1, 0.0, pltpu.roll(v, lanes - 1, v.ndim - 1))
    return lower + upper


def along_y(tiles, low, high):
    row = lax.broadcasted_iota(jnp.int32, tiles[0].shape, 0)
    lower = [low] + [pltpu.roll(t, 1, 0) for t in tiles]
    upper = [pltpu.roll(t, 7, 0) for t in tiles] + [high]
    return [
        jnp.where(row == 0, lower[i], lower[i + 1]) + jnp.where(row == 7, upper[i + 1], upper[i])
        for i in range(len(tiles))
    ]


def relaxed(v, total, a, b):
    keep = 1.0 - relaxation
    return (
        keep * v[0] + a * total[0] + b * v[1],
        keep * v[1] + a * total[1] - b * v[0],
    )


def tiles_of(value):
    return [value[i : i + 8] for i in range(0, value.shape[0], 8)]


def tiles_at(ref, at, rows):
    return [ref[i : i + 8, :] for i in range(at, at + rows, 8)]


def sweep_brick(values, e, excite, cx, cy, source, beside, a, b, emit):
    for x in range(cx):
        sums = []
        for p in range(2):
            at = (p * excite + e) * cx + x
            edge = [jnp.broadcast_to(beside[side, at : at + 1, :], (8, source.shape[1])) for side in range(2)]
            here = values[p][x + 1]
            total = [n + along_z(t) + y for n, t, y in zip(tiles_at(source, at * cy, cy), here, along_y(here, *edge))]
            for other in (values[p][x], values[p][x + 2]):
                if other is not None:
                    total = [n + t for n, t in zip(total, other)]
            sums.append(total)
        new = []
        for i in range(cy // 8):
            rows = slice(x * cy + i * 8, x * cy + i * 8 + 8)
            new.append(
                relaxed((values[0][x + 1][i], values[1][x + 1][i]), (sums[0][i], sums[1][i]), a[rows, :], b[rows, :])
            )
        for p in range(2):
            emit(p, x, [pair[p] for pair in new])


def below_above(axis, first, second):
    even = is_even(axis)

    def pick(one, two):
        def rows(at, size):
            return jnp.where(even, one[at : at + size, :].astype(f32), two[at : at + size, :].astype(f32))

        return rows

    return pick(second, first), pick(first, second)


def edge_body(
    real_table, loss_table, field, source, kinds, first, second, table, layers, kind_rows, mat_real, mat_loss,
    sem, kind_sem, table_sem
):
    total, cy, nz = field.shape
    cx = kinds.shape[0]
    even = is_even("shard")
    faces = ((cy - 2, cy - 1), (1, 0))
    copies = [
        pltpu.make_async_copy(real_table, mat_real, table_sem.at[0]),
        pltpu.make_async_copy(loss_table, mat_loss, table_sem.at[1]),
    ]
    for i, (inner, outer) in enumerate(faces):
        for k, (ref, y) in enumerate(((field, inner), (field, outer), (source, outer))):
            copies.append(pltpu.make_async_copy(ref.at[:, y], layers.at[i, k], sem.at[i, k]))
        for k in range(2):
            copies.append(
                pltpu.make_async_copy(kinds.at[:, outer], kind_rows.at[i, pl.ds(k * cx, cx)], kind_sem.at[i, k])
            )
    for copy in copies:
        copy.start()
    for copy in copies:
        copy.wait()
    for k in range(mat_real.shape[0]):
        table[k : k + 1, :] = jnp.full((1, nz), mat_real[k], f32)
        table[mat_real.shape[0] + k : mat_real.shape[0] + k + 1, :] = jnp.full((1, nz), mat_loss[k], f32)
    row = lax.broadcasted_iota(jnp.int32, (8, nz), 0) & (cx - 1)
    for i in range(2):
        a, b = coefficients(kind_rows[i], table, 0)
        for j in range(0, total // 2, 8):
            v, sums = [], []
            for part in range(2):
                rows = slice(part * (total // 2) + j, part * (total // 2) + j + 8)
                here = layers[i, 1, rows, :]
                n = layers[i, 0, rows, :] + layers[i, 2, rows, :] + along_z(here)
                n = n + jnp.where(row == 0, 0.0, pltpu.roll(here, 1, 0))
                n = n + jnp.where(row == cx - 1, 0.0, pltpu.roll(here, 7, 0))
                v.append(here)
                sums.append(n)
            new = relaxed(v, sums, a, b)
            for part in range(2):
                layers[i, 2, part * (total // 2) + j : part * (total // 2) + j + 8, :] = new[part]
    for place, k in ((0, 1), (1, 2)):
        rows = slice(place * total, (place + 1) * total)
        first[rows, :] = jnp.where(even, layers[0, k], layers[1, k]).astype(bf16)
        second[rows, :] = jnp.where(even, layers[1, k], layers[0, k]).astype(bf16)
    kind = [jnp.concatenate([kind_rows[i].astype(f32) + 1.0] * 2, axis=0) for i in range(2)]
    first[2 * total :, :] = jnp.where(even, kind[0], kind[1]).astype(bf16)
    second[2 * total :, :] = jnp.where(even, kind[1], kind[0]).astype(bf16)


def edges(mat_real, mat_loss, field, source, kinds):
    total, _, nz = field.shape
    assert 2 * kinds.shape[0] == 8
    message = pltpu.VMEM((2 * total + 16, nz), bf16)
    anywhere = pl.BlockSpec(memory_space=pl.ANY)
    return pl.pallas_call(
        edge_body,
        out_shape=(message, message, pltpu.VMEM((2 * mat_real.shape[0], nz), f32)),
        in_specs=[anywhere] * 5,
        scratch_shapes=[
            pltpu.VMEM((2, 3, total, nz), f32),
            pltpu.VMEM((2, 8, nz), jnp.int32),
            pltpu.SMEM(mat_real.shape, f32),
            pltpu.SMEM(mat_loss.shape, f32),
            pltpu.SemaphoreType.DMA((2, 3)),
            pltpu.SemaphoreType.DMA((2, 2)),
            pltpu.SemaphoreType.DMA((2,)),
        ],
        compiler_params=params(6),
        name="edges",
    )(*left(mat_real, mat_loss, field, source, kinds))


def faces(field, kinds, cx, cy):
    channels = field.shape[0] // (cx * cy)

    def body(field, kinds, first, second):
        even = is_even("space")
        for message, x in ((first, jnp.where(even, cx - 1, 0)), (second, jnp.where(even, 0, cx - 1))):
            for c in range(channels):
                rows = pl.ds(pl.multiple_of((c * cx + x) * cy, cy), cy)
                message[c * cy : (c + 1) * cy, :] = field[rows, :].astype(bf16)
            kind = kinds[pl.ds(pl.multiple_of(x * cy, cy), cy), :].astype(f32) + 1.0
            message[channels * cy :, :] = kind.astype(bf16)

    message = pltpu.VMEM((channels * cy + cy, field.shape[1]), bf16)
    return pl.pallas_call(body, out_shape=(message, message), compiler_params=params(6), name="faces")(
        *held(field, kinds)
    )


def first_body(
    table, field, source, kinds, got_first, got_second,
    sweep, columns, column_a, to_first, to_second, near, a_all, b_all, *, cx, cy
):
    total = field.shape[0] // cy
    channels = total // cx
    excite = channels // 2
    a_all[...], b_all[...] = coefficients(kinds[...], table, 0)

    for side, (halo, own_y) in enumerate(zip(below_above("shard", got_first, got_second), (0, cy - 1))):
        kind = halo(2 * total, 16)[0:8].astype(jnp.int32)
        col_a = coefficients(kind, table, 1)[0]
        column_a[side] = col_a
        near[side] = halo(0, total)
        for j in range(0, total, 16):
            part = halo(total + j, 16)
            for k in (0, 8):
                own = field[pl.ds((j + k) * cy + own_y, 8, stride=cy), :]
                columns[side, j + k : j + k + 8] = part[k : k + 8] + col_a * own
    for e in range(excite):
        values = [
            [None] + [tiles_at(field, ((p * excite + e) * cx + x) * cy, cy) for x in range(cx)] + [None]
            for p in range(2)
        ]

        def emit(p, x, new, e=e):
            at = ((p * excite + e) * cx + x) * cy
            sweep[at : at + cy, :] = jnp.concatenate(new, axis=0)

        sweep_brick(values, e, excite, cx, cy, source, near, a_all, b_all, emit)
    even_x = is_even("space")
    plane = channels * cy
    for message, x in ((to_first, jnp.where(even_x, cx - 1, 0)), (to_second, jnp.where(even_x, 0, cx - 1))):
        for c in range(channels):
            rows = pl.ds(pl.multiple_of((c * cx + x) * cy, cy), cy)
            message[c * cy : (c + 1) * cy, :] = sweep[rows, :].astype(bf16)
        for side in range(2):
            corner = jnp.concatenate(
                [near.at[side][pl.ds(c * cx + x, 8, stride=cx), :] for c in range(0, channels, 8)], axis=0
            )
            at = plane + side * channels
            message[at : at + channels, :] = corner.astype(bf16)


def first_sweep(table, field, source, kinds, got_first, got_second, cx, cy):
    total, nz = field.shape[0] // cy, field.shape[1]
    channels = total // cx
    vmem = pl.BlockSpec(memory_space=pltpu.VMEM)
    message = pltpu.VMEM((channels * cy + 2 * channels, nz), bf16)
    return pl.pallas_call(
        lambda *refs: first_body(*refs, cx=cx, cy=cy),
        out_shape=(
            pltpu.VMEM(field.shape, f32),
            pltpu.VMEM((2, total, nz), f32),
            pltpu.VMEM((2, 8, nz), f32),
            message,
            message,
        ),
        in_specs=[vmem] * 6,
        out_specs=(vmem,) * 5,
        scratch_shapes=[pltpu.VMEM((2, total, nz), f32)] + [pltpu.VMEM((cx * cy, nz), f32)] * 2,
        compiler_params=params(8),
        name="first_sweep",
    )(*held(table, field, source, kinds, got_first, got_second))


def steps(
    volume_field,
    source,
    material,
    mat_real,
    mat_loss,
    surface_map,
    near_boxes,
    near_blocks,
    radiate,
    interp,
    phase_angle,
    far_parents,
    far_kind,
    translate,
):
    every = ("space", "shard")
    groups = lax.axis_size("space")
    slices = lax.axis_size("shard")
    _, cells_x, cells_y, cells_z = volume_field.shape[1:]
    cosine, sine, chosen, depth = prepare(phase_angle, surface_map, cells_x, cells_y, cells_z)
    weights = radiate.reshape(2 * radiate.shape[1], radiate.shape[2])
    field = volume_field.reshape(-1, cells_z)
    flat_source = source.reshape(-1, cells_z)
    kinds = material.reshape(-1, cells_z)
    bricks = (-1, cells_y, cells_z)
    *to_y, table = edges(mat_real, mat_loss, volume_field.reshape(bricks), source.reshape(bricks), material)
    field, flat_source, interp, kinds, *to_y = lax.optimization_barrier((field, flat_source, interp, kinds, *to_y))
    got_y = swap(*to_y, "shard")
    got_early = swap(*faces(field, kinds, cells_x, cells_y), "space")
    sweep, columns, column_a, *to_x = first_sweep(
        table, field, flat_source, kinds, *got_y, cells_x, cells_y
    )
    got_late = swap(*to_x, "space")
    current, currents, pieces = up(
        (table, field, sweep, columns, column_a, flat_source, kinds, *got_early, *got_late),
        chosen,
        depth,
        near_boxes.shape[0],
        weights,
        interp,
        cosine,
        sine,
        cells_x,
        cells_y,
        groups,
        slices,
    )
    directed = lax.all_to_all(pieces.reshape((groups * slices,) + pieces.shape[2:]), every, split_axis=0, concat_axis=0, tiled=True)
    first, second = swap(currents, currents, "shard")
    factors, order = tables(far_parents.T, far_kind.T, translate)
    combined = far_combine(order, directed, factors, far_parents.shape[0])
    incoming = lax.all_to_all(combined, every, split_axis=0, concat_axis=0, tiled=True)
    near, cosine, sine = near_force(near_boxes.T, currents, first, second, near_blocks, phase_angle)
    forcing = down(incoming, near, weights, interp, cosine, sine, groups, slices)
    return (current.reshape(volume_field.shape), forcing)


def solution(mesh):
    return jax.shard_map(
        steps,
        mesh=mesh,
        in_specs=(
            P(None, None, "space", "shard", None),
            P(None, None, "space", "shard", None),
            P("space", "shard", None),
            P(),
            P(),
            P(("space", "shard"), None),
            P(("space", "shard"), None),
            P(),
            P(),
            P(),
            P(),
            P(),
            P(),
            P(None, None, "shard"),
        ),
        out_specs=(P(None, None, "space", "shard", None), P(("space", "shard"), None, None)),
        check_vma=False,
    )
```

```python
import jax
import jax.numpy as jnp
from jax import lax
from jax.experimental import pallas as pl
from jax.experimental.pallas import tpu as pltpu
from jax.sharding import PartitionSpec as P


relaxation = 0.8
f32 = jnp.float32
bf16 = jnp.bfloat16
CHILDREN = 8


def held(*arrays):
    return [pltpu.with_memory_space_constraint(a, pltpu.VMEM) for a in arrays]


def left(*arrays):
    return [pltpu.with_memory_space_constraint(a, pltpu.HBM) for a in arrays]


def params(mib):
    return pltpu.CompilerParams(vmem_limit_bytes=mib << 20)


def dot(a, b):
    return jnp.dot(a, b, preferred_element_type=f32)


def dot_t(a, b):
    return lax.dot_general(a, b, (((1,), (1,)), ((), ())), preferred_element_type=f32)


def half_turn(v):
    half = v.shape[-2] // 2
    rows = lax.broadcasted_iota(jnp.int32, v.shape, v.ndim - 2)
    swapped = pltpu.roll(v, half, v.ndim - 2)
    return jnp.where(rows < half, -swapped, swapped)


def log2(n):
    assert n & (n - 1) == 0
    return n.bit_length() - 1


def prepare(angle, smap, cx, cy, nz):
    boxes, unknowns = smap.shape

    def body(angle, smap, cosine, sine, chosen, depth):
        cosine[...] = jnp.cos(angle[...])
        sine[...] = jnp.sin(angle[...])
        level = lax.broadcasted_iota(jnp.int32, (nz, unknowns), 0)
        for b in range(boxes):
            key = smap[b : b + 1, :]
            key_z = key & (nz - 1)
            key_x = key >> (log2(nz) + log2(cy))
            lanes = slice(b * unknowns, (b + 1) * unknowns)
            for x in range(cx):
                hit = level == jnp.where(key_x == x, key_z, -1)
                chosen[x * nz : (x + 1) * nz, lanes] = jnp.where(hit, 1.0, 0.0).astype(bf16)
            depth[:, lanes] = jnp.broadcast_to((key >> log2(nz)) & (cy - 1), (8, unknowns))

    shape = pltpu.VMEM(angle.shape, f32)
    return pl.pallas_call(
        body,
        out_shape=(
            shape,
            shape,
            pltpu.VMEM((cx * nz, boxes * unknowns), bf16),
            pltpu.VMEM((8, boxes * unknowns), jnp.int32),
        ),
        compiler_params=params(6),
        name="prepare",
    )(*held(angle, smap))


def swap_pairs(n, first):
    pairs = []
    for i in range(first, n - 1, 2):
        pairs += [(i, i + 1), (i + 1, i)]
    return pairs


def swap(for_even, for_odd, axis):
    n = lax.axis_size(axis)
    received = []
    for k, value in enumerate((for_even, for_odd)):
        received.append(lax.ppermute(value, axis, swap_pairs(n, k)))
    return received


def second_sweep(
    table, field, sweep, columns, column_a, source, kinds, early_first, early_second, late_first, late_second,
    out, beside, a_all, b_all, store, cx, cy
):
    total = field.shape[0] // cy
    channels = total // cx
    excite = channels // 2
    plane = channels * cy
    a_all[...], b_all[...] = coefficients(kinds[...], table, 0)
    early = below_above("space", early_first, early_second)
    late = below_above("space", late_first, late_second)
    ends = (0, cx - 1)
    for y_side in range(2):
        beside[y_side] = columns[y_side]
        for x_side, x in enumerate(ends):
            corner = late[x_side](plane + y_side * channels, channels)
            factor = column_a[y_side, x : x + 1, :]
            for c in range(0, channels, 8):
                rows = pl.ds(c * cx + x, 8, stride=cx)
                beside.at[y_side][rows, :] = beside.at[y_side][rows, :] + factor * corner[c : c + 8]
    face_a = [
        coefficients(early[side](plane, cy).astype(jnp.int32), table, 1)[0]
        for side in range(2)
    ]
    for e in range(excite):
        values = []
        for p in range(2):
            c = p * excite + e
            own = [tiles_at(sweep, (c * cx + x) * cy, cy) for x in range(cx)]
            outer = []
            for side, x in enumerate(ends):
                raw = tiles_of(early[side](c * cy, cy))
                factors = tiles_at(a_all, x * cy, cy)
                own[x] = [t + f * h for t, f, h in zip(own[x], factors, raw)]
                part = tiles_of(late[side](c * cy, cy))
                before = tiles_at(field, (c * cx + x) * cy, cy)
                outer.append([q + f * t for q, f, t in zip(part, tiles_of(face_a[side]), before)])
            values.append([outer[0]] + own + [outer[1]])

        def emit(p, x, new, e=e):
            at = ((p * excite + e) * cx + x) * cy
            whole = jnp.concatenate(new, axis=0)
            out[at : at + cy, :] = whole
            store(p * excite + e, x, whole)

        sweep_brick(values, e, excite, cx, cy, source, beside, a_all, b_all, emit)


def gather_rows(parts):
    row = lax.broadcasted_iota(jnp.int32, parts[0].shape, 0)
    upper = row < 4
    fours = [
        jnp.where(upper, parts[r], parts[r + 4]) + pltpu.roll(jnp.where(upper, parts[r + 4], parts[r]), 4, 0)
        for r in range(4)
    ]
    second = (row & 2) == 0
    twos = [
        jnp.where(second, fours[r] + pltpu.roll(fours[r], 6, 0), fours[r + 2] + pltpu.roll(fours[r + 2], 2, 0))
        for r in range(2)
    ]
    first = (row & 1) == 0
    return jnp.where(first, twos[0] + pltpu.roll(twos[0], 7, 0), twos[1] + pltpu.roll(twos[1], 1, 0))


def up_body(
    table, field, sweep, columns, column_a, source, kinds, early_first, early_second, late_first, late_second,
    chosen, depth, radiate, interp, cosine, sine, volume, cur, out,
    beside, cells, rows, fresh, a_all, b_all, sent, sem, sent_sem, *, cx, cy, groups, slices
):
    nz = field.shape[1]
    channels = field.shape[0] // (cx * cy)
    excite = channels // 2
    group = excite // groups
    assert 2 * group == 8 and cy % 8 == 0
    boxes = cur.shape[0]
    unknowns = depth.shape[1] // boxes

    def store(c, x, value):
        cells[c * cy : (c + 1) * cy, x * nz : (x + 1) * nz] = value.astype(bf16)

    second_sweep(
        table, field, sweep, columns, column_a, source, kinds, early_first, early_second, late_first, late_second,
        fresh, beside, a_all, b_all, store, cx, cy
    )
    leaving = pltpu.make_async_copy(fresh, volume, sem)
    leaving.start()
    moves = [leaving]
    pair = 2
    for b in range(0, boxes, pair):
        lanes = slice(b * unknowns, (b + pair) * unknowns)
        picked = dot(cells[...], chosen[:, lanes])
        key_y = depth[:, lanes]
        row = lax.broadcasted_iota(jnp.int32, key_y.shape, 0)
        hits = [key_y == row + y for y in range(0, cy, 8)]
        found = []
        for s in range(groups):
            parts = []
            for r in range(2 * group):
                c = (r // group) * excite + s * group + r % group
                kept = jnp.zeros(key_y.shape, f32)
                for i, hit in enumerate(hits):
                    kept = jnp.where(hit, picked[c * cy + i * 8 : c * cy + i * 8 + 8], kept)
                parts.append(kept)
            found.append(gather_rows(parts))
        found = jnp.concatenate(found, axis=0)
        for j in range(pair):
            own = found[:, j * unknowns : (j + 1) * unknowns].reshape(groups, 2 * group, unknowns)
            turned = half_turn(own)
            both = jnp.concatenate([own, turned], axis=2).reshape(channels, 2 * unknowns)
            rows[(b + j) * channels : (b + j + 1) * channels, :] = both.astype(bf16)
            parts = [
                jnp.concatenate([own[s, t * group : (t + 1) * group] for s in range(groups)], axis=0)
                for t in range(2)
            ]
            cur[b + j] = jnp.concatenate(parts, axis=1).astype(bf16)
    leaf = dot(rows[...], radiate[...]).astype(bf16)
    directions = interp.shape[1]
    width = directions // slices
    tile = max(width, 256)
    parents = boxes // CHILDREN
    for n in range(0, directions, tile):
        spread = dot(leaf, interp[:, n : n + tile]).reshape(parents, CHILDREN, groups, 2 * group, tile)
        along = jnp.zeros((parents, groups, 2 * group, tile), f32)
        across = jnp.zeros((parents, groups, 2 * group, tile), f32)
        for child in range(CHILDREN):
            along = along + cosine[child : child + 1, n : n + tile] * spread[:, child]
            across = across + sine[child : child + 1, n : n + tile] * spread[:, child]
        whole = (along + half_turn(across)).astype(bf16)
        for s in range(groups):
            piece = jnp.concatenate([whole[p, s] for p in range(parents)], axis=0)
            for k in range(tile // width):
                out[s, n // width + k] = piece[:, k * width : (k + 1) * width]
    for move in moves:
        move.wait()


def up(volume_args, chosen, depth, boxes, radiate, interp, cosine, sine, cx, cy, groups, slices):
    field = volume_args[1]
    nz = field.shape[1]
    total = field.shape[0] // cy
    channels = total // cx
    unknowns = depth.shape[1] // boxes
    width = interp.shape[1] // slices
    piece_rows = boxes // CHILDREN * (channels // groups)
    vmem = pl.BlockSpec(memory_space=pltpu.VMEM)
    hbm = pl.BlockSpec(memory_space=pltpu.HBM)
    return pl.pallas_call(
        lambda *refs: up_body(*refs, cx=cx, cy=cy, groups=groups, slices=slices),
        out_shape=(
            pltpu.HBM(field.shape, f32),
            pltpu.VMEM((boxes, channels // 2, 2 * unknowns), bf16),
            pltpu.HBM((groups, slices, piece_rows, width), bf16),
        ),
        in_specs=[vmem] * 17,
        out_specs=(hbm, vmem, vmem),
        scratch_shapes=[
            pltpu.VMEM((2, total, nz), f32),
            pltpu.VMEM((channels * cy, cx * nz), bf16),
            pltpu.VMEM((boxes * channels, 2 * unknowns), bf16),
            pltpu.VMEM(field.shape, f32),
            pltpu.VMEM((cx * cy, nz), f32),
            pltpu.VMEM((cx * cy, nz), f32),
            pltpu.VMEM((groups, slices, piece_rows, width), bf16),
            pltpu.SemaphoreType.DMA(()),
            pltpu.SemaphoreType.DMA((interp.shape[1] // max(width, 256),)),
        ],
        compiler_params=params(16), name="up",
    )(*held(*volume_args, chosen, depth, radiate, interp, cosine, sine))


def tables(lists, kinds, translate):
    far, targets = lists.shape

    def body(lists, kinds, translate, factors, order):
        def one(t, _):
            for f in range(far):
                order[t * far + f] = lists[f, t]
                factors[t * far + f] = translate[kinds[f, t]]
            return 0

        lax.fori_loop(0, targets, one, 0, unroll=2)

    smem = pl.BlockSpec(memory_space=pltpu.SMEM)
    vmem = pl.BlockSpec(memory_space=pltpu.VMEM)
    return pl.pallas_call(
        body,
        out_shape=(
            pltpu.VMEM((targets * far,) + translate.shape[1:], f32),
            jax.ShapeDtypeStruct((targets * far,), jnp.int32),
        ),
        in_specs=[smem, smem, vmem],
        out_specs=(vmem, smem),
        compiler_params=params(8),
        name="tables",
    )(lists, kinds, *held(translate))


def far_body(order, sources, factors, out, plain, sent, sem, *, targets):
    devices, piece_rows, width = sources.shape
    far = order.shape[0] // targets
    per = targets // devices
    tile = piece_rows // per
    plain[...] = sources[...].astype(f32).reshape(targets, tile, width)

    def one(d, _):
        results = []
        for j in range(per):
            along = jnp.zeros((tile, width), f32)
            across = jnp.zeros((tile, width), f32)
            for f in range(far):
                pair = d * (per * far) + (j * far + f)
                source = plain[order[pair]]
                factor = factors[pair]
                along = along + factor[0:1] * source
                across = across + factor[1:2] * source
            results.append(along + half_turn(across))
        sent[d] = jnp.concatenate(results, axis=0).astype(bf16)
        return 0

    parts = sem.shape[0]
    moves = []
    for part in range(parts):
        first = part * (devices // parts)
        lax.fori_loop(first, first + devices // parts, one, 0, unroll=4)
        some = pl.ds(first, devices // parts)
        moves.append(pltpu.make_async_copy(sent.at[some], out.at[some], sem.at[part]))
        moves[-1].start()
    for move in moves:
        move.wait()


def far_combine(order, sources, factors, targets):
    devices, piece_rows, width = sources.shape
    tile = piece_rows // (targets // devices)
    smem = pl.BlockSpec(memory_space=pltpu.SMEM)
    vmem = pl.BlockSpec(memory_space=pltpu.VMEM)
    return pl.pallas_call(
        lambda *refs: far_body(*refs, targets=targets),
        out_shape=pltpu.HBM(sources.shape, bf16),
        in_specs=[smem, vmem, vmem],
        out_specs=pl.BlockSpec(memory_space=pltpu.HBM),
        scratch_shapes=[
            pltpu.VMEM((targets, tile, width), f32),
            pltpu.VMEM(sources.shape, bf16),
            pltpu.SemaphoreType.DMA((4,)),
        ],
        compiler_params=params(8),
        name="far",
    )(order, *held(sources, factors))


def near_body(lists, own, first, second, blocks, angle, out, cosine, sine, boxes_all, rows):
    cosine[...] = jnp.cos(angle[...])
    sine[...] = jnp.sin(angle[...])
    boxes, excite, k = own.shape
    slots = lists.shape[0]
    shard = lax.axis_index("shard")
    base = (lax.axis_index("space") * lax.axis_size("shard") + shard) * boxes
    even = lax.rem(shard, 2) == 0
    above = jnp.where(even, 0, boxes)
    below = jnp.where(even, 3 * boxes, 2 * boxes)
    boxes_all[0:boxes] = own[...]
    boxes_all[boxes : 2 * boxes] = first[...]
    boxes_all[2 * boxes : 3 * boxes] = second[...]
    for b in range(boxes):
        for s in range(slots):
            away = lists[s, b] - base
            spot = away + jnp.where(away < 0, below, jnp.where(away < boxes, 0, above))
            rows[b * excite : (b + 1) * excite, s * k : (s + 1) * k] = boxes_all[spot]
    out[...] = dot(rows[...], blocks[...]).reshape(out.shape)


def near_force(lists, own, first, second, blocks, angle):
    boxes, excite, k = own.shape
    slots = lists.shape[0]
    smem = pl.BlockSpec(memory_space=pltpu.SMEM)
    vmem = pl.BlockSpec(memory_space=pltpu.VMEM)
    return pl.pallas_call(
        near_body,
        out_shape=(pltpu.VMEM((boxes, excite, k), f32),) + (pltpu.VMEM(angle.shape, f32),) * 2,
        in_specs=[smem] + [vmem] * 5,
        out_specs=(vmem,) * 3,
        scratch_shapes=[
            pltpu.VMEM((3 * boxes, excite, k), bf16),
            pltpu.VMEM((boxes * excite, slots * k), bf16),
        ],
        compiler_params=params(6), name="near",
    )(lists, *held(own, first, second, blocks.reshape(slots * k, k), angle))


def down_body(pieces, near, radiate, interp, cosine, sine, out, shifted, sent, sem, *, groups, slices):
    _, _, width = pieces.shape
    boxes, excite, both = out.shape
    unknowns = both // 2
    group = excite // groups
    tile = 2 * group
    parents = boxes // CHILDREN
    for h in range(slices):
        lanes = slice(h * width, (h + 1) * width)
        for s in range(0, groups, 2):
            pair = [pieces[(s + k) * slices + h].astype(f32) for k in range(2)]
            for p in range(parents):
                incoming = jnp.concatenate([v[p * tile : (p + 1) * tile] for v in pair], axis=0)
                turned = half_turn(incoming.reshape(2, tile, width)).reshape(2 * tile, width)
                for child in range(CHILDREN):
                    row = ((p * CHILDREN + child) * groups + s) * tile
                    value = cosine[child : child + 1, lanes] * incoming - sine[child : child + 1, lanes] * turned
                    shifted[row : row + 2 * tile, lanes] = value.astype(bf16)
    leaf_in = dot_t(shifted[...], interp[...]).astype(bf16)
    parts = sem.shape[0]
    count = boxes // parts
    box_rows = groups * tile
    moves = []
    for part in range(parts):
        first = part * count
        some = leaf_in[first * box_rows : (first + count) * box_rows]
        back = dot_t(some, radiate[...]).reshape(count, groups, tile, both)
        own = back[..., :unknowns] - half_turn(back[..., unknowns:])
        for b in range(count):
            halves = [
                jnp.concatenate([own[b, s, t * group : (t + 1) * group] for s in range(groups)], axis=0)
                for t in range(2)
            ]
            sent[first + b] = jnp.concatenate(halves, axis=1) + near[first + b]
        some = pl.ds(first, count)
        moves.append(pltpu.make_async_copy(sent.at[some], out.at[some], sem.at[part]))
        moves[-1].start()
    for move in moves:
        move.wait()


def down(pieces, near, radiate, interp, cosine, sine, groups, slices):
    boxes, excite, _ = near.shape
    vmem = pl.BlockSpec(memory_space=pltpu.VMEM)
    return pl.pallas_call(
        lambda *refs: down_body(*refs, groups=groups, slices=slices),
        out_shape=pltpu.HBM(near.shape, f32),
        in_specs=[vmem] * 6,
        out_specs=pl.BlockSpec(memory_space=pltpu.HBM),
        scratch_shapes=[
            pltpu.VMEM((boxes * excite * 2, interp.shape[1]), bf16),
            pltpu.VMEM(near.shape, f32),
            pltpu.SemaphoreType.DMA((4,)),
        ],
        compiler_params=params(16),
        name="down",
    )(*held(pieces, near, radiate, interp, cosine, sine))


def is_even(axis):
    return lax.rem(lax.axis_index(axis), 2) == 0


def coefficients(kinds, table, base):
    mats = table.shape[0] // 2
    diagonal = jnp.full(kinds.shape, 6.0, f32)
    loss = jnp.zeros(kinds.shape, f32)
    for k in range(mats):
        present = kinds == k + base
        diagonal = jnp.where(present, 6.0 + table[k : k + 1, :], diagonal)
        loss = jnp.where(present, table[mats + k : mats + k + 1, :], loss)
    a = relaxation / diagonal
    if base > 0:
        a = jnp.where(kinds < base, 0.0, a)
    return a, a * loss


def along_z(v):
    lanes = v.shape[-1]
    lane = lax.broadcasted_iota(jnp.int32, v.shape, v.ndim - 1)
    lower = jnp.where(lane == 0, 0.0, pltpu.roll(v, 1, v.ndim - 1))
    upper = jnp.where(lane == lanes - 1, 0.0, pltpu.roll(v, lanes - 1, v.ndim - 1))
    return lower + upper


def along_y(tiles, low, high):
    row = lax.broadcasted_iota(jnp.int32, tiles[0].shape, 0)
    lower = [low] + [pltpu.roll(t, 1, 0) for t in tiles]
    upper = [pltpu.roll(t, 7, 0) for t in tiles] + [high]
    return [
        jnp.where(row == 0, lower[i], lower[i + 1]) + jnp.where(row == 7, upper[i + 1], upper[i])
        for i in range(len(tiles))
    ]


def relaxed(v, total, a, b):
    keep = 1.0 - relaxation
    return (
        keep * v[0] + a * total[0] + b * v[1],
        keep * v[1] + a * total[1] - b * v[0],
    )


def tiles_of(value):
    return [value[i : i + 8] for i in range(0, value.shape[0], 8)]


def tiles_at(ref, at, rows):
    return [ref[i : i + 8, :] for i in range(at, at + rows, 8)]


def sweep_brick(values, e, excite, cx, cy, source, beside, a, b, emit):
    for x in range(cx):
        sums = []
        for p in range(2):
            at = (p * excite + e) * cx + x
            edge = [jnp.broadcast_to(beside[side, at : at + 1, :], (8, source.shape[1])) for side in range(2)]
            here = values[p][x + 1]
            total = [n + along_z(t) + y for n, t, y in zip(tiles_at(source, at * cy, cy), here, along_y(here, *edge))]
            for other in (values[p][x], values[p][x + 2]):
                if other is not None:
                    total = [n + t for n, t in zip(total, other)]
            sums.append(total)
        new = []
        for i in range(cy // 8):
            rows = slice(x * cy + i * 8, x * cy + i * 8 + 8)
            new.append(
                relaxed((values[0][x + 1][i], values[1][x + 1][i]), (sums[0][i], sums[1][i]), a[rows, :], b[rows, :])
            )
        for p in range(2):
            emit(p, x, [pair[p] for pair in new])


def below_above(axis, first, second):
    even = is_even(axis)

    def pick(one, two):
        def rows(at, size):
            return jnp.where(even, one[at : at + size, :].astype(f32), two[at : at + size, :].astype(f32))

        return rows

    return pick(second, first), pick(first, second)


def edge_body(
    real_table, loss_table, field, source, kinds, first, second, table, layers, kind_rows, mat_real, mat_loss,
    sem, kind_sem, table_sem
):
    total, cy, nz = field.shape
    cx = kinds.shape[0]
    even = is_even("shard")
    faces = ((cy - 2, cy - 1), (1, 0))
    copies = [
        pltpu.make_async_copy(real_table, mat_real, table_sem.at[0]),
        pltpu.make_async_copy(loss_table, mat_loss, table_sem.at[1]),
    ]
    for i, (inner, outer) in enumerate(faces):
        for k, (ref, y) in enumerate(((field, inner), (field, outer), (source, outer))):
            copies.append(pltpu.make_async_copy(ref.at[:, y], layers.at[i, k], sem.at[i, k]))
        for k in range(2):
            copies.append(
                pltpu.make_async_copy(kinds.at[:, outer], kind_rows.at[i, pl.ds(k * cx, cx)], kind_sem.at[i, k])
            )
    for copy in copies:
        copy.start()
    for copy in copies:
        copy.wait()
    for k in range(mat_real.shape[0]):
        table[k : k + 1, :] = jnp.full((1, nz), mat_real[k], f32)
        table[mat_real.shape[0] + k : mat_real.shape[0] + k + 1, :] = jnp.full((1, nz), mat_loss[k], f32)
    row = lax.broadcasted_iota(jnp.int32, (8, nz), 0) & (cx - 1)
    for i in range(2):
        a, b = coefficients(kind_rows[i], table, 0)
        for j in range(0, total // 2, 8):
            v, sums = [], []
            for part in range(2):
                rows = slice(part * (total // 2) + j, part * (total // 2) + j + 8)
                here = layers[i, 1, rows, :]
                n = layers[i, 0, rows, :] + layers[i, 2, rows, :] + along_z(here)
                n = n + jnp.where(row == 0, 0.0, pltpu.roll(here, 1, 0))
                n = n + jnp.where(row == cx - 1, 0.0, pltpu.roll(here, 7, 0))
                v.append(here)
                sums.append(n)
            new = relaxed(v, sums, a, b)
            for part in range(2):
                layers[i, 2, part * (total // 2) + j : part * (total // 2) + j + 8, :] = new[part]
    for place, k in ((0, 1), (1, 2)):
        rows = slice(place * total, (place + 1) * total)
        first[rows, :] = jnp.where(even, layers[0, k], layers[1, k]).astype(bf16)
        second[rows, :] = jnp.where(even, layers[1, k], layers[0, k]).astype(bf16)
    kind = [jnp.concatenate([kind_rows[i].astype(f32) + 1.0] * 2, axis=0) for i in range(2)]
    first[2 * total :, :] = jnp.where(even, kind[0], kind[1]).astype(bf16)
    second[2 * total :, :] = jnp.where(even, kind[1], kind[0]).astype(bf16)


def edges(mat_real, mat_loss, field, source, kinds):
    total, _, nz = field.shape
    assert 2 * kinds.shape[0] == 8
    message = pltpu.VMEM((2 * total + 16, nz), bf16)
    anywhere = pl.BlockSpec(memory_space=pl.ANY)
    return pl.pallas_call(
        edge_body,
        out_shape=(message, message, pltpu.VMEM((2 * mat_real.shape[0], nz), f32)),
        in_specs=[anywhere] * 5,
        scratch_shapes=[
            pltpu.VMEM((2, 3, total, nz), f32),
            pltpu.VMEM((2, 8, nz), jnp.int32),
            pltpu.SMEM(mat_real.shape, f32),
            pltpu.SMEM(mat_loss.shape, f32),
            pltpu.SemaphoreType.DMA((2, 3)),
            pltpu.SemaphoreType.DMA((2, 2)),
            pltpu.SemaphoreType.DMA((2,)),
        ],
        compiler_params=params(6),
        name="edges",
    )(*left(mat_real, mat_loss, field, source, kinds))


def faces(field, kinds, cx, cy):
    channels = field.shape[0] // (cx * cy)

    def body(field, kinds, first, second):
        even = is_even("space")
        for message, x in ((first, jnp.where(even, cx - 1, 0)), (second, jnp.where(even, 0, cx - 1))):
            for c in range(channels):
                rows = pl.ds(pl.multiple_of((c * cx + x) * cy, cy), cy)
                message[c * cy : (c + 1) * cy, :] = field[rows, :].astype(bf16)
            kind = kinds[pl.ds(pl.multiple_of(x * cy, cy), cy), :].astype(f32) + 1.0
            message[channels * cy :, :] = kind.astype(bf16)

    message = pltpu.VMEM((channels * cy + cy, field.shape[1]), bf16)
    return pl.pallas_call(body, out_shape=(message, message), compiler_params=params(6), name="faces")(
        *held(field, kinds)
    )


def first_body(
    table, field, source, kinds, got_first, got_second,
    sweep, columns, column_a, to_first, to_second, near, a_all, b_all, *, cx, cy
):
    total = field.shape[0] // cy
    channels = total // cx
    excite = channels // 2
    a_all[...], b_all[...] = coefficients(kinds[...], table, 0)

    for side, (halo, own_y) in enumerate(zip(below_above("shard", got_first, got_second), (0, cy - 1))):
        kind = halo(2 * total, 16)[0:8].astype(jnp.int32)
        col_a = coefficients(kind, table, 1)[0]
        column_a[side] = col_a
        near[side] = halo(0, total)
        for j in range(0, total, 16):
            part = halo(total + j, 16)
            for k in (0, 8):
                own = field[pl.ds((j + k) * cy + own_y, 8, stride=cy), :]
                columns[side, j + k : j + k + 8] = part[k : k + 8] + col_a * own
    for e in range(excite):
        values = [
            [None] + [tiles_at(field, ((p * excite + e) * cx + x) * cy, cy) for x in range(cx)] + [None]
            for p in range(2)
        ]

        def emit(p, x, new, e=e):
            at = ((p * excite + e) * cx + x) * cy
            sweep[at : at + cy, :] = jnp.concatenate(new, axis=0)

        sweep_brick(values, e, excite, cx, cy, source, near, a_all, b_all, emit)
    even_x = is_even("space")
    plane = channels * cy
    for message, x in ((to_first, jnp.where(even_x, cx - 1, 0)), (to_second, jnp.where(even_x, 0, cx - 1))):
        for c in range(channels):
            rows = pl.ds(pl.multiple_of((c * cx + x) * cy, cy), cy)
            message[c * cy : (c + 1) * cy, :] = sweep[rows, :].astype(bf16)
        for side in range(2):
            corner = jnp.concatenate(
                [near.at[side][pl.ds(c * cx + x, 8, stride=cx), :] for c in range(0, channels, 8)], axis=0
            )
            at = plane + side * channels
            message[at : at + channels, :] = corner.astype(bf16)


def first_sweep(table, field, source, kinds, got_first, got_second, cx, cy):
    total, nz = field.shape[0] // cy, field.shape[1]
    channels = total // cx
    vmem = pl.BlockSpec(memory_space=pltpu.VMEM)
    message = pltpu.VMEM((channels * cy + 2 * channels, nz), bf16)
    return pl.pallas_call(
        lambda *refs: first_body(*refs, cx=cx, cy=cy),
        out_shape=(
            pltpu.VMEM(field.shape, f32),
            pltpu.VMEM((2, total, nz), f32),
            pltpu.VMEM((2, 8, nz), f32),
            message,
            message,
        ),
        in_specs=[vmem] * 6,
        out_specs=(vmem,) * 5,
        scratch_shapes=[pltpu.VMEM((2, total, nz), f32)] + [pltpu.VMEM((cx * cy, nz), f32)] * 2,
        compiler_params=params(8),
        name="first_sweep",
    )(*held(table, field, source, kinds, got_first, got_second))


def steps(
    volume_field,
    source,
    material,
    mat_real,
    mat_loss,
    surface_map,
    near_boxes,
    near_blocks,
    radiate,
    interp,
    phase_angle,
    far_parents,
    far_kind,
    translate,
):
    every = ("space", "shard")
    groups = lax.axis_size("space")
    slices = lax.axis_size("shard")
    _, cells_x, cells_y, cells_z = volume_field.shape[1:]
    cosine, sine, chosen, depth = prepare(phase_angle, surface_map, cells_x, cells_y, cells_z)
    weights = radiate.reshape(2 * radiate.shape[1], radiate.shape[2])
    field = volume_field.reshape(-1, cells_z)
    flat_source = source.reshape(-1, cells_z)
    kinds = material.reshape(-1, cells_z)
    bricks = (-1, cells_y, cells_z)
    *to_y, table = edges(mat_real, mat_loss, volume_field.reshape(bricks), source.reshape(bricks), material)
    field, flat_source, interp, kinds, *to_y = lax.optimization_barrier((field, flat_source, interp, kinds, *to_y))
    got_y = swap(*to_y, "shard")
    got_early = swap(*faces(field, kinds, cells_x, cells_y), "space")
    sweep, columns, column_a, *to_x = first_sweep(
        table, field, flat_source, kinds, *got_y, cells_x, cells_y
    )
    got_late = swap(*to_x, "space")
    current, currents, pieces = up(
        (table, field, sweep, columns, column_a, flat_source, kinds, *got_early, *got_late),
        chosen,
        depth,
        near_boxes.shape[0],
        weights,
        interp,
        cosine,
        sine,
        cells_x,
        cells_y,
        groups,
        slices,
    )
    directed = lax.all_to_all(pieces.reshape((groups * slices,) + pieces.shape[2:]), every, split_axis=0, concat_axis=0, tiled=True)
    first, second = swap(currents, currents, "shard")
    factors, order = tables(far_parents.T, far_kind.T, translate)
    combined = far_combine(order, directed, factors, far_parents.shape[0])
    incoming = lax.all_to_all(combined, every, split_axis=0, concat_axis=0, tiled=True)
    near, cosine, sine = near_force(near_boxes.T, currents, first, second, near_blocks, phase_angle)
    forcing = down(incoming, near, weights, interp, cosine, sine, groups, slices)
    return (current.reshape(volume_field.shape), forcing)


def solution(mesh):
    return jax.shard_map(
        steps,
        mesh=mesh,
        in_specs=(
            P(None, None, "space", "shard", None),
            P(None, None, "space", "shard", None),
            P("space", "shard", None),
            P(),
            P(),
            P(("space", "shard"), None),
            P(("space", "shard"), None),
            P(),
            P(),
            P(),
            P(),
            P(),
            P(),
            P(None, None, "shard"),
        ),
        out_specs=(P(None, None, "space", "shard", None), P(("space", "shard"), None, None)),
        check_vma=False,
    )
```

```python
import jax
import jax.numpy as jnp
from jax import lax
from jax.experimental import pallas as pl
from jax.experimental.pallas import tpu as pltpu
from jax.sharding import PartitionSpec as P


relaxation = 0.8
f32 = jnp.float32
bf16 = jnp.bfloat16
CHILDREN = 8


def held(*arrays):
    return [pltpu.with_memory_space_constraint(a, pltpu.VMEM) for a in arrays]


def left(*arrays):
    return [pltpu.with_memory_space_constraint(a, pltpu.HBM) for a in arrays]


def params(mib):
    return pltpu.CompilerParams(vmem_limit_bytes=mib << 20)


def dot(a, b):
    return jnp.dot(a, b, preferred_element_type=f32)


def dot_t(a, b):
    return lax.dot_general(a, b, (((1,), (1,)), ((), ())), preferred_element_type=f32)


def half_turn(v):
    half = v.shape[-2] // 2
    rows = lax.broadcasted_iota(jnp.int32, v.shape, v.ndim - 2)
    swapped = pltpu.roll(v, half, v.ndim - 2)
    return jnp.where(rows < half, -swapped, swapped)


def log2(n):
    assert n & (n - 1) == 0
    return n.bit_length() - 1


def prepare(angle, smap, cx, cy, nz):
    boxes, unknowns = smap.shape

    def body(angle, smap, cosine, sine, chosen, depth):
        cosine[...] = jnp.cos(angle[...])
        sine[...] = jnp.sin(angle[...])
        level = lax.broadcasted_iota(jnp.int32, (nz, unknowns), 0)
        for b in range(boxes):
            key = smap[b : b + 1, :]
            key_z = key & (nz - 1)
            key_x = key >> (log2(nz) + log2(cy))
            lanes = slice(b * unknowns, (b + 1) * unknowns)
            for x in range(cx):
                hit = level == jnp.where(key_x == x, key_z, -1)
                chosen[x * nz : (x + 1) * nz, lanes] = jnp.where(hit, 1.0, 0.0).astype(bf16)
            depth[:, lanes] = jnp.broadcast_to((key >> log2(nz)) & (cy - 1), (8, unknowns))

    shape = pltpu.VMEM(angle.shape, f32)
    return pl.pallas_call(
        body,
        out_shape=(
            shape,
            shape,
            pltpu.VMEM((cx * nz, boxes * unknowns), bf16),
            pltpu.VMEM((8, boxes * unknowns), jnp.int32),
        ),
        compiler_params=params(6),
        name="prepare",
    )(*held(angle, smap))


def swap_pairs(n, first):
    pairs = []
    for i in range(first, n - 1, 2):
        pairs += [(i, i + 1), (i + 1, i)]
    return pairs


def swap(for_even, for_odd, axis):
    n = lax.axis_size(axis)
    received = []
    for k, value in enumerate((for_even, for_odd)):
        received.append(lax.ppermute(value, axis, swap_pairs(n, k)))
    return received


def second_sweep(
    table, field, sweep, columns, column_a, source, kinds, early_first, early_second, late_first, late_second,
    out, beside, a_all, b_all, store, cx, cy
):
    total = field.shape[0] // cy
    channels = total // cx
    excite = channels // 2
    plane = channels * cy
    a_all[...], b_all[...] = coefficients(kinds[...], table, 0)
    early = below_above("space", early_first, early_second)
    late = below_above("space", late_first, late_second)
    ends = (0, cx - 1)
    for y_side in range(2):
        beside[y_side] = columns[y_side]
        for x_side, x in enumerate(ends):
            corner = late[x_side](plane + y_side * channels, channels)
            factor = column_a[y_side, x : x + 1, :]
            for c in range(0, channels, 8):
                rows = pl.ds(c * cx + x, 8, stride=cx)
                beside.at[y_side][rows, :] = beside.at[y_side][rows, :] + factor * corner[c : c + 8]
    face_a = [
        coefficients(early[side](plane, cy).astype(jnp.int32), table, 1)[0]
        for side in range(2)
    ]
    for e in range(excite):
        values = []
        for p in range(2):
            c = p * excite + e
            own = [tiles_at(sweep, (c * cx + x) * cy, cy) for x in range(cx)]
            outer = []
            for side, x in enumerate(ends):
                raw = tiles_of(early[side](c * cy, cy))
                factors = tiles_at(a_all, x * cy, cy)
                own[x] = [t + f * h for t, f, h in zip(own[x], factors, raw)]
                part = tiles_of(late[side](c * cy, cy))
                before = tiles_at(field, (c * cx + x) * cy, cy)
                outer.append([q + f * t for q, f, t in zip(part, tiles_of(face_a[side]), before)])
            values.append([outer[0]] + own + [outer[1]])

        def emit(p, x, new, e=e):
            at = ((p * excite + e) * cx + x) * cy
            whole = jnp.concatenate(new, axis=0)
            out[at : at + cy, :] = whole
            store(p * excite + e, x, whole)

        sweep_brick(values, e, excite, cx, cy, source, beside, a_all, b_all, emit)


def gather_rows(parts):
    row = lax.broadcasted_iota(jnp.int32, parts[0].shape, 0)
    upper = row < 4
    fours = [
        jnp.where(upper, parts[r], parts[r + 4]) + pltpu.roll(jnp.where(upper, parts[r + 4], parts[r]), 4, 0)
        for r in range(4)
    ]
    second = (row & 2) == 0
    twos = [
        jnp.where(second, fours[r] + pltpu.roll(fours[r], 6, 0), fours[r + 2] + pltpu.roll(fours[r + 2], 2, 0))
        for r in range(2)
    ]
    first = (row & 1) == 0
    return jnp.where(first, twos[0] + pltpu.roll(twos[0], 7, 0), twos[1] + pltpu.roll(twos[1], 1, 0))


def up_body(
    table, field, sweep, columns, column_a, source, kinds, early_first, early_second, late_first, late_second,
    chosen, depth, radiate, interp, cosine, sine, volume, cur, out,
    beside, cells, rows, fresh, a_all, b_all, sent, sem, sent_sem, *, cx, cy, groups, slices
):
    nz = field.shape[1]
    channels = field.shape[0] // (cx * cy)
    excite = channels // 2
    group = excite // groups
    assert 2 * group == 8 and cy % 8 == 0
    boxes = cur.shape[0]
    unknowns = depth.shape[1] // boxes

    def store(c, x, value):
        cells[c * cy : (c + 1) * cy, x * nz : (x + 1) * nz] = value.astype(bf16)

    second_sweep(
        table, field, sweep, columns, column_a, source, kinds, early_first, early_second, late_first, late_second,
        fresh, beside, a_all, b_all, store, cx, cy
    )
    leaving = pltpu.make_async_copy(fresh, volume, sem)
    leaving.start()
    moves = [leaving]
    pair = 2
    for b in range(0, boxes, pair):
        lanes = slice(b * unknowns, (b + pair) * unknowns)
        picked = dot(cells[...], chosen[:, lanes])
        key_y = depth[:, lanes]
        row = lax.broadcasted_iota(jnp.int32, key_y.shape, 0)
        hits = [key_y == row + y for y in range(0, cy, 8)]
        found = []
        for s in range(groups):
            parts = []
            for r in range(2 * group):
                c = (r // group) * excite + s * group + r % group
                kept = jnp.zeros(key_y.shape, f32)
                for i, hit in enumerate(hits):
                    kept = jnp.where(hit, picked[c * cy + i * 8 : c * cy + i * 8 + 8], kept)
                parts.append(kept)
            found.append(gather_rows(parts))
        found = jnp.concatenate(found, axis=0)
        for j in range(pair):
            own = found[:, j * unknowns : (j + 1) * unknowns].reshape(groups, 2 * group, unknowns)
            turned = half_turn(own)
            both = jnp.concatenate([own, turned], axis=2).reshape(channels, 2 * unknowns)
            rows[(b + j) * channels : (b + j + 1) * channels, :] = both.astype(bf16)
            parts = [
                jnp.concatenate([own[s, t * group : (t + 1) * group] for s in range(groups)], axis=0)
                for t in range(2)
            ]
            cur[b + j] = jnp.concatenate(parts, axis=1).astype(bf16)
    leaf = dot(rows[...], radiate[...]).astype(bf16)
    directions = interp.shape[1]
    width = directions // slices
    tile = max(width, 256)
    parents = boxes // CHILDREN
    for n in range(0, directions, tile):
        spread = dot(leaf, interp[:, n : n + tile]).reshape(parents, CHILDREN, groups, 2 * group, tile)
        along = jnp.zeros((parents, groups, 2 * group, tile), f32)
        across = jnp.zeros((parents, groups, 2 * group, tile), f32)
        for child in range(CHILDREN):
            along = along + cosine[child : child + 1, n : n + tile] * spread[:, child]
            across = across + sine[child : child + 1, n : n + tile] * spread[:, child]
        whole = (along + half_turn(across)).astype(bf16)
        for s in range(groups):
            piece = jnp.concatenate([whole[p, s] for p in range(parents)], axis=0)
            for k in range(tile // width):
                out[s, n // width + k] = piece[:, k * width : (k + 1) * width]
    for move in moves:
        move.wait()


def up(volume_args, chosen, depth, boxes, radiate, interp, cosine, sine, cx, cy, groups, slices):
    field = volume_args[1]
    nz = field.shape[1]
    total = field.shape[0] // cy
    channels = total // cx
    unknowns = depth.shape[1] // boxes
    width = interp.shape[1] // slices
    piece_rows = boxes // CHILDREN * (channels // groups)
    vmem = pl.BlockSpec(memory_space=pltpu.VMEM)
    hbm = pl.BlockSpec(memory_space=pltpu.HBM)
    return pl.pallas_call(
        lambda *refs: up_body(*refs, cx=cx, cy=cy, groups=groups, slices=slices),
        out_shape=(
            pltpu.HBM(field.shape, f32),
            pltpu.HBM((boxes, channels // 2, 2 * unknowns), bf16),
            pltpu.HBM((groups, slices, piece_rows, width), bf16),
        ),
        in_specs=[vmem] * 17,
        out_specs=(hbm, vmem, vmem),
        scratch_shapes=[
            pltpu.VMEM((2, total, nz), f32),
            pltpu.VMEM((channels * cy, cx * nz), bf16),
            pltpu.VMEM((boxes * channels, 2 * unknowns), bf16),
            pltpu.VMEM(field.shape, f32),
            pltpu.VMEM((cx * cy, nz), f32),
            pltpu.VMEM((cx * cy, nz), f32),
            pltpu.VMEM((groups, slices, piece_rows, width), bf16),
            pltpu.SemaphoreType.DMA(()),
            pltpu.SemaphoreType.DMA((interp.shape[1] // max(width, 256),)),
        ],
        compiler_params=params(16), name="up",
    )(*held(*volume_args, chosen, depth, radiate, interp, cosine, sine))


def tables(lists, kinds, translate):
    far, targets = lists.shape

    def body(lists, kinds, translate, factors, order):
        def one(t, _):
            for f in range(far):
                order[t * far + f] = lists[f, t]
                factors[t * far + f] = translate[kinds[f, t]]
            return 0

        lax.fori_loop(0, targets, one, 0, unroll=2)

    smem = pl.BlockSpec(memory_space=pltpu.SMEM)
    vmem = pl.BlockSpec(memory_space=pltpu.VMEM)
    return pl.pallas_call(
        body,
        out_shape=(
            pltpu.VMEM((targets * far,) + translate.shape[1:], f32),
            jax.ShapeDtypeStruct((targets * far,), jnp.int32),
        ),
        in_specs=[smem, smem, vmem],
        out_specs=(vmem, smem),
        compiler_params=params(8),
        name="tables",
    )(lists, kinds, *held(translate))


def far_body(order, sources, factors, out, plain, sent, sem, *, targets):
    devices, piece_rows, width = sources.shape
    far = order.shape[0] // targets
    per = targets // devices
    tile = piece_rows // per
    plain[...] = sources[...].astype(f32).reshape(targets, tile, width)

    def one(d, _):
        results = []
        for j in range(per):
            along = jnp.zeros((tile, width), f32)
            across = jnp.zeros((tile, width), f32)
            for f in range(far):
                pair = d * (per * far) + (j * far + f)
                source = plain[order[pair]]
                factor = factors[pair]
                along = along + factor[0:1] * source
                across = across + factor[1:2] * source
            results.append(along + half_turn(across))
        sent[d] = jnp.concatenate(results, axis=0).astype(bf16)
        return 0

    parts = sem.shape[0]
    moves = []
    for part in range(parts):
        first = part * (devices // parts)
        lax.fori_loop(first, first + devices // parts, one, 0, unroll=4)
        some = pl.ds(first, devices // parts)
        moves.append(pltpu.make_async_copy(sent.at[some], out.at[some], sem.at[part]))
        moves[-1].start()
    for move in moves:
        move.wait()


def far_combine(order, sources, factors, targets):
    devices, piece_rows, width = sources.shape
    tile = piece_rows // (targets // devices)
    smem = pl.BlockSpec(memory_space=pltpu.SMEM)
    vmem = pl.BlockSpec(memory_space=pltpu.VMEM)
    return pl.pallas_call(
        lambda *refs: far_body(*refs, targets=targets),
        out_shape=pltpu.HBM(sources.shape, bf16),
        in_specs=[smem, vmem, vmem],
        out_specs=pl.BlockSpec(memory_space=pltpu.HBM),
        scratch_shapes=[
            pltpu.VMEM((targets, tile, width), f32),
            pltpu.VMEM(sources.shape, bf16),
            pltpu.SemaphoreType.DMA((4,)),
        ],
        compiler_params=params(8),
        name="far",
    )(order, *held(sources, factors))


def near_body(
    lists, own, first, second, blocks, angle, radiate, out, cosine, sine, weights, boxes_all, rows, sem
):
    fetch = pltpu.make_async_copy(radiate, weights, sem)
    fetch.start()
    cosine[...] = jnp.cos(angle[...])
    sine[...] = jnp.sin(angle[...])
    boxes, excite, k = own.shape
    slots = lists.shape[0]
    shard = lax.axis_index("shard")
    base = (lax.axis_index("space") * lax.axis_size("shard") + shard) * boxes
    even = lax.rem(shard, 2) == 0
    above = jnp.where(even, 0, boxes)
    below = jnp.where(even, 3 * boxes, 2 * boxes)
    boxes_all[0:boxes] = own[...]
    boxes_all[boxes : 2 * boxes] = first[...]
    boxes_all[2 * boxes : 3 * boxes] = second[...]
    for b in range(boxes):
        for s in range(slots):
            away = lists[s, b] - base
            spot = away + jnp.where(away < 0, below, jnp.where(away < boxes, 0, above))
            rows[b * excite : (b + 1) * excite, s * k : (s + 1) * k] = boxes_all[spot]
    out[...] = dot(rows[...], blocks[...]).reshape(out.shape)
    fetch.wait()


def near_force(lists, own, first, second, blocks, angle, radiate):
    boxes, excite, k = own.shape
    slots = lists.shape[0]
    smem = pl.BlockSpec(memory_space=pltpu.SMEM)
    vmem = pl.BlockSpec(memory_space=pltpu.VMEM)
    return pl.pallas_call(
        near_body,
        out_shape=(
            pltpu.VMEM((boxes, excite, k), f32),
            pltpu.VMEM(angle.shape, f32),
            pltpu.VMEM(angle.shape, f32),
            pltpu.VMEM(radiate.shape, radiate.dtype),
        ),
        in_specs=[smem] + [vmem] * 5 + [pl.BlockSpec(memory_space=pltpu.HBM)],
        out_specs=(vmem,) * 4,
        scratch_shapes=[
            pltpu.VMEM((3 * boxes, excite, k), bf16),
            pltpu.VMEM((boxes * excite, slots * k), bf16),
            pltpu.SemaphoreType.DMA(()),
        ],
        compiler_params=params(6),
        name="near",
    )(lists, *left(own, first, second), *held(blocks.reshape(slots * k, k), angle), *left(radiate))


def down_body(pieces, near, radiate, interp, cosine, sine, out, shifted, sent, sem, *, groups, slices):
    _, _, width = pieces.shape
    boxes, excite, both = out.shape
    unknowns = both // 2
    group = excite // groups
    tile = 2 * group
    parents = boxes // CHILDREN
    for h in range(slices):
        lanes = slice(h * width, (h + 1) * width)
        for s in range(0, groups, 2):
            pair = [pieces[(s + k) * slices + h].astype(f32) for k in range(2)]
            for p in range(parents):
                incoming = jnp.concatenate([v[p * tile : (p + 1) * tile] for v in pair], axis=0)
                turned = half_turn(incoming.reshape(2, tile, width)).reshape(2 * tile, width)
                for child in range(CHILDREN):
                    row = ((p * CHILDREN + child) * groups + s) * tile
                    value = cosine[child : child + 1, lanes] * incoming - sine[child : child + 1, lanes] * turned
                    shifted[row : row + 2 * tile, lanes] = value.astype(bf16)
    leaf_in = dot_t(shifted[...], interp[...]).astype(bf16)
    parts = sem.shape[0]
    count = boxes // parts
    box_rows = groups * tile
    moves = []
    for part in range(parts):
        first = part * count
        some = leaf_in[first * box_rows : (first + count) * box_rows]
        back = dot_t(some, radiate[...]).reshape(count, groups, tile, both)
        own = back[..., :unknowns] - half_turn(back[..., unknowns:])
        for b in range(count):
            halves = [
                jnp.concatenate([own[b, s, t * group : (t + 1) * group] for s in range(groups)], axis=0)
                for t in range(2)
            ]
            sent[first + b] = jnp.concatenate(halves, axis=1) + near[first + b]
        some = pl.ds(first, count)
        moves.append(pltpu.make_async_copy(sent.at[some], out.at[some], sem.at[part]))
        moves[-1].start()
    for move in moves:
        move.wait()


def down(pieces, near, radiate, interp, cosine, sine, groups, slices):
    boxes, excite, _ = near.shape
    vmem = pl.BlockSpec(memory_space=pltpu.VMEM)
    return pl.pallas_call(
        lambda *refs: down_body(*refs, groups=groups, slices=slices),
        out_shape=pltpu.HBM(near.shape, f32),
        in_specs=[vmem] * 6,
        out_specs=pl.BlockSpec(memory_space=pltpu.HBM),
        scratch_shapes=[
            pltpu.VMEM((boxes * excite * 2, interp.shape[1]), bf16),
            pltpu.VMEM(near.shape, f32),
            pltpu.SemaphoreType.DMA((4,)),
        ],
        compiler_params=params(16),
        name="down",
    )(*held(pieces, near, radiate, interp, cosine, sine))


def is_even(axis):
    return lax.rem(lax.axis_index(axis), 2) == 0


def coefficients(kinds, table, base):
    mats = table.shape[0] // 2
    diagonal = jnp.full(kinds.shape, 6.0, f32)
    loss = jnp.zeros(kinds.shape, f32)
    for k in range(mats):
        present = kinds == k + base
        diagonal = jnp.where(present, 6.0 + table[k : k + 1, :], diagonal)
        loss = jnp.where(present, table[mats + k : mats + k + 1, :], loss)
    a = relaxation / diagonal
    if base > 0:
        a = jnp.where(kinds < base, 0.0, a)
    return a, a * loss


def along_z(v):
    lanes = v.shape[-1]
    lane = lax.broadcasted_iota(jnp.int32, v.shape, v.ndim - 1)
    lower = jnp.where(lane == 0, 0.0, pltpu.roll(v, 1, v.ndim - 1))
    upper = jnp.where(lane == lanes - 1, 0.0, pltpu.roll(v, lanes - 1, v.ndim - 1))
    return lower + upper


def along_y(tiles, low, high):
    row = lax.broadcasted_iota(jnp.int32, tiles[0].shape, 0)
    lower = [low] + [pltpu.roll(t, 1, 0) for t in tiles]
    upper = [pltpu.roll(t, 7, 0) for t in tiles] + [high]
    return [
        jnp.where(row == 0, lower[i], lower[i + 1]) + jnp.where(row == 7, upper[i + 1], upper[i])
        for i in range(len(tiles))
    ]


def relaxed(v, total, a, b):
    keep = 1.0 - relaxation
    return (
        keep * v[0] + a * total[0] + b * v[1],
        keep * v[1] + a * total[1] - b * v[0],
    )


def tiles_of(value):
    return [value[i : i + 8] for i in range(0, value.shape[0], 8)]


def tiles_at(ref, at, rows):
    return [ref[i : i + 8, :] for i in range(at, at + rows, 8)]


def sweep_brick(values, e, excite, cx, cy, source, beside, a, b, emit):
    for x in range(cx):
        sums = []
        for p in range(2):
            at = (p * excite + e) * cx + x
            edge = [jnp.broadcast_to(beside[side, at : at + 1, :], (8, source.shape[1])) for side in range(2)]
            here = values[p][x + 1]
            total = [n + along_z(t) + y for n, t, y in zip(tiles_at(source, at * cy, cy), here, along_y(here, *edge))]
            for other in (values[p][x], values[p][x + 2]):
                if other is not None:
                    total = [n + t for n, t in zip(total, other)]
            sums.append(total)
        new = []
        for i in range(cy // 8):
            rows = slice(x * cy + i * 8, x * cy + i * 8 + 8)
            new.append(
                relaxed((values[0][x + 1][i], values[1][x + 1][i]), (sums[0][i], sums[1][i]), a[rows, :], b[rows, :])
            )
        for p in range(2):
            emit(p, x, [pair[p] for pair in new])


def below_above(axis, first, second):
    even = is_even(axis)

    def pick(one, two):
        def rows(at, size):
            return jnp.where(even, one[at : at + size, :].astype(f32), two[at : at + size, :].astype(f32))

        return rows

    return pick(second, first), pick(first, second)


def edge_body(
    real_table, loss_table, field, source, kinds, first, second, table, layers, kind_rows, mat_real, mat_loss,
    sem, kind_sem, table_sem
):
    total, cy, nz = field.shape
    cx = kinds.shape[0]
    even = is_even("shard")
    faces = ((cy - 2, cy - 1), (1, 0))
    copies = [
        pltpu.make_async_copy(real_table, mat_real, table_sem.at[0]),
        pltpu.make_async_copy(loss_table, mat_loss, table_sem.at[1]),
    ]
    for i, (inner, outer) in enumerate(faces):
        for k, (ref, y) in enumerate(((field, inner), (field, outer), (source, outer))):
            copies.append(pltpu.make_async_copy(ref.at[:, y], layers.at[i, k], sem.at[i, k]))
        for k in range(2):
            copies.append(
                pltpu.make_async_copy(kinds.at[:, outer], kind_rows.at[i, pl.ds(k * cx, cx)], kind_sem.at[i, k])
            )
    for copy in copies:
        copy.start()
    for copy in copies:
        copy.wait()
    for k in range(mat_real.shape[0]):
        table[k : k + 1, :] = jnp.full((1, nz), mat_real[k], f32)
        table[mat_real.shape[0] + k : mat_real.shape[0] + k + 1, :] = jnp.full((1, nz), mat_loss[k], f32)
    row = lax.broadcasted_iota(jnp.int32, (8, nz), 0) & (cx - 1)
    for i in range(2):
        a, b = coefficients(kind_rows[i], table, 0)
        for j in range(0, total // 2, 8):
            v, sums = [], []
            for part in range(2):
                rows = slice(part * (total // 2) + j, part * (total // 2) + j + 8)
                here = layers[i, 1, rows, :]
                n = layers[i, 0, rows, :] + layers[i, 2, rows, :] + along_z(here)
                n = n + jnp.where(row == 0, 0.0, pltpu.roll(here, 1, 0))
                n = n + jnp.where(row == cx - 1, 0.0, pltpu.roll(here, 7, 0))
                v.append(here)
                sums.append(n)
            new = relaxed(v, sums, a, b)
            for part in range(2):
                layers[i, 2, part * (total // 2) + j : part * (total // 2) + j + 8, :] = new[part]
    for place, k in ((0, 1), (1, 2)):
        rows = slice(place * total, (place + 1) * total)
        first[rows, :] = jnp.where(even, layers[0, k], layers[1, k]).astype(bf16)
        second[rows, :] = jnp.where(even, layers[1, k], layers[0, k]).astype(bf16)
    kind = [jnp.concatenate([kind_rows[i].astype(f32) + 1.0] * 2, axis=0) for i in range(2)]
    first[2 * total :, :] = jnp.where(even, kind[0], kind[1]).astype(bf16)
    second[2 * total :, :] = jnp.where(even, kind[1], kind[0]).astype(bf16)


def edges(mat_real, mat_loss, field, source, kinds):
    total, _, nz = field.shape
    assert 2 * kinds.shape[0] == 8
    message = pltpu.VMEM((2 * total + 16, nz), bf16)
    anywhere = pl.BlockSpec(memory_space=pl.ANY)
    return pl.pallas_call(
        edge_body,
        out_shape=(message, message, pltpu.VMEM((2 * mat_real.shape[0], nz), f32)),
        in_specs=[anywhere] * 5,
        scratch_shapes=[
            pltpu.VMEM((2, 3, total, nz), f32),
            pltpu.VMEM((2, 8, nz), jnp.int32),
            pltpu.SMEM(mat_real.shape, f32),
            pltpu.SMEM(mat_loss.shape, f32),
            pltpu.SemaphoreType.DMA((2, 3)),
            pltpu.SemaphoreType.DMA((2, 2)),
            pltpu.SemaphoreType.DMA((2,)),
        ],
        compiler_params=params(6),
        name="edges",
    )(*left(mat_real, mat_loss, field, source, kinds))


def faces(field, kinds, cx, cy):
    channels = field.shape[0] // (cx * cy)

    def body(field, kinds, first, second):
        even = is_even("space")
        for message, x in ((first, jnp.where(even, cx - 1, 0)), (second, jnp.where(even, 0, cx - 1))):
            for c in range(channels):
                rows = pl.ds(pl.multiple_of((c * cx + x) * cy, cy), cy)
                message[c * cy : (c + 1) * cy, :] = field[rows, :].astype(bf16)
            kind = kinds[pl.ds(pl.multiple_of(x * cy, cy), cy), :].astype(f32) + 1.0
            message[channels * cy :, :] = kind.astype(bf16)

    message = pltpu.VMEM((channels * cy + cy, field.shape[1]), bf16)
    return pl.pallas_call(body, out_shape=(message, message), compiler_params=params(6), name="faces")(
        *held(field, kinds)
    )


def first_body(
    table, field, source, kinds, got_first, got_second,
    sweep, columns, column_a, to_first, to_second, near, a_all, b_all, *, cx, cy
):
    total = field.shape[0] // cy
    channels = total // cx
    excite = channels // 2
    a_all[...], b_all[...] = coefficients(kinds[...], table, 0)

    for side, (halo, own_y) in enumerate(zip(below_above("shard", got_first, got_second), (0, cy - 1))):
        kind = halo(2 * total, 16)[0:8].astype(jnp.int32)
        col_a = coefficients(kind, table, 1)[0]
        column_a[side] = col_a
        near[side] = halo(0, total)
        for j in range(0, total, 16):
            part = halo(total + j, 16)
            for k in (0, 8):
                own = field[pl.ds((j + k) * cy + own_y, 8, stride=cy), :]
                columns[side, j + k : j + k + 8] = part[k : k + 8] + col_a * own
    for e in range(excite):
        values = [
            [None] + [tiles_at(field, ((p * excite + e) * cx + x) * cy, cy) for x in range(cx)] + [None]
            for p in range(2)
        ]

        def emit(p, x, new, e=e):
            at = ((p * excite + e) * cx + x) * cy
            sweep[at : at + cy, :] = jnp.concatenate(new, axis=0)

        sweep_brick(values, e, excite, cx, cy, source, near, a_all, b_all, emit)
    even_x = is_even("space")
    plane = channels * cy
    for message, x in ((to_first, jnp.where(even_x, cx - 1, 0)), (to_second, jnp.where(even_x, 0, cx - 1))):
        for c in range(channels):
            rows = pl.ds(pl.multiple_of((c * cx + x) * cy, cy), cy)
            message[c * cy : (c + 1) * cy, :] = sweep[rows, :].astype(bf16)
        for side in range(2):
            corner = jnp.concatenate(
                [near.at[side][pl.ds(c * cx + x, 8, stride=cx), :] for c in range(0, channels, 8)], axis=0
            )
            at = plane + side * channels
            message[at : at + channels, :] = corner.astype(bf16)


def first_sweep(table, field, source, kinds, got_first, got_second, cx, cy):
    total, nz = field.shape[0] // cy, field.shape[1]
    channels = total // cx
    vmem = pl.BlockSpec(memory_space=pltpu.VMEM)
    message = pltpu.VMEM((channels * cy + 2 * channels, nz), bf16)
    return pl.pallas_call(
        lambda *refs: first_body(*refs, cx=cx, cy=cy),
        out_shape=(
            pltpu.VMEM(field.shape, f32),
            pltpu.VMEM((2, total, nz), f32),
            pltpu.VMEM((2, 8, nz), f32),
            message,
            message,
        ),
        in_specs=[vmem] * 6,
        out_specs=(vmem,) * 5,
        scratch_shapes=[pltpu.VMEM((2, total, nz), f32)] + [pltpu.VMEM((cx * cy, nz), f32)] * 2,
        compiler_params=params(8),
        name="first_sweep",
    )(*held(table, field, source, kinds, got_first, got_second))


def steps(
    volume_field,
    source,
    material,
    mat_real,
    mat_loss,
    surface_map,
    near_boxes,
    near_blocks,
    radiate,
    interp,
    phase_angle,
    far_parents,
    far_kind,
    translate,
):
    every = ("space", "shard")
    groups = lax.axis_size("space")
    slices = lax.axis_size("shard")
    _, cells_x, cells_y, cells_z = volume_field.shape[1:]
    cosine, sine, chosen, depth = prepare(phase_angle, surface_map, cells_x, cells_y, cells_z)
    weights = radiate.reshape(2 * radiate.shape[1], radiate.shape[2])
    field = volume_field.reshape(-1, cells_z)
    flat_source = source.reshape(-1, cells_z)
    kinds = material.reshape(-1, cells_z)
    bricks = (-1, cells_y, cells_z)
    *to_y, table = edges(mat_real, mat_loss, volume_field.reshape(bricks), source.reshape(bricks), material)
    field, flat_source, interp, kinds, *to_y = lax.optimization_barrier((field, flat_source, interp, kinds, *to_y))
    got_y = swap(*to_y, "shard")
    got_early = swap(*faces(field, kinds, cells_x, cells_y), "space")
    sweep, columns, column_a, *to_x = first_sweep(
        table, field, flat_source, kinds, *got_y, cells_x, cells_y
    )
    got_late = swap(*to_x, "space")
    current, currents, pieces = up(
        (table, field, sweep, columns, column_a, flat_source, kinds, *got_early, *got_late),
        chosen,
        depth,
        near_boxes.shape[0],
        weights,
        interp,
        cosine,
        sine,
        cells_x,
        cells_y,
        groups,
        slices,
    )
    directed = lax.all_to_all(pieces.reshape((groups * slices,) + pieces.shape[2:]), every, split_axis=0, concat_axis=0, tiled=True)
    first, second = swap(currents, currents, "shard")
    factors, order = tables(far_parents.T, far_kind.T, translate)
    combined = far_combine(order, directed, factors, far_parents.shape[0])
    incoming = lax.all_to_all(combined, every, split_axis=0, concat_axis=0, tiled=True)
    near, cosine, sine, weights = near_force(
        near_boxes.T, currents, first, second, near_blocks, phase_angle, weights
    )
    forcing = down(incoming, near, weights, interp, cosine, sine, groups, slices)
    return (current.reshape(volume_field.shape), forcing)


def solution(mesh):
    return jax.shard_map(
        steps,
        mesh=mesh,
        in_specs=(
            P(None, None, "space", "shard", None),
            P(None, None, "space", "shard", None),
            P("space", "shard", None),
            P(),
            P(),
            P(("space", "shard"), None),
            P(("space", "shard"), None),
            P(),
            P(),
            P(),
            P(),
            P(),
            P(),
            P(None, None, "shard"),
        ),
        out_specs=(P(None, None, "space", "shard", None), P(("space", "shard"), None, None)),
        check_vma=False,
    )
```

```python
import jax
import jax.numpy as jnp
from jax import lax
from jax.experimental import pallas as pl
from jax.experimental.pallas import tpu as pltpu
from jax.sharding import PartitionSpec as P


relaxation = 0.8
f32 = jnp.float32
bf16 = jnp.bfloat16
CHILDREN = 8


def held(*arrays):
    return [pltpu.with_memory_space_constraint(a, pltpu.VMEM) for a in arrays]


def left(*arrays):
    return [pltpu.with_memory_space_constraint(a, pltpu.HBM) for a in arrays]


def params(mib):
    return pltpu.CompilerParams(vmem_limit_bytes=mib << 20)


def dot(a, b):
    return jnp.dot(a, b, preferred_element_type=f32)


def dot_t(a, b):
    return lax.dot_general(a, b, (((1,), (1,)), ((), ())), preferred_element_type=f32)


def half_turn(v):
    half = v.shape[-2] // 2
    rows = lax.broadcasted_iota(jnp.int32, v.shape, v.ndim - 2)
    swapped = pltpu.roll(v, half, v.ndim - 2)
    return jnp.where(rows < half, -swapped, swapped)


def log2(n):
    assert n & (n - 1) == 0
    return n.bit_length() - 1


def prepare(angle, smap, cx, cy, nz):
    boxes, unknowns = smap.shape

    def body(angle, smap, cosine, sine, chosen, depth):
        cosine[...] = jnp.cos(angle[...])
        sine[...] = jnp.sin(angle[...])
        level = lax.broadcasted_iota(jnp.int32, (nz, unknowns), 0)
        for b in range(boxes):
            key = smap[b : b + 1, :]
            key_z = key & (nz - 1)
            key_x = key >> (log2(nz) + log2(cy))
            lanes = slice(b * unknowns, (b + 1) * unknowns)
            for x in range(cx):
                hit = level == jnp.where(key_x == x, key_z, -1)
                chosen[x * nz : (x + 1) * nz, lanes] = jnp.where(hit, 1.0, 0.0).astype(bf16)
            depth[:, lanes] = jnp.broadcast_to((key >> log2(nz)) & (cy - 1), (8, unknowns))

    shape = pltpu.VMEM(angle.shape, f32)
    return pl.pallas_call(
        body,
        out_shape=(
            shape,
            shape,
            pltpu.VMEM((cx * nz, boxes * unknowns), bf16),
            pltpu.VMEM((8, boxes * unknowns), jnp.int32),
        ),
        compiler_params=params(6),
        name="prepare",
    )(*held(angle, smap))


def swap_pairs(n, first):
    pairs = []
    for i in range(first, n - 1, 2):
        pairs += [(i, i + 1), (i + 1, i)]
    return pairs


def swap(for_even, for_odd, axis):
    n = lax.axis_size(axis)
    received = []
    for k, value in enumerate((for_even, for_odd)):
        received.append(lax.ppermute(value, axis, swap_pairs(n, k)))
    return received


def second_sweep(
    table, field, sweep, columns, column_a, source, kinds, early_first, early_second, late_first, late_second,
    out, beside, a_all, b_all, store, cx, cy
):
    total = field.shape[0] // cy
    channels = total // cx
    excite = channels // 2
    plane = channels * cy
    a_all[...], b_all[...] = coefficients(kinds[...], table, 0)
    early = below_above("space", early_first, early_second)
    late = below_above("space", late_first, late_second)
    ends = (0, cx - 1)
    for y_side in range(2):
        beside[y_side] = columns[y_side]
        for x_side, x in enumerate(ends):
            corner = late[x_side](plane + y_side * channels, channels)
            factor = column_a[y_side, x : x + 1, :]
            for c in range(0, channels, 8):
                rows = pl.ds(c * cx + x, 8, stride=cx)
                beside.at[y_side][rows, :] = beside.at[y_side][rows, :] + factor * corner[c : c + 8]
    face_a = [
        coefficients(early[side](plane, cy).astype(jnp.int32), table, 1)[0]
        for side in range(2)
    ]
    for e in range(excite):
        values = []
        for p in range(2):
            c = p * excite + e
            own = [tiles_at(sweep, (c * cx + x) * cy, cy) for x in range(cx)]
            outer = []
            for side, x in enumerate(ends):
                raw = tiles_of(early[side](c * cy, cy))
                factors = tiles_at(a_all, x * cy, cy)
                own[x] = [t + f * h for t, f, h in zip(own[x], factors, raw)]
                part = tiles_of(late[side](c * cy, cy))
                before = tiles_at(field, (c * cx + x) * cy, cy)
                outer.append([q + f * t for q, f, t in zip(part, tiles_of(face_a[side]), before)])
            values.append([outer[0]] + own + [outer[1]])

        def emit(p, x, new, e=e):
            at = ((p * excite + e) * cx + x) * cy
            whole = jnp.concatenate(new, axis=0)
            out[at : at + cy, :] = whole
            store(p * excite + e, x, whole)

        sweep_brick(values, e, excite, cx, cy, source, beside, a_all, b_all, emit)


def gather_rows(parts):
    row = lax.broadcasted_iota(jnp.int32, parts[0].shape, 0)
    upper = row < 4
    fours = [
        jnp.where(upper, parts[r], parts[r + 4]) + pltpu.roll(jnp.where(upper, parts[r + 4], parts[r]), 4, 0)
        for r in range(4)
    ]
    second = (row & 2) == 0
    twos = [
        jnp.where(second, fours[r] + pltpu.roll(fours[r], 6, 0), fours[r + 2] + pltpu.roll(fours[r + 2], 2, 0))
        for r in range(2)
    ]
    first = (row & 1) == 0
    return jnp.where(first, twos[0] + pltpu.roll(twos[0], 7, 0), twos[1] + pltpu.roll(twos[1], 1, 0))


def up_body(
    table, field, sweep, columns, column_a, source, kinds, early_first, early_second, late_first, late_second,
    chosen, depth, radiate, interp, cosine, sine, volume, cur, out,
    beside, cells, rows, fresh, a_all, b_all, sent, sem, sent_sem, *, cx, cy, groups, slices
):
    nz = field.shape[1]
    channels = field.shape[0] // (cx * cy)
    excite = channels // 2
    group = excite // groups
    assert 2 * group == 8 and cy % 8 == 0
    boxes = cur.shape[0]
    unknowns = depth.shape[1] // boxes

    def store(c, x, value):
        cells[c * cy : (c + 1) * cy, x * nz : (x + 1) * nz] = value.astype(bf16)

    second_sweep(
        table, field, sweep, columns, column_a, source, kinds, early_first, early_second, late_first, late_second,
        fresh, beside, a_all, b_all, store, cx, cy
    )
    leaving = pltpu.make_async_copy(fresh, volume, sem)
    leaving.start()
    moves = [leaving]
    pair = 4
    for b in range(0, boxes, pair):
        lanes = slice(b * unknowns, (b + pair) * unknowns)
        picked = dot(cells[...], chosen[:, lanes])
        key_y = depth[:, lanes]
        row = lax.broadcasted_iota(jnp.int32, key_y.shape, 0)
        hits = [key_y == row + y for y in range(0, cy, 8)]
        found = []
        for s in range(groups):
            parts = []
            for r in range(2 * group):
                c = (r // group) * excite + s * group + r % group
                kept = jnp.zeros(key_y.shape, f32)
                for i, hit in enumerate(hits):
                    kept = jnp.where(hit, picked[c * cy + i * 8 : c * cy + i * 8 + 8], kept)
                parts.append(kept)
            found.append(gather_rows(parts))
        found = jnp.concatenate(found, axis=0)
        for j in range(pair):
            own = found[:, j * unknowns : (j + 1) * unknowns].reshape(groups, 2 * group, unknowns)
            turned = half_turn(own)
            both = jnp.concatenate([own, turned], axis=2).reshape(channels, 2 * unknowns)
            rows[(b + j) * channels : (b + j + 1) * channels, :] = both.astype(bf16)
            parts = [
                jnp.concatenate([own[s, t * group : (t + 1) * group] for s in range(groups)], axis=0)
                for t in range(2)
            ]
            cur[b + j] = jnp.concatenate(parts, axis=1).astype(bf16)
    leaf = dot(rows[...], radiate[...]).astype(bf16)
    directions = interp.shape[1]
    width = directions // slices
    tile = max(width, 512)
    parents = boxes // CHILDREN
    for n in range(0, directions, tile):
        spread = dot(leaf, interp[:, n : n + tile]).reshape(parents, CHILDREN, groups, 2 * group, tile)
        along = jnp.zeros((parents, groups, 2 * group, tile), f32)
        across = jnp.zeros((parents, groups, 2 * group, tile), f32)
        for child in range(CHILDREN):
            along = along + cosine[child : child + 1, n : n + tile] * spread[:, child]
            across = across + sine[child : child + 1, n : n + tile] * spread[:, child]
        whole = (along + half_turn(across)).astype(bf16)
        for s in range(groups):
            piece = jnp.concatenate([whole[p, s] for p in range(parents)], axis=0)
            for k in range(tile // width):
                out[s, n // width + k] = piece[:, k * width : (k + 1) * width]
    for move in moves:
        move.wait()


def up(volume_args, chosen, depth, boxes, radiate, interp, cosine, sine, cx, cy, groups, slices):
    field = volume_args[1]
    nz = field.shape[1]
    total = field.shape[0] // cy
    channels = total // cx
    unknowns = depth.shape[1] // boxes
    width = interp.shape[1] // slices
    piece_rows = boxes // CHILDREN * (channels // groups)
    vmem = pl.BlockSpec(memory_space=pltpu.VMEM)
    hbm = pl.BlockSpec(memory_space=pltpu.HBM)
    return pl.pallas_call(
        lambda *refs: up_body(*refs, cx=cx, cy=cy, groups=groups, slices=slices),
        out_shape=(
            pltpu.HBM(field.shape, f32),
            pltpu.HBM((boxes, channels // 2, 2 * unknowns), bf16),
            pltpu.HBM((groups, slices, piece_rows, width), bf16),
        ),
        in_specs=[vmem] * 17,
        out_specs=(hbm, vmem, vmem),
        scratch_shapes=[
            pltpu.VMEM((2, total, nz), f32),
            pltpu.VMEM((channels * cy, cx * nz), bf16),
            pltpu.VMEM((boxes * channels, 2 * unknowns), bf16),
            pltpu.VMEM(field.shape, f32),
            pltpu.VMEM((cx * cy, nz), f32),
            pltpu.VMEM((cx * cy, nz), f32),
            pltpu.VMEM((groups, slices, piece_rows, width), bf16),
            pltpu.SemaphoreType.DMA(()),
            pltpu.SemaphoreType.DMA((interp.shape[1] // max(width, 256),)),
        ],
        compiler_params=params(16), name="up",
    )(*held(*volume_args, chosen, depth, radiate, interp, cosine, sine))


def tables(lists, kinds, translate):
    far, targets = lists.shape

    def body(lists, kinds, translate, factors, order):
        def one(t, _):
            for f in range(far):
                order[t * far + f] = lists[f, t]
                factors[t * far + f] = translate[kinds[f, t]]
            return 0

        lax.fori_loop(0, targets, one, 0, unroll=2)

    smem = pl.BlockSpec(memory_space=pltpu.SMEM)
    vmem = pl.BlockSpec(memory_space=pltpu.VMEM)
    return pl.pallas_call(
        body,
        out_shape=(
            pltpu.VMEM((targets * far,) + translate.shape[1:], f32),
            jax.ShapeDtypeStruct((targets * far,), jnp.int32),
        ),
        in_specs=[smem, smem, vmem],
        out_specs=(vmem, smem),
        compiler_params=params(8),
        name="tables",
    )(lists, kinds, *held(translate))


def far_body(order, sources, factors, out, plain, sent, sem, *, targets):
    devices, piece_rows, width = sources.shape
    far = order.shape[0] // targets
    per = targets // devices
    tile = piece_rows // per
    plain[...] = sources[...].astype(f32).reshape(targets, tile, width)

    def one(d, _):
        results = []
        for j in range(per):
            along = jnp.zeros((tile, width), f32)
            across = jnp.zeros((tile, width), f32)
            for f in range(far):
                pair = d * (per * far) + (j * far + f)
                source = plain[order[pair]]
                factor = factors[pair]
                along = along + factor[0:1] * source
                across = across + factor[1:2] * source
            results.append(along + half_turn(across))
        sent[d] = jnp.concatenate(results, axis=0).astype(bf16)
        return 0

    parts = sem.shape[0]
    moves = []
    for part in range(parts):
        first = part * (devices // parts)
        lax.fori_loop(first, first + devices // parts, one, 0, unroll=8)
        some = pl.ds(first, devices // parts)
        moves.append(pltpu.make_async_copy(sent.at[some], out.at[some], sem.at[part]))
        moves[-1].start()
    for move in moves:
        move.wait()


def far_combine(order, sources, factors, targets):
    devices, piece_rows, width = sources.shape
    tile = piece_rows // (targets // devices)
    smem = pl.BlockSpec(memory_space=pltpu.SMEM)
    vmem = pl.BlockSpec(memory_space=pltpu.VMEM)
    return pl.pallas_call(
        lambda *refs: far_body(*refs, targets=targets),
        out_shape=pltpu.HBM(sources.shape, bf16),
        in_specs=[smem, vmem, vmem],
        out_specs=pl.BlockSpec(memory_space=pltpu.HBM),
        scratch_shapes=[
            pltpu.VMEM((targets, tile, width), f32),
            pltpu.VMEM(sources.shape, bf16),
            pltpu.SemaphoreType.DMA((4,)),
        ],
        compiler_params=params(8),
        name="far",
    )(order, *held(sources, factors))


def near_body(
    lists, own, first, second, blocks, angle, radiate, out, cosine, sine, weights, boxes_all, rows, sem
):
    fetch = pltpu.make_async_copy(radiate, weights, sem)
    fetch.start()
    cosine[...] = jnp.cos(angle[...])
    sine[...] = jnp.sin(angle[...])
    boxes, excite, k = own.shape
    slots = lists.shape[0]
    shard = lax.axis_index("shard")
    base = (lax.axis_index("space") * lax.axis_size("shard") + shard) * boxes
    even = lax.rem(shard, 2) == 0
    above = jnp.where(even, 0, boxes)
    below = jnp.where(even, 3 * boxes, 2 * boxes)
    boxes_all[0:boxes] = own[...]
    boxes_all[boxes : 2 * boxes] = first[...]
    boxes_all[2 * boxes : 3 * boxes] = second[...]
    for b in range(boxes):
        for s in range(slots):
            away = lists[s, b] - base
            spot = away + jnp.where(away < 0, below, jnp.where(away < boxes, 0, above))
            rows[b * excite : (b + 1) * excite, s * k : (s + 1) * k] = boxes_all[spot]
    out[...] = dot(rows[...], blocks[...]).reshape(out.shape)
    fetch.wait()


def near_force(lists, own, first, second, blocks, angle, radiate):
    boxes, excite, k = own.shape
    slots = lists.shape[0]
    smem = pl.BlockSpec(memory_space=pltpu.SMEM)
    vmem = pl.BlockSpec(memory_space=pltpu.VMEM)
    return pl.pallas_call(
        near_body,
        out_shape=(
            pltpu.VMEM((boxes, excite, k), f32),
            pltpu.VMEM(angle.shape, f32),
            pltpu.VMEM(angle.shape, f32),
            pltpu.VMEM(radiate.shape, radiate.dtype),
        ),
        in_specs=[smem] + [vmem] * 5 + [pl.BlockSpec(memory_space=pltpu.HBM)],
        out_specs=(vmem,) * 4,
        scratch_shapes=[
            pltpu.VMEM((3 * boxes, excite, k), bf16),
            pltpu.VMEM((boxes * excite, slots * k), bf16),
            pltpu.SemaphoreType.DMA(()),
        ],
        compiler_params=params(6),
        name="near",
    )(lists, *left(own, first, second), *held(blocks.reshape(slots * k, k), angle), *left(radiate))


def down_body(pieces, near, radiate, interp, cosine, sine, out, shifted, sent, sem, *, groups, slices):
    _, _, width = pieces.shape
    boxes, excite, both = out.shape
    unknowns = both // 2
    group = excite // groups
    tile = 2 * group
    parents = boxes // CHILDREN
    for h in range(slices):
        lanes = slice(h * width, (h + 1) * width)
        for s in range(0, groups, 2):
            pair = [pieces[(s + k) * slices + h].astype(f32) for k in range(2)]
            for p in range(parents):
                incoming = jnp.concatenate([v[p * tile : (p + 1) * tile] for v in pair], axis=0)
                turned = half_turn(incoming.reshape(2, tile, width)).reshape(2 * tile, width)
                for child in range(CHILDREN):
                    row = ((p * CHILDREN + child) * groups + s) * tile
                    value = cosine[child : child + 1, lanes] * incoming - sine[child : child + 1, lanes] * turned
                    shifted[row : row + 2 * tile, lanes] = value.astype(bf16)
    leaf_in = dot_t(shifted[...], interp[...]).astype(bf16)
    parts = sem.shape[0]
    count = boxes // parts
    box_rows = groups * tile
    moves = []
    for part in range(parts):
        first = part * count
        some = leaf_in[first * box_rows : (first + count) * box_rows]
        back = dot_t(some, radiate[...]).reshape(count, groups, tile, both)
        own = back[..., :unknowns] - half_turn(back[..., unknowns:])
        for b in range(count):
            halves = [
                jnp.concatenate([own[b, s, t * group : (t + 1) * group] for s in range(groups)], axis=0)
                for t in range(2)
            ]
            sent[first + b] = jnp.concatenate(halves, axis=1) + near[first + b]
        some = pl.ds(first, count)
        moves.append(pltpu.make_async_copy(sent.at[some], out.at[some], sem.at[part]))
        moves[-1].start()
    for move in moves:
        move.wait()


def down(pieces, near, radiate, interp, cosine, sine, groups, slices):
    boxes, excite, _ = near.shape
    vmem = pl.BlockSpec(memory_space=pltpu.VMEM)
    return pl.pallas_call(
        lambda *refs: down_body(*refs, groups=groups, slices=slices),
        out_shape=pltpu.HBM(near.shape, f32),
        in_specs=[vmem] * 6,
        out_specs=pl.BlockSpec(memory_space=pltpu.HBM),
        scratch_shapes=[
            pltpu.VMEM((boxes * excite * 2, interp.shape[1]), bf16),
            pltpu.VMEM(near.shape, f32),
            pltpu.SemaphoreType.DMA((4,)),
        ],
        compiler_params=params(16),
        name="down",
    )(*held(pieces, near, radiate, interp, cosine, sine))


def is_even(axis):
    return lax.rem(lax.axis_index(axis), 2) == 0


def coefficients(kinds, table, base):
    mats = table.shape[0] // 2
    diagonal = jnp.full(kinds.shape, 6.0, f32)
    loss = jnp.zeros(kinds.shape, f32)
    for k in range(mats):
        present = kinds == k + base
        diagonal = jnp.where(present, 6.0 + table[k : k + 1, :], diagonal)
        loss = jnp.where(present, table[mats + k : mats + k + 1, :], loss)
    a = relaxation / diagonal
    if base > 0:
        a = jnp.where(kinds < base, 0.0, a)
    return a, a * loss


def along_z(v):
    lanes = v.shape[-1]
    lane = lax.broadcasted_iota(jnp.int32, v.shape, v.ndim - 1)
    lower = jnp.where(lane == 0, 0.0, pltpu.roll(v, 1, v.ndim - 1))
    upper = jnp.where(lane == lanes - 1, 0.0, pltpu.roll(v, lanes - 1, v.ndim - 1))
    return lower + upper


def along_y(tiles, low, high):
    row = lax.broadcasted_iota(jnp.int32, tiles[0].shape, 0)
    lower = [low] + [pltpu.roll(t, 1, 0) for t in tiles]
    upper = [pltpu.roll(t, 7, 0) for t in tiles] + [high]
    return [
        jnp.where(row == 0, lower[i], lower[i + 1]) + jnp.where(row == 7, upper[i + 1], upper[i])
        for i in range(len(tiles))
    ]


def relaxed(v, total, a, b):
    keep = 1.0 - relaxation
    return (
        keep * v[0] + a * total[0] + b * v[1],
        keep * v[1] + a * total[1] - b * v[0],
    )


def tiles_of(value):
    return [value[i : i + 8] for i in range(0, value.shape[0], 8)]


def tiles_at(ref, at, rows):
    return [ref[i : i + 8, :] for i in range(at, at + rows, 8)]


def sweep_brick(values, e, excite, cx, cy, source, beside, a, b, emit):
    for x in range(cx):
        sums = []
        for p in range(2):
            at = (p * excite + e) * cx + x
            edge = [jnp.broadcast_to(beside[side, at : at + 1, :], (8, source.shape[1])) for side in range(2)]
            here = values[p][x + 1]
            total = [n + along_z(t) + y for n, t, y in zip(tiles_at(source, at * cy, cy), here, along_y(here, *edge))]
            for other in (values[p][x], values[p][x + 2]):
                if other is not None:
                    total = [n + t for n, t in zip(total, other)]
            sums.append(total)
        new = []
        for i in range(cy // 8):
            rows = slice(x * cy + i * 8, x * cy + i * 8 + 8)
            new.append(
                relaxed((values[0][x + 1][i], values[1][x + 1][i]), (sums[0][i], sums[1][i]), a[rows, :], b[rows, :])
            )
        for p in range(2):
            emit(p, x, [pair[p] for pair in new])


def below_above(axis, first, second):
    even = is_even(axis)

    def pick(one, two):
        def rows(at, size):
            return jnp.where(even, one[at : at + size, :].astype(f32), two[at : at + size, :].astype(f32))

        return rows

    return pick(second, first), pick(first, second)


def edge_body(
    real_table, loss_table, field, source, kinds, first, second, table, layers, kind_rows, mat_real, mat_loss,
    sem, kind_sem, table_sem
):
    total, cy, nz = field.shape
    cx = kinds.shape[0]
    even = is_even("shard")
    faces = ((cy - 2, cy - 1), (1, 0))
    copies = [
        pltpu.make_async_copy(real_table, mat_real, table_sem.at[0]),
        pltpu.make_async_copy(loss_table, mat_loss, table_sem.at[1]),
    ]
    for i, (inner, outer) in enumerate(faces):
        for k, (ref, y) in enumerate(((field, inner), (field, outer), (source, outer))):
            copies.append(pltpu.make_async_copy(ref.at[:, y], layers.at[i, k], sem.at[i, k]))
        for k in range(2):
            copies.append(
                pltpu.make_async_copy(kinds.at[:, outer], kind_rows.at[i, pl.ds(k * cx, cx)], kind_sem.at[i, k])
            )
    for copy in copies:
        copy.start()
    for copy in copies:
        copy.wait()
    for k in range(mat_real.shape[0]):
        table[k : k + 1, :] = jnp.full((1, nz), mat_real[k], f32)
        table[mat_real.shape[0] + k : mat_real.shape[0] + k + 1, :] = jnp.full((1, nz), mat_loss[k], f32)
    row = lax.broadcasted_iota(jnp.int32, (8, nz), 0) & (cx - 1)
    for i in range(2):
        a, b = coefficients(kind_rows[i], table, 0)
        for j in range(0, total // 2, 8):
            v, sums = [], []
            for part in range(2):
                rows = slice(part * (total // 2) + j, part * (total // 2) + j + 8)
                here = layers[i, 1, rows, :]
                n = layers[i, 0, rows, :] + layers[i, 2, rows, :] + along_z(here)
                n = n + jnp.where(row == 0, 0.0, pltpu.roll(here, 1, 0))
                n = n + jnp.where(row == cx - 1, 0.0, pltpu.roll(here, 7, 0))
                v.append(here)
                sums.append(n)
            new = relaxed(v, sums, a, b)
            for part in range(2):
                layers[i, 2, part * (total // 2) + j : part * (total // 2) + j + 8, :] = new[part]
    for place, k in ((0, 1), (1, 2)):
        rows = slice(place * total, (place + 1) * total)
        first[rows, :] = jnp.where(even, layers[0, k], layers[1, k]).astype(bf16)
        second[rows, :] = jnp.where(even, layers[1, k], layers[0, k]).astype(bf16)
    kind = [jnp.concatenate([kind_rows[i].astype(f32) + 1.0] * 2, axis=0) for i in range(2)]
    first[2 * total :, :] = jnp.where(even, kind[0], kind[1]).astype(bf16)
    second[2 * total :, :] = jnp.where(even, kind[1], kind[0]).astype(bf16)


def edges(mat_real, mat_loss, field, source, kinds):
    total, _, nz = field.shape
    assert 2 * kinds.shape[0] == 8
    message = pltpu.VMEM((2 * total + 16, nz), bf16)
    anywhere = pl.BlockSpec(memory_space=pl.ANY)
    return pl.pallas_call(
        edge_body,
        out_shape=(message, message, pltpu.VMEM((2 * mat_real.shape[0], nz), f32)),
        in_specs=[anywhere] * 5,
        scratch_shapes=[
            pltpu.VMEM((2, 3, total, nz), f32),
            pltpu.VMEM((2, 8, nz), jnp.int32),
            pltpu.SMEM(mat_real.shape, f32),
            pltpu.SMEM(mat_loss.shape, f32),
            pltpu.SemaphoreType.DMA((2, 3)),
            pltpu.SemaphoreType.DMA((2, 2)),
            pltpu.SemaphoreType.DMA((2,)),
        ],
        compiler_params=params(6),
        name="edges",
    )(*left(mat_real, mat_loss, field, source, kinds))


def faces(field, kinds, cx, cy):
    channels = field.shape[0] // (cx * cy)

    def body(field, kinds, first, second):
        even = is_even("space")
        for message, x in ((first, jnp.where(even, cx - 1, 0)), (second, jnp.where(even, 0, cx - 1))):
            for c in range(channels):
                rows = pl.ds(pl.multiple_of((c * cx + x) * cy, cy), cy)
                message[c * cy : (c + 1) * cy, :] = field[rows, :].astype(bf16)
            kind = kinds[pl.ds(pl.multiple_of(x * cy, cy), cy), :].astype(f32) + 1.0
            message[channels * cy :, :] = kind.astype(bf16)

    message = pltpu.VMEM((channels * cy + cy, field.shape[1]), bf16)
    return pl.pallas_call(body, out_shape=(message, message), compiler_params=params(6), name="faces")(
        *held(field, kinds)
    )


def first_body(
    table, field, source, kinds, got_first, got_second,
    sweep, columns, column_a, to_first, to_second, near, a_all, b_all, *, cx, cy
):
    total = field.shape[0] // cy
    channels = total // cx
    excite = channels // 2
    a_all[...], b_all[...] = coefficients(kinds[...], table, 0)

    for side, (halo, own_y) in enumerate(zip(below_above("shard", got_first, got_second), (0, cy - 1))):
        kind = halo(2 * total, 16)[0:8].astype(jnp.int32)
        col_a = coefficients(kind, table, 1)[0]
        column_a[side] = col_a
        near[side] = halo(0, total)
        for j in range(0, total, 16):
            part = halo(total + j, 16)
            for k in (0, 8):
                own = field[pl.ds((j + k) * cy + own_y, 8, stride=cy), :]
                columns[side, j + k : j + k + 8] = part[k : k + 8] + col_a * own
    for e in range(excite):
        values = [
            [None] + [tiles_at(field, ((p * excite + e) * cx + x) * cy, cy) for x in range(cx)] + [None]
            for p in range(2)
        ]

        def emit(p, x, new, e=e):
            at = ((p * excite + e) * cx + x) * cy
            sweep[at : at + cy, :] = jnp.concatenate(new, axis=0)

        sweep_brick(values, e, excite, cx, cy, source, near, a_all, b_all, emit)
    even_x = is_even("space")
    plane = channels * cy
    for message, x in ((to_first, jnp.where(even_x, cx - 1, 0)), (to_second, jnp.where(even_x, 0, cx - 1))):
        for c in range(channels):
            rows = pl.ds(pl.multiple_of((c * cx + x) * cy, cy), cy)
            message[c * cy : (c + 1) * cy, :] = sweep[rows, :].astype(bf16)
        for side in range(2):
            corner = jnp.concatenate(
                [near.at[side][pl.ds(c * cx + x, 8, stride=cx), :] for c in range(0, channels, 8)], axis=0
            )
            at = plane + side * channels
            message[at : at + channels, :] = corner.astype(bf16)


def first_sweep(table, field, source, kinds, got_first, got_second, cx, cy):
    total, nz = field.shape[0] // cy, field.shape[1]
    channels = total // cx
    vmem = pl.BlockSpec(memory_space=pltpu.VMEM)
    message = pltpu.VMEM((channels * cy + 2 * channels, nz), bf16)
    return pl.pallas_call(
        lambda *refs: first_body(*refs, cx=cx, cy=cy),
        out_shape=(
            pltpu.VMEM(field.shape, f32),
            pltpu.VMEM((2, total, nz), f32),
            pltpu.VMEM((2, 8, nz), f32),
            message,
            message,
        ),
        in_specs=[vmem] * 6,
        out_specs=(vmem,) * 5,
        scratch_shapes=[pltpu.VMEM((2, total, nz), f32)] + [pltpu.VMEM((cx * cy, nz), f32)] * 2,
        compiler_params=params(8),
        name="first_sweep",
    )(*held(table, field, source, kinds, got_first, got_second))


def steps(
    volume_field,
    source,
    material,
    mat_real,
    mat_loss,
    surface_map,
    near_boxes,
    near_blocks,
    radiate,
    interp,
    phase_angle,
    far_parents,
    far_kind,
    translate,
):
    every = ("space", "shard")
    groups = lax.axis_size("space")
    slices = lax.axis_size("shard")
    _, cells_x, cells_y, cells_z = volume_field.shape[1:]
    cosine, sine, chosen, depth = prepare(phase_angle, surface_map, cells_x, cells_y, cells_z)
    weights = radiate.reshape(2 * radiate.shape[1], radiate.shape[2])
    field = volume_field.reshape(-1, cells_z)
    flat_source = source.reshape(-1, cells_z)
    kinds = material.reshape(-1, cells_z)
    bricks = (-1, cells_y, cells_z)
    *to_y, table = edges(mat_real, mat_loss, volume_field.reshape(bricks), source.reshape(bricks), material)
    field, flat_source, interp, kinds, *to_y = lax.optimization_barrier((field, flat_source, interp, kinds, *to_y))
    got_y = swap(*to_y, "shard")
    got_early = swap(*faces(field, kinds, cells_x, cells_y), "space")
    sweep, columns, column_a, *to_x = first_sweep(
        table, field, flat_source, kinds, *got_y, cells_x, cells_y
    )
    got_late = swap(*to_x, "space")
    current, currents, pieces = up(
        (table, field, sweep, columns, column_a, flat_source, kinds, *got_early, *got_late),
        chosen,
        depth,
        near_boxes.shape[0],
        weights,
        interp,
        cosine,
        sine,
        cells_x,
        cells_y,
        groups,
        slices,
    )
    directed = lax.all_to_all(pieces.reshape((groups * slices,) + pieces.shape[2:]), every, split_axis=0, concat_axis=0, tiled=True)
    first, second = swap(currents, currents, "shard")
    factors, order = tables(far_parents.T, far_kind.T, translate)
    combined = far_combine(order, directed, factors, far_parents.shape[0])
    incoming = lax.all_to_all(combined, every, split_axis=0, concat_axis=0, tiled=True)
    near, cosine, sine, weights = near_force(
        near_boxes.T, currents, first, second, near_blocks, phase_angle, weights
    )
    forcing = down(incoming, near, weights, interp, cosine, sine, groups, slices)
    return (current.reshape(volume_field.shape), forcing)


def solution(mesh):
    return jax.shard_map(
        steps,
        mesh=mesh,
        in_specs=(
            P(None, None, "space", "shard", None),
            P(None, None, "space", "shard", None),
            P("space", "shard", None),
            P(),
            P(),
            P(("space", "shard"), None),
            P(("space", "shard"), None),
            P(),
            P(),
            P(),
            P(),
            P(),
            P(),
            P(None, None, "shard"),
        ),
        out_specs=(P(None, None, "space", "shard", None), P(("space", "shard"), None, None)),
        check_vma=False,
    )
```
